128 devices in a mesh: req: 16 (over z, x), tok: 8 (over y, core).
Axes of the slice: x: 4, y: 4, z: 4, core: 2. Of those that a mesh axis runs over, the one named last changes fastest.
Arguments:
- queries: bfloat16 [8192, 2048], P('req', 'tok'), may hold values from -6 to 6
- suffix_kv: bfloat16 [8192, 2048], P('req'), may hold values from -6 to 6
- prefix_cache: bfloat16 [8192, 2048], P('req'), may hold values from -24 to 24
- q_gain: float32 [256], replicated, may hold values from 0.1 to 1.9
- k_gain: float32 [256], replicated, may hold values from 0.1 to 1.9
- lengths: int32 [16, 3], P('req'), may hold values from 1 to 256, 512 in all within a row
- group_of: int32 [16], replicated, may hold values from 0 to 1
- owner_order: int32 [16], replicated, may hold values from 0 to 15, each once
- residual: bfloat16 [8192, 2560], P('req'), may hold values from -6 to 6
- w_out: bfloat16 [2048, 2560], P('tok'), may hold values from -0.125 to 0.125
- attn_gain: float32 [2560], replicated, may hold values from 0.1 to 1.9
- ffn_in_gain: float32 [2560], replicated, may hold values from 0.1 to 1.9
- ffn_out_gain: float32 [2560], replicated, may hold values from 0.1 to 1.9
- w_gate: bfloat16 [2560, 10240], P(None, 'tok'), may hold values from -0.125 to 0.125
- w_up: bfloat16 [2560, 10240], P(None, 'tok'), may hold values from -0.125 to 0.125
- w_down: bfloat16 [10240, 2560], P('tok'), may hold values from -0.0625 to 0.0625
Outputs:
- layer_out: bfloat16 [8192, 2560], P(('req', 'tok'))
The draws below stay inside these ranges and needn't reach their ends.
Inputs may be any that keep to these rules, and one draw needn't show every extreme that they name: The 3 lengths of each req index sum to 512; the largest is exactly 256. `owner_order`: each req index appears once; entries g * 8 to g * 8 + 7 name the holders of group g's prefix.
All inputs are finite; a program needn't handle non-finite values.
Results may differ from the reference program's by a relative error of at most 0.02.
Values may be sent and summed in bfloat16 or wider, within the bound.
A program may use at most 128 MiB of HBM per device.

```python
import math
import jax
import jax.numpy as jnp
import numpy as np
from jax import lax

D = 2560
H = 8
KVH = 4
HD = 256
FF = 10240
SUF_CAP = 512
PROWS = 512
REQ_DEV = 3
GROUPS = 2
SUF_MAX = 256
SUFFIX = 8192
CACHE_ROWS = 8192
N_REQ = 16


def draw_queries(key, part):
    own_key = jax.random.fold_in(key, 11)
    values_out = jnp.clip(jax.random.normal(own_key, (SUFFIX, H * HD), jnp.float32), -6.0, 6.0)
    return values_out.astype(jnp.bfloat16)


def draw_prefix_cache(key, part):
    own_key = jax.random.fold_in(key, 12)
    values_out = jnp.clip(jax.random.normal(own_key, (CACHE_ROWS, 2 * KVH * HD), jnp.float32), -6.0, 6.0)
    return values_out.astype(jnp.bfloat16)


def plant(entries, key, least, largest):
    extent = entries.shape
    index_at = [jax.random.randint(jax.random.fold_in(key, axis), (), 0, extent[axis]) for axis in range(len(extent))]
    entries = entries.at[tuple(index_at)].set(least)
    longest = extent.index(max(extent))
    index_at[longest] = (index_at[longest] + 1) % extent[longest]
    return entries.at[tuple(index_at)].set(largest)


def block_levels(key, shape, pieces, low, high):
    factor_of = 1.0
    for axis_at, shards_of in pieces:
        heights = jax.random.uniform(jax.random.fold_in(jax.random.fold_in(key, 6), axis_at), (shards_of,), jnp.float32, low / len(pieces), high / len(pieces))
        factor_of = factor_of * jnp.repeat(jnp.exp(heights), shape[axis_at] // shards_of).reshape((-1,) + (1,) * (len(shape) - 1 - axis_at))
    return factor_of


def profile(count, total, limit, slope):
    loads = [(1 << 20) // math.isqrt(grade ** slope) + 1 for grade in range(2, count + 1)]
    spare, given = total - limit - (count - 1), [1] * (count - 1)
    while spare > 0:
        movable = [i for i in range(count - 1) if given[i] < limit]
        mass, budget = sum([loads[i] for i in movable]), spare
        for i in movable:
            extra = min(limit - given[i], max(1, budget * loads[i] // mass), spare)
            given[i] = given[i] + extra
            spare = spare - extra
    return np.array([limit] + given)


def uneven(key, amount, total, bound, slope):
    if amount == 2:
        one = jax.random.randint(key, (), max(1, total - bound), min(bound, total - 1) + 1)
        return jnp.stack([one, total - one])
    tallies = jnp.asarray(profile(amount, total, bound, slope), jnp.int32)
    couples = (amount - 1) // 2
    donor, sink = tallies[1:1 + 2 * couples:2], tallies[2:2 + 2 * couples:2]
    margin = jnp.minimum(donor - 1, bound - sink)
    shifted = jax.random.randint(jax.random.fold_in(key, 1), (couples,), 0, 1 << 20) % (margin + 1)
    tallies = tallies.at[1:1 + 2 * couples:2].set(donor - shifted).at[2:2 + 2 * couples:2].set(sink + shifted)
    return tallies[jax.random.permutation(jax.random.fold_in(key, 2), amount)]


def gaussian(rng, dims, spread, limit, pieces=(), kind=jnp.bfloat16):
    drawn = jax.random.normal(rng, dims, jnp.float32) * spread
    if len(pieces) > 0:
        drawn = block_levels(rng, dims, pieces, -0.22, 0.18) * drawn
    return jnp.clip(drawn, min=-limit, max=limit).astype(kind)


def setup_inputs(seed: int = 0) -> dict:
    keys = jax.random.split(jax.random.key(seed), 17)
    return {
        "queries": draw_queries(jax.random.fold_in(keys[16], 71), 0),
        "suffix_kv": gaussian(keys[1], (SUFFIX, 2 * KVH * HD), 1.0, 6.0, ((0, 16),)),
        "prefix_cache": draw_prefix_cache(jax.random.fold_in(keys[16], 71), 0),
        "q_gain": jnp.clip(1.0 + 0.18 * jax.random.normal(keys[3], (HD,), jnp.float32), 0.1, 1.9),
        "k_gain": jnp.clip(1.0 + 0.18 * jax.random.normal(keys[4], (HD,), jnp.float32), 0.1, 1.9),
        "lengths": jax.vmap(lambda own: uneven(own, REQ_DEV, SUF_CAP, SUF_MAX, 2))(jax.random.split(keys[5], N_REQ)).reshape((N_REQ, REQ_DEV)).astype(jnp.int32),
        "group_of": plant(jax.random.randint(keys[6], (N_REQ,), 0, GROUPS), jax.random.fold_in(keys[6], 1), 0, GROUPS - 1).astype(jnp.int32),
        "owner_order": jax.random.permutation(keys[7], N_REQ).astype(jnp.int32),
        "residual": gaussian(keys[8], (SUFFIX, D), 1.0, 6.0, ((0, 16),)),
        "w_out": gaussian(keys[9], (H * HD, D), (H * HD) ** -0.5, 0.125, ((0, 8),)),
        "attn_gain": jnp.clip(1.0 + 0.18 * jax.random.normal(keys[10], (D,), jnp.float32), 0.1, 1.9),
        "ffn_in_gain": jnp.clip(1.0 + 0.18 * jax.random.normal(keys[11], (D,), jnp.float32), 0.1, 1.9),
        "ffn_out_gain": jnp.clip(1.0 + 0.18 * jax.random.normal(keys[12], (D,), jnp.float32), 0.1, 1.9),
        "w_gate": gaussian(keys[13], (D, FF), D ** -0.5, 0.125, ((1, 8),)),
        "w_up": gaussian(keys[14], (D, FF), D ** -0.5, 0.125, ((1, 8),)),
        "w_down": gaussian(keys[15], (FF, D), FF ** -0.5, 0.0625, ((0, 8),)),
    }


EPSILON = 1e-06
MASKED = -1e+30

def rms_scale(values_in, gain_vec):
    return values_in * lax.rsqrt(lax.optimization_barrier(jnp.mean(values_in * values_in, axis=-1, keepdims=True)) + EPSILON) * gain_vec

def reference(queries, suffix_kv, prefix_cache, q_gain, k_gain, lengths, group_of, owner_order, residual, w_out, attn_gain, ffn_in_gain, ffn_out_gain, w_gate, w_up, w_down):
    kv_width = KVH * HD
    head_ratio = H // KVH
    score_scale = HD ** (-0.5)
    owner_table = owner_order.reshape(GROUPS, N_REQ // GROUPS)
    cache_blocks = prefix_cache.reshape(N_REQ, PROWS, 2 * kv_width)
    query_blocks = queries.reshape(N_REQ, SUF_CAP, H, HD)
    suffix_blocks = suffix_kv.reshape(N_REQ, SUF_CAP, 2 * kv_width)
    positions = jnp.arange(SUF_CAP, dtype=jnp.int32)

    def one_index(req_index):
        query_normed = rms_scale(query_blocks[req_index].astype(jnp.float32), q_gain).astype(jnp.bfloat16)
        own_kv = suffix_blocks[req_index]
        suf_keys = rms_scale(own_kv[:, :kv_width].reshape(SUF_CAP, KVH, HD).astype(jnp.float32), k_gain).astype(jnp.bfloat16)
        suf_vals = own_kv[:, kv_width:].reshape(SUF_CAP, KVH, HD)
        owner_ids = jnp.take(owner_table, group_of[req_index], axis=0)
        shared = jnp.take(cache_blocks, owner_ids, axis=0).reshape(-1, 2 * kv_width)
        all_keys = jnp.concatenate([shared[:, :kv_width].reshape(-1, KVH, HD), suf_keys], axis=0)
        all_vals = jnp.concatenate([shared[:, kv_width:].reshape(-1, KVH, HD), suf_vals], axis=0)
        seg_ends = jnp.cumsum(lengths[req_index]).astype(jnp.int32)
        segment = lax.optimization_barrier(jnp.sum((positions[:, None] >= seg_ends[None, :]).astype(jnp.int32), axis=1))
        causal = (segment[:, None] == segment[None, :]) & (positions[None, :] <= positions[:, None])
        visible = jnp.concatenate([jnp.ones((SUF_CAP, shared.shape[0]), jnp.bool_), causal], axis=1)
        outputs = []
        for head_idx in range(H):
            kv_idx = head_idx // head_ratio
            scores = jnp.dot(query_normed[:, head_idx], all_keys[:, kv_idx].T, preferred_element_type=jnp.float32) * score_scale
            scores = jnp.where(visible, scores, MASKED)
            row_max = lax.optimization_barrier(jnp.max(scores, axis=-1, keepdims=True))
            weights = jnp.exp(scores - row_max)
            row_sum = lax.optimization_barrier(jnp.sum(weights, axis=-1, keepdims=True))
            head_out = jnp.dot(weights.astype(jnp.bfloat16), all_vals[:, kv_idx], preferred_element_type=jnp.float32) / row_sum
            outputs.append(head_out)
        return jnp.concatenate(outputs, axis=1).astype(jnp.bfloat16)
    attention = lax.map(one_index, jnp.arange(N_REQ, dtype=jnp.int32)).reshape(N_REQ * SUF_CAP, H * HD)
    projected = jnp.dot(attention, w_out, preferred_element_type=jnp.float32)
    mixed_rows = residual.astype(jnp.float32) + rms_scale(projected, attn_gain)
    normed = rms_scale(mixed_rows, ffn_in_gain).astype(jnp.bfloat16)
    gate = jnp.dot(normed, w_gate, preferred_element_type=jnp.float32)
    upward = jnp.dot(normed, w_up, preferred_element_type=jnp.float32)
    hidden = (jax.nn.gelu(gate, approximate=True) * upward).astype(jnp.bfloat16)
    down = jnp.dot(hidden, w_down, preferred_element_type=jnp.float32)
    return (mixed_rows + rms_scale(down, ffn_out_gain)).astype(jnp.bfloat16)
```

```python
import jax
import jax.numpy as jnp
from jax import lax
from jax.sharding import PartitionSpec as P

H = 8
KVH = 4
HD = 256
GROUPS = 2


EPSILON = 1e-06
MASKED = -1e30


def rms_scale(values_in, gain_vec):
    return (
        values_in
        * lax.rsqrt(jnp.mean(values_in * values_in, axis=-1, keepdims=True) + EPSILON)
        * gain_vec
    )


def norm_heads(values_in, gain_vec, head_count):
    row_count = values_in.shape[0]
    shaped = values_in.astype(jnp.float32).reshape(row_count, head_count, HD)
    return rms_scale(shaped, gain_vec).astype(jnp.bfloat16).reshape(row_count, head_count * HD)


def local(
    queries,
    suffix_kv,
    prefix_cache,
    q_gain,
    k_gain,
    lengths,
    group_of,
    owner_order,
    residual,
    w_out,
    attn_gain,
    ffn_in_gain,
    ffn_out_gain,
    w_gate,
    w_up,
    w_down,
):
    req_count = lax.axis_size("req")
    tok_count = lax.axis_size("tok")
    req_index = lax.axis_index("req")
    tok_index = lax.axis_index("tok")
    row_count = queries.shape[0]
    heads_here = queries.shape[1] // HD
    head_ratio = H // KVH
    kv_first = tok_index * heads_here // head_ratio
    kv_width = KVH * HD
    own_count = req_count // GROUPS

    with jax.named_scope("prefix_gather"):
        pref_keys = lax.dynamic_slice_in_dim(prefix_cache, kv_first * HD, HD, 1)
        pref_vals = lax.dynamic_slice_in_dim(prefix_cache, kv_width + kv_first * HD, HD, 1)
        pref_kv = jnp.concatenate([pref_keys, pref_vals], axis=1)
        gathered = lax.all_gather(pref_kv, "req", axis=0, tiled=False)
        own_group = group_of[req_index]
        owner_ids = lax.dynamic_slice_in_dim(owner_order, own_group * own_count, own_count)
        shared = jnp.take(gathered, owner_ids, axis=0).reshape(-1, 2 * HD)

    with jax.named_scope("attention"):
        query_normed = norm_heads(queries, q_gain, heads_here)
        suf_keys = norm_heads(
            lax.dynamic_slice_in_dim(suffix_kv, kv_first * HD, HD, 1), k_gain, 1
        )
        suf_vals = lax.dynamic_slice_in_dim(suffix_kv, kv_width + kv_first * HD, HD, 1)
        all_keys = jnp.concatenate([shared[:, :HD], suf_keys], axis=0)
        all_vals = jnp.concatenate([shared[:, HD:], suf_vals], axis=0)
        seg_ends = jnp.cumsum(lengths[0])
        positions = jnp.arange(row_count, dtype=jnp.int32)
        segment = jnp.sum((positions[:, None] >= seg_ends[None, :]).astype(jnp.int32), axis=1)
        causal = (segment[:, None] == segment[None, :]) & (positions[None, :] <= positions[:, None])
        visible = jnp.concatenate(
            [jnp.ones((row_count, shared.shape[0]), jnp.bool_), causal], axis=1
        )
        outputs = []
        for head_idx in range(heads_here):
            head_q = query_normed[:, head_idx * HD:(head_idx + 1) * HD]
            scores = jnp.dot(head_q, all_keys.T, preferred_element_type=jnp.float32) * HD ** (-0.5)
            scores = jnp.where(visible, scores, MASKED)
            row_max = jnp.max(scores, axis=-1, keepdims=True)
            weights = jnp.exp(scores - row_max)
            row_sum = jnp.sum(weights, axis=-1, keepdims=True)
            head_out = jnp.dot(
                weights.astype(jnp.bfloat16), all_vals, preferred_element_type=jnp.float32
            ) / row_sum
            outputs.append(head_out)
        attention = jnp.concatenate(outputs, axis=1).astype(jnp.bfloat16)

    share = row_count // tok_count
    first_row = tok_index * share
    with jax.named_scope("out_projection"):
        projected = lax.psum_scatter(
            jnp.dot(attention, w_out, preferred_element_type=jnp.float32),
            "tok",
            scatter_dimension=0,
            tiled=True,
        )
        residual_share = lax.dynamic_slice_in_dim(residual, first_row, share, 0)
        mixed_share = residual_share.astype(jnp.float32) + rms_scale(projected, attn_gain)
        normed_share = rms_scale(mixed_share, ffn_in_gain).astype(jnp.bfloat16)
        normed = lax.all_gather(normed_share, "tok", axis=0, tiled=True)
    with jax.named_scope("feed_forward"):
        gate = jnp.dot(normed, w_gate, preferred_element_type=jnp.float32)
        upward = jnp.dot(normed, w_up, preferred_element_type=jnp.float32)
        hidden = (jax.nn.gelu(gate, approximate=True) * upward).astype(jnp.bfloat16)
        down_share = lax.psum_scatter(
            jnp.dot(hidden, w_down, preferred_element_type=jnp.float32),
            "tok",
            scatter_dimension=0,
            tiled=True,
        )
    return (mixed_share + rms_scale(down_share, ffn_out_gain)).astype(jnp.bfloat16)


def solution(mesh):
    in_specs = (
        P("req", "tok"),
        P("req", None),
        P("req", None),
        P(),
        P(),
        P("req", None),
        P(),
        P(),
        P("req", None),
        P("tok", None),
        P(),
        P(),
        P(),
        P(None, "tok"),
        P(None, "tok"),
        P("tok", None),
    )
    out_specs = P(("req", "tok"), None)
    return jax.shard_map(local, mesh=mesh, in_specs=in_specs, out_specs=out_specs, check_vma=False)
```

```python
import jax
import jax.numpy as jnp
from jax import lax
from jax.sharding import PartitionSpec as P

H = 8
KVH = 4
HD = 256
GROUPS = 2


EPSILON = 1e-06
MASKED = -1e30


def rms_scale(values_in, gain_vec):
    return (
        values_in
        * lax.rsqrt(jnp.mean(values_in * values_in, axis=-1, keepdims=True) + EPSILON)
        * gain_vec
    )


def norm_heads(values_in, gain_vec, head_count):
    row_count = values_in.shape[0]
    shaped = values_in.astype(jnp.float32).reshape(row_count, head_count, HD)
    return rms_scale(shaped, gain_vec).astype(jnp.bfloat16).reshape(row_count, head_count * HD)


def local(
    queries,
    suffix_kv,
    prefix_cache,
    q_gain,
    k_gain,
    lengths,
    group_of,
    owner_order,
    residual,
    w_out,
    attn_gain,
    ffn_in_gain,
    ffn_out_gain,
    w_gate,
    w_up,
    w_down,
):
    req_count = lax.axis_size("req")
    tok_count = lax.axis_size("tok")
    req_index = lax.axis_index("req")
    tok_index = lax.axis_index("tok")
    row_count = queries.shape[0]
    heads_here = queries.shape[1] // HD
    head_ratio = H // KVH
    kv_first = tok_index * heads_here // head_ratio
    kv_width = KVH * HD
    own_count = req_count // GROUPS

    with jax.named_scope("prefix_gather"):
        pref_keys = lax.dynamic_slice_in_dim(prefix_cache, kv_first * HD, HD, 1)
        pref_vals = lax.dynamic_slice_in_dim(prefix_cache, kv_width + kv_first * HD, HD, 1)
        pref_kv = jnp.concatenate([pref_keys, pref_vals], axis=1)
        half_rows = pref_kv.shape[0] // 2
        core = tok_index % 2
        my_half = lax.dynamic_slice_in_dim(pref_kv, core * half_rows, half_rows, 0)
        gathered = lax.all_gather(my_half, "req", axis=0, tiled=False)
        own_group = group_of[req_index]
        owner_ids = lax.dynamic_slice_in_dim(owner_order, own_group * own_count, own_count)
        picked = jnp.take(gathered, owner_ids, axis=0).reshape(-1, 2 * HD)
        partner = [(t, t ^ 1) for t in range(tok_count)]
        swapped = lax.ppermute(picked, "tok", perm=partner)
        shared = jnp.concatenate([picked, swapped], axis=0)

    with jax.named_scope("attention"):
        query_normed = norm_heads(queries, q_gain, heads_here)
        suf_keys = norm_heads(
            lax.dynamic_slice_in_dim(suffix_kv, kv_first * HD, HD, 1), k_gain, 1
        )
        suf_vals = lax.dynamic_slice_in_dim(suffix_kv, kv_width + kv_first * HD, HD, 1)
        all_keys = jnp.concatenate([shared[:, :HD], suf_keys], axis=0)
        all_vals = jnp.concatenate([shared[:, HD:], suf_vals], axis=0)
        seg_ends = jnp.cumsum(lengths[0])
        positions = jnp.arange(row_count, dtype=jnp.int32)
        segment = jnp.sum((positions[:, None] >= seg_ends[None, :]).astype(jnp.int32), axis=1)
        causal = (segment[:, None] == segment[None, :]) & (positions[None, :] <= positions[:, None])
        visible = jnp.concatenate(
            [jnp.ones((row_count, shared.shape[0]), jnp.bool_), causal], axis=1
        )
        outputs = []
        for head_idx in range(heads_here):
            head_q = query_normed[:, head_idx * HD:(head_idx + 1) * HD]
            scores = jnp.dot(head_q, all_keys.T, preferred_element_type=jnp.float32) * HD ** (-0.5)
            scores = jnp.where(visible, scores, MASKED)
            row_max = jnp.max(scores, axis=-1, keepdims=True)
            weights = jnp.exp(scores - row_max)
            row_sum = jnp.sum(weights, axis=-1, keepdims=True)
            head_out = jnp.dot(
                weights.astype(jnp.bfloat16), all_vals, preferred_element_type=jnp.float32
            ) / row_sum
            outputs.append(head_out)
        attention = jnp.concatenate(outputs, axis=1).astype(jnp.bfloat16)

    share = row_count // tok_count
    first_row = tok_index * share
    with jax.named_scope("out_projection"):
        projected = lax.psum_scatter(
            jnp.dot(attention, w_out, preferred_element_type=jnp.float32).astype(jnp.bfloat16),
            "tok",
            scatter_dimension=0,
            tiled=True,
        )
        residual_share = lax.dynamic_slice_in_dim(residual, first_row, share, 0)
        mixed_share = residual_share.astype(jnp.float32) + rms_scale(
            projected.astype(jnp.float32), attn_gain
        )
        normed_share = rms_scale(mixed_share, ffn_in_gain).astype(jnp.bfloat16)
        normed = lax.all_gather(normed_share, "tok", axis=0, tiled=True)
    with jax.named_scope("feed_forward"):
        gate = jnp.dot(normed, w_gate, preferred_element_type=jnp.float32)
        upward = jnp.dot(normed, w_up, preferred_element_type=jnp.float32)
        hidden = (jax.nn.gelu(gate, approximate=True) * upward).astype(jnp.bfloat16)
        down_share = lax.psum_scatter(
            jnp.dot(hidden, w_down, preferred_element_type=jnp.float32).astype(jnp.bfloat16),
            "tok",
            scatter_dimension=0,
            tiled=True,
        )
    return (mixed_share + rms_scale(down_share.astype(jnp.float32), ffn_out_gain)).astype(
        jnp.bfloat16
    )


def solution(mesh):
    in_specs = (
        P("req", "tok"),
        P("req", None),
        P("req", None),
        P(),
        P(),
        P("req", None),
        P(),
        P(),
        P("req", None),
        P("tok", None),
        P(),
        P(),
        P(),
        P(None, "tok"),
        P(None, "tok"),
        P("tok", None),
    )
    out_specs = P(("req", "tok"), None)
    return jax.shard_map(local, mesh=mesh, in_specs=in_specs, out_specs=out_specs, check_vma=False)
```

```python
import jax
import jax.numpy as jnp
from jax import lax
from jax.sharding import PartitionSpec as P
from jax.experimental import pallas as pl
from jax.experimental.pallas import tpu as pltpu

H = 8
KVH = 4
HD = 256
GROUPS = 2


EPSILON = 1e-06
MASKED = -1e30


def rms_scale(values_in, gain_vec):
    return (
        values_in
        * lax.rsqrt(jnp.mean(values_in * values_in, axis=-1, keepdims=True) + EPSILON)
        * gain_vec
    )


def norm_heads(values_in, gain_vec, head_count):
    row_count = values_in.shape[0]
    shaped = values_in.astype(jnp.float32).reshape(row_count, head_count, HD)
    return rms_scale(shaped, gain_vec).astype(jnp.bfloat16).reshape(row_count, head_count * HD)


def gather_tok_kernel(tok_count, w_ref, out_ref, send_sem, recv_sem, local_sem):
    mesh_ids = pl.DeviceIdType.MESH
    me = lax.axis_index("tok")
    up = lax.rem(me + 2, tok_count)
    down = lax.rem(me + tok_count - 2, tok_count)
    far = lax.rem(me + 4, tok_count)
    partner = me + 1 - 2 * lax.rem(me, 2)
    half = w_ref.shape[0] // 2

    barrier = pltpu.get_barrier_semaphore()
    for peer in (up, down, partner):
        pl.semaphore_signal(barrier, inc=1, device_id={"tok": peer}, device_id_type=mesh_ids)
    pl.semaphore_wait(barrier, 3)

    def remote(src, dst, slot, peer):
        return pltpu.make_async_remote_copy(
            src_ref=src,
            dst_ref=dst,
            send_sem=send_sem.at[slot],
            recv_sem=recv_sem.at[slot],
            device_id={"tok": peer},
            device_id_type=mesh_ids,
        )

    local = pltpu.make_async_copy(w_ref, out_ref.at[me], local_sem.at[0])
    local.start()
    to_up = remote(w_ref, out_ref.at[me], 0, up)
    to_down = remote(w_ref, out_ref.at[me], 1, down)
    to_up.start()
    to_down.start()
    remote(w_ref, out_ref.at[down], 0, down).wait_recv()
    remote(w_ref, out_ref.at[up], 1, up).wait_recv()

    first = pl.ds(0, half)
    second = pl.ds(half, half)
    fwd_up = remote(out_ref.at[down, first], out_ref.at[down, first], 2, up)
    fwd_down = remote(out_ref.at[up, second], out_ref.at[up, second], 3, down)
    fwd_up.start()
    fwd_down.start()
    remote(out_ref.at[far, first], out_ref.at[far, first], 2, down).wait_recv()
    remote(out_ref.at[far, second], out_ref.at[far, second], 3, up).wait_recv()
    local.wait()

    mine = (me, up, down, far)
    theirs = (
        partner,
        lax.rem(partner + 2, tok_count),
        lax.rem(partner + tok_count - 2, tok_count),
        lax.rem(partner + 4, tok_count),
    )
    to_partner = []
    for idx, slot in enumerate(mine):
        copy = remote(out_ref.at[slot], out_ref.at[slot], 4 + idx, partner)
        copy.start()
        to_partner.append(copy)
    for idx, slot in enumerate(theirs):
        remote(out_ref.at[slot], out_ref.at[slot], 4 + idx, partner).wait_recv()
    for copy in [to_up, to_down, fwd_up, fwd_down] + to_partner:
        copy.wait_send()


def gather_over_tok(block, tok_count):
    assert tok_count == 8
    rows, cols = block.shape
    return pl.pallas_call(
        lambda *refs: gather_tok_kernel(tok_count, *refs),
        out_shape=jax.ShapeDtypeStruct((tok_count, rows, cols), block.dtype),
        in_specs=[pl.BlockSpec(memory_space=pl.ANY)],
        out_specs=pl.BlockSpec(memory_space=pl.ANY),
        scratch_shapes=[
            pltpu.SemaphoreType.DMA((8,)),
            pltpu.SemaphoreType.DMA((8,)),
            pltpu.SemaphoreType.DMA((1,)),
        ],
        compiler_params=pltpu.CompilerParams(collective_id=0, has_side_effects=True),
        cost_estimate=pl.CostEstimate(
            flops=0, transcendentals=0, bytes_accessed=2 * tok_count * rows * cols * 2
        ),
    )(block)


def local(
    queries,
    suffix_kv,
    prefix_cache,
    q_gain,
    k_gain,
    lengths,
    group_of,
    owner_order,
    residual,
    w_out,
    attn_gain,
    ffn_in_gain,
    ffn_out_gain,
    w_gate,
    w_up,
    w_down,
):
    req_count = lax.axis_size("req")
    tok_count = lax.axis_size("tok")
    req_index = lax.axis_index("req")
    tok_index = lax.axis_index("tok")
    row_count = queries.shape[0]
    heads_here = queries.shape[1] // HD
    head_ratio = H // KVH
    kv_first = tok_index * heads_here // head_ratio
    kv_width = KVH * HD
    own_count = req_count // GROUPS

    with jax.named_scope("prefix_gather"):
        pref_keys = lax.dynamic_slice_in_dim(prefix_cache, kv_first * HD, HD, 1)
        pref_vals = lax.dynamic_slice_in_dim(prefix_cache, kv_width + kv_first * HD, HD, 1)
        pref_kv = jnp.concatenate([pref_keys, pref_vals], axis=1)
        half_rows = pref_kv.shape[0] // 2
        core = tok_index % 2
        my_half = lax.dynamic_slice_in_dim(pref_kv, core * half_rows, half_rows, 0)
        gathered = lax.all_gather(my_half, "req", axis=0, tiled=False)
        w_out_all = gather_over_tok(w_out, tok_count).reshape(-1, w_out.shape[1])
        gathered, w_out_all = lax.optimization_barrier((gathered, w_out_all))
        own_group = group_of[req_index]
        owner_ids = lax.dynamic_slice_in_dim(owner_order, own_group * own_count, own_count)
        picked = jnp.take(gathered, owner_ids, axis=0).reshape(-1, 2 * HD)
        partner = [(t, t ^ 1) for t in range(tok_count)]
        swapped = lax.ppermute(picked, "tok", perm=partner)
        shared = jnp.concatenate([picked, swapped], axis=0)

    with jax.named_scope("attention"):
        query_normed = norm_heads(queries, q_gain, heads_here)
        suf_keys = norm_heads(
            lax.dynamic_slice_in_dim(suffix_kv, kv_first * HD, HD, 1), k_gain, 1
        )
        suf_vals = lax.dynamic_slice_in_dim(suffix_kv, kv_width + kv_first * HD, HD, 1)
        all_keys = jnp.concatenate([shared[:, :HD], suf_keys], axis=0)
        all_vals = jnp.concatenate([shared[:, HD:], suf_vals], axis=0)
        seg_ends = jnp.cumsum(lengths[0])
        positions = jnp.arange(row_count, dtype=jnp.int32)
        segment = jnp.sum((positions[:, None] >= seg_ends[None, :]).astype(jnp.int32), axis=1)
        causal = (segment[:, None] == segment[None, :]) & (positions[None, :] <= positions[:, None])
        visible = jnp.concatenate(
            [jnp.ones((row_count, shared.shape[0]), jnp.bool_), causal], axis=1
        )
        outputs = []
        for head_idx in range(heads_here):
            head_q = query_normed[:, head_idx * HD:(head_idx + 1) * HD]
            scores = jnp.dot(head_q, all_keys.T, preferred_element_type=jnp.float32) * HD ** (-0.5)
            scores = jnp.where(visible, scores, MASKED)
            row_max = jnp.max(scores, axis=-1, keepdims=True)
            weights = jnp.exp(scores - row_max)
            row_sum = jnp.sum(weights, axis=-1, keepdims=True)
            head_out = jnp.dot(
                weights.astype(jnp.bfloat16), all_vals, preferred_element_type=jnp.float32
            ) / row_sum
            outputs.append(head_out)
        attention = jnp.concatenate(outputs, axis=1).astype(jnp.bfloat16)

    share = row_count // tok_count
    first_row = tok_index * share
    with jax.named_scope("out_projection"):
        attention_all = lax.all_gather(attention, "tok", axis=1, tiled=True)
        projected = jnp.dot(attention_all, w_out_all, preferred_element_type=jnp.float32)
        mixed_rows = residual.astype(jnp.float32) + rms_scale(projected, attn_gain)
        normed = rms_scale(mixed_rows, ffn_in_gain).astype(jnp.bfloat16)
        mixed_share = lax.dynamic_slice_in_dim(mixed_rows, first_row, share, 0)
    with jax.named_scope("feed_forward"):
        gate = jnp.dot(normed, w_gate, preferred_element_type=jnp.float32)
        upward = jnp.dot(normed, w_up, preferred_element_type=jnp.float32)
        hidden = (jax.nn.gelu(gate, approximate=True) * upward).astype(jnp.bfloat16)
        down_share = lax.psum_scatter(
            jnp.dot(hidden, w_down, preferred_element_type=jnp.float32).astype(jnp.bfloat16),
            "tok",
            scatter_dimension=0,
            tiled=True,
        )
    return (mixed_share + rms_scale(down_share.astype(jnp.float32), ffn_out_gain)).astype(
        jnp.bfloat16
    )


def solution(mesh):
    in_specs = (
        P("req", "tok"),
        P("req", None),
        P("req", None),
        P(),
        P(),
        P("req", None),
        P(),
        P(),
        P("req", None),
        P("tok", None),
        P(),
        P(),
        P(),
        P(None, "tok"),
        P(None, "tok"),
        P("tok", None),
    )
    out_specs = P(("req", "tok"), None)
    return jax.shard_map(local, mesh=mesh, in_specs=in_specs, out_specs=out_specs, check_vma=False)
```

```python
import jax
import jax.numpy as jnp
from jax import lax
from jax.sharding import PartitionSpec as P
from jax.experimental import pallas as pl
from jax.experimental.pallas import tpu as pltpu

H = 8
KVH = 4
HD = 256
GROUPS = 2


EPSILON = 1e-06
MASKED = -1e30


def rms_scale(values_in, gain_vec):
    return (
        values_in
        * lax.rsqrt(jnp.mean(values_in * values_in, axis=-1, keepdims=True) + EPSILON)
        * gain_vec
    )


def norm_heads(values_in, gain_vec, head_count):
    row_count = values_in.shape[0]
    shaped = values_in.astype(jnp.float32).reshape(row_count, head_count, HD)
    return rms_scale(shaped, gain_vec).astype(jnp.bfloat16).reshape(row_count, head_count * HD)


def gather_tok_kernel(tok_count, w_ref, out_ref, send_sem, recv_sem, local_sem):
    mesh_ids = pl.DeviceIdType.MESH
    me = lax.axis_index("tok")
    up = lax.rem(me + 2, tok_count)
    down = lax.rem(me + tok_count - 2, tok_count)
    far = lax.rem(me + 4, tok_count)
    partner = me + 1 - 2 * lax.rem(me, 2)
    half = w_ref.shape[0] // 2

    barrier = pltpu.get_barrier_semaphore()
    for peer in (up, down, partner):
        pl.semaphore_signal(barrier, inc=1, device_id={"tok": peer}, device_id_type=mesh_ids)
    pl.semaphore_wait(barrier, 3)

    def remote(src, dst, slot, peer):
        return pltpu.make_async_remote_copy(
            src_ref=src,
            dst_ref=dst,
            send_sem=send_sem.at[slot],
            recv_sem=recv_sem.at[slot],
            device_id={"tok": peer},
            device_id_type=mesh_ids,
        )

    local = pltpu.make_async_copy(w_ref, out_ref.at[me], local_sem.at[0])
    local.start()
    to_up = remote(w_ref, out_ref.at[me], 0, up)
    to_down = remote(w_ref, out_ref.at[me], 1, down)
    to_up.start()
    to_down.start()
    remote(w_ref, out_ref.at[down], 0, down).wait_recv()
    remote(w_ref, out_ref.at[up], 1, up).wait_recv()

    first = pl.ds(0, half)
    second = pl.ds(half, half)
    fwd_up = remote(out_ref.at[down, first], out_ref.at[down, first], 2, up)
    fwd_down = remote(out_ref.at[up, second], out_ref.at[up, second], 3, down)
    fwd_up.start()
    fwd_down.start()
    remote(out_ref.at[far, first], out_ref.at[far, first], 2, down).wait_recv()
    remote(out_ref.at[far, second], out_ref.at[far, second], 3, up).wait_recv()
    local.wait()

    mine = (me, up, down, far)
    theirs = (
        partner,
        lax.rem(partner + 2, tok_count),
        lax.rem(partner + tok_count - 2, tok_count),
        lax.rem(partner + 4, tok_count),
    )
    to_partner = []
    for idx, slot in enumerate(mine):
        copy = remote(out_ref.at[slot], out_ref.at[slot], 4 + idx, partner)
        copy.start()
        to_partner.append(copy)
    for idx, slot in enumerate(theirs):
        remote(out_ref.at[slot], out_ref.at[slot], 4 + idx, partner).wait_recv()
    for copy in [to_up, to_down, fwd_up, fwd_down] + to_partner:
        copy.wait_send()


def gather_over_tok(block, tok_count, collective_id):
    assert tok_count == 8
    rows, cols = block.shape
    return pl.pallas_call(
        lambda *refs: gather_tok_kernel(tok_count, *refs),
        out_shape=jax.ShapeDtypeStruct((tok_count, rows, cols), block.dtype),
        in_specs=[pl.BlockSpec(memory_space=pl.ANY)],
        out_specs=pl.BlockSpec(memory_space=pl.ANY),
        scratch_shapes=[
            pltpu.SemaphoreType.DMA((8,)),
            pltpu.SemaphoreType.DMA((8,)),
            pltpu.SemaphoreType.DMA((1,)),
        ],
        compiler_params=pltpu.CompilerParams(collective_id=collective_id, has_side_effects=True),
        cost_estimate=pl.CostEstimate(
            flops=0, transcendentals=0, bytes_accessed=2 * tok_count * rows * cols * 2
        ),
    )(block)


def local(
    queries,
    suffix_kv,
    prefix_cache,
    q_gain,
    k_gain,
    lengths,
    group_of,
    owner_order,
    residual,
    w_out,
    attn_gain,
    ffn_in_gain,
    ffn_out_gain,
    w_gate,
    w_up,
    w_down,
):
    req_count = lax.axis_size("req")
    tok_count = lax.axis_size("tok")
    req_index = lax.axis_index("req")
    tok_index = lax.axis_index("tok")
    row_count = queries.shape[0]
    heads_here = queries.shape[1] // HD
    head_ratio = H // KVH
    kv_first = tok_index * heads_here // head_ratio
    kv_width = KVH * HD
    own_count = req_count // GROUPS

    with jax.named_scope("prefix_gather"):
        pref_keys = lax.dynamic_slice_in_dim(prefix_cache, kv_first * HD, HD, 1)
        pref_vals = lax.dynamic_slice_in_dim(prefix_cache, kv_width + kv_first * HD, HD, 1)
        pref_kv = jnp.concatenate([pref_keys, pref_vals], axis=1)
        half_rows = pref_kv.shape[0] // 2
        core = tok_index % 2
        my_half = lax.dynamic_slice_in_dim(pref_kv, core * half_rows, half_rows, 0)
        gathered = lax.all_gather(my_half, "req", axis=0, tiled=False)
        w_out_all = gather_over_tok(w_out, tok_count, 0)
        gathered, w_out_all = lax.optimization_barrier((gathered, w_out_all))
        own_group = group_of[req_index]
        owner_ids = lax.dynamic_slice_in_dim(owner_order, own_group * own_count, own_count)
        picked = jnp.take(gathered, owner_ids, axis=0).reshape(-1, 2 * HD)
        partner = [(t, t ^ 1) for t in range(tok_count)]
        swapped = lax.ppermute(picked, "tok", perm=partner)
        shared = jnp.concatenate([picked, swapped], axis=0)

    with jax.named_scope("attention"):
        query_normed = norm_heads(queries, q_gain, heads_here)
        suf_keys = norm_heads(
            lax.dynamic_slice_in_dim(suffix_kv, kv_first * HD, HD, 1), k_gain, 1
        )
        suf_vals = lax.dynamic_slice_in_dim(suffix_kv, kv_width + kv_first * HD, HD, 1)
        all_keys = jnp.concatenate([shared[:, :HD], suf_keys], axis=0)
        all_vals = jnp.concatenate([shared[:, HD:], suf_vals], axis=0)
        seg_ends = jnp.cumsum(lengths[0])
        positions = jnp.arange(row_count, dtype=jnp.int32)
        segment = jnp.sum((positions[:, None] >= seg_ends[None, :]).astype(jnp.int32), axis=1)
        causal = (segment[:, None] == segment[None, :]) & (positions[None, :] <= positions[:, None])
        visible = jnp.concatenate(
            [jnp.ones((row_count, shared.shape[0]), jnp.bool_), causal], axis=1
        )
        outputs = []
        for head_idx in range(heads_here):
            head_q = query_normed[:, head_idx * HD:(head_idx + 1) * HD]
            scores = jnp.dot(head_q, all_keys.T, preferred_element_type=jnp.float32) * HD ** (-0.5)
            scores = jnp.where(visible, scores, MASKED)
            row_max = jnp.max(scores, axis=-1, keepdims=True)
            weights = jnp.exp(scores - row_max)
            row_sum = jnp.sum(weights, axis=-1, keepdims=True)
            head_out = jnp.dot(
                weights.astype(jnp.bfloat16), all_vals, preferred_element_type=jnp.float32
            ) / row_sum
            outputs.append(head_out)
        attention = jnp.concatenate(outputs, axis=1).astype(jnp.bfloat16)

    share = row_count // tok_count
    first_row = tok_index * share
    with jax.named_scope("out_projection"):
        attention_all = gather_over_tok(attention, tok_count, 1)
        projected = jnp.einsum(
            "srd,sdc->rc", attention_all, w_out_all, preferred_element_type=jnp.float32
        )
        mixed_rows = residual.astype(jnp.float32) + rms_scale(projected, attn_gain)
        normed = rms_scale(mixed_rows, ffn_in_gain).astype(jnp.bfloat16)
        mixed_share = lax.dynamic_slice_in_dim(mixed_rows, first_row, share, 0)
    with jax.named_scope("feed_forward"):
        gate = jnp.dot(normed, w_gate, preferred_element_type=jnp.float32)
        upward = jnp.dot(normed, w_up, preferred_element_type=jnp.float32)
        hidden = (jax.nn.gelu(gate, approximate=True) * upward).astype(jnp.bfloat16)
        down_share = lax.psum_scatter(
            jnp.dot(hidden, w_down, preferred_element_type=jnp.float32).astype(jnp.bfloat16),
            "tok",
            scatter_dimension=0,
            tiled=True,
        )
    return (mixed_share + rms_scale(down_share.astype(jnp.float32), ffn_out_gain)).astype(
        jnp.bfloat16
    )


def solution(mesh):
    in_specs = (
        P("req", "tok"),
        P("req", None),
        P("req", None),
        P(),
        P(),
        P("req", None),
        P(),
        P(),
        P("req", None),
        P("tok", None),
        P(),
        P(),
        P(),
        P(None, "tok"),
        P(None, "tok"),
        P("tok", None),
    )
    out_specs = P(("req", "tok"), None)
    return jax.shard_map(local, mesh=mesh, in_specs=in_specs, out_specs=out_specs, check_vma=False)
```

```python
import jax
import jax.numpy as jnp
from jax import lax
from jax.sharding import PartitionSpec as P
from jax.experimental import pallas as pl
from jax.experimental.pallas import tpu as pltpu

H = 8
KVH = 4
HD = 256
GROUPS = 2


EPSILON = 1e-06
MASKED = -1e30


def rms_scale(values_in, gain_vec):
    return (
        values_in
        * lax.rsqrt(jnp.mean(values_in * values_in, axis=-1, keepdims=True) + EPSILON)
        * gain_vec
    )


def norm_heads(values_in, gain_vec, head_count):
    row_count = values_in.shape[0]
    shaped = values_in.astype(jnp.float32).reshape(row_count, head_count, HD)
    return rms_scale(shaped, gain_vec).astype(jnp.bfloat16).reshape(row_count, head_count * HD)


def gather_tok_kernel(tok_count, w_ref, out_ref, send_sem, recv_sem, local_sem):
    mesh_ids = pl.DeviceIdType.MESH
    me = lax.axis_index("tok")
    up = lax.rem(me + 2, tok_count)
    down = lax.rem(me + tok_count - 2, tok_count)
    far = lax.rem(me + 4, tok_count)
    partner = me + 1 - 2 * lax.rem(me, 2)
    half = w_ref.shape[0] // 2

    barrier = pltpu.get_barrier_semaphore()
    for peer in (up, down, partner):
        pl.semaphore_signal(barrier, inc=1, device_id={"tok": peer}, device_id_type=mesh_ids)
    pl.semaphore_wait(barrier, 3)

    def remote(src, dst, slot, peer):
        return pltpu.make_async_remote_copy(
            src_ref=src,
            dst_ref=dst,
            send_sem=send_sem.at[slot],
            recv_sem=recv_sem.at[slot],
            device_id={"tok": peer},
            device_id_type=mesh_ids,
        )

    local = pltpu.make_async_copy(w_ref, out_ref.at[me], local_sem.at[0])
    local.start()
    to_up = remote(w_ref, out_ref.at[me], 0, up)
    to_down = remote(w_ref, out_ref.at[me], 1, down)
    to_up.start()
    to_down.start()
    remote(w_ref, out_ref.at[down], 0, down).wait_recv()
    remote(w_ref, out_ref.at[up], 1, up).wait_recv()

    first = pl.ds(0, half)
    second = pl.ds(half, half)
    fwd_up = remote(out_ref.at[down, first], out_ref.at[down, first], 2, up)
    fwd_down = remote(out_ref.at[up, second], out_ref.at[up, second], 3, down)
    fwd_up.start()
    fwd_down.start()
    remote(out_ref.at[far, first], out_ref.at[far, first], 2, down).wait_recv()
    remote(out_ref.at[far, second], out_ref.at[far, second], 3, up).wait_recv()
    local.wait()

    mine = (me, up, down, far)
    theirs = (
        partner,
        lax.rem(partner + 2, tok_count),
        lax.rem(partner + tok_count - 2, tok_count),
        lax.rem(partner + 4, tok_count),
    )
    to_partner = []
    for idx, slot in enumerate(mine):
        copy = remote(out_ref.at[slot], out_ref.at[slot], 4 + idx, partner)
        copy.start()
        to_partner.append(copy)
    for idx, slot in enumerate(theirs):
        remote(out_ref.at[slot], out_ref.at[slot], 4 + idx, partner).wait_recv()
    for copy in [to_up, to_down, fwd_up, fwd_down] + to_partner:
        copy.wait_send()


def gather_over_tok(block, tok_count, collective_id):
    assert tok_count == 8
    rows, cols = block.shape
    return pl.pallas_call(
        lambda *refs: gather_tok_kernel(tok_count, *refs),
        out_shape=jax.ShapeDtypeStruct((tok_count, rows, cols), block.dtype),
        in_specs=[pl.BlockSpec(memory_space=pl.ANY)],
        out_specs=pl.BlockSpec(memory_space=pl.ANY),
        scratch_shapes=[
            pltpu.SemaphoreType.DMA((8,)),
            pltpu.SemaphoreType.DMA((8,)),
            pltpu.SemaphoreType.DMA((1,)),
        ],
        compiler_params=pltpu.CompilerParams(collective_id=collective_id, has_side_effects=True),
        cost_estimate=pl.CostEstimate(
            flops=0, transcendentals=0, bytes_accessed=2 * tok_count * rows * cols * 2
        ),
    )(block)


def scatter_tok_kernel(tok_count, part_ref, out_ref, chip_in, cross_out, cross_in, send_sem, recv_sem):
    mesh_ids = pl.DeviceIdType.MESH
    me = lax.axis_index("tok")
    up = lax.rem(me + 2, tok_count)
    down = lax.rem(me + tok_count - 2, tok_count)
    far = lax.rem(me + 4, tok_count)
    partner = me + 1 - 2 * lax.rem(me, 2)
    share = out_ref.shape[0]

    barrier = pltpu.get_barrier_semaphore()
    for peer in (up, down, far, partner):
        pl.semaphore_signal(barrier, inc=1, device_id={"tok": peer}, device_id_type=mesh_ids)
    pl.semaphore_wait(barrier, 4)

    def remote(src, dst, slot, peer):
        return pltpu.make_async_remote_copy(
            src_ref=src,
            dst_ref=dst,
            send_sem=send_sem.at[slot],
            recv_sem=recv_sem.at[slot],
            device_id={"tok": peer},
            device_id_type=mesh_ids,
        )

    def family(base):
        return (
            base,
            lax.rem(base + 2, tok_count),
            lax.rem(base + tok_count - 2, tok_count),
            lax.rem(base + 4, tok_count),
        )

    def rows_of(block):
        return pl.ds(pl.multiple_of(block * share, share), share)

    sends = []
    for idx, block in enumerate(family(partner)):
        copy = remote(part_ref.at[rows_of(block)], chip_in.at[idx], idx, partner)
        copy.start()
        sends.append(copy)
    mine = family(me)
    for idx in range(4):
        remote(part_ref.at[rows_of(mine[idx])], chip_in.at[idx], idx, partner).wait_recv()

    for idx in range(1, 4):
        summed = part_ref[rows_of(mine[idx]), :] + chip_in[idx]
        cross_out[idx - 1] = summed.astype(cross_out.dtype)
    for src_idx, dst_idx, peer in ((0, 1, up), (1, 0, down), (2, 2, far)):
        copy = remote(cross_out.at[src_idx], cross_in.at[dst_idx], 4 + dst_idx, peer)
        copy.start()
        sends.append(copy)
    total = part_ref[rows_of(me), :] + chip_in[0]
    for idx, peer in ((0, up), (1, down), (2, far)):
        remote(cross_out.at[idx], cross_in.at[idx], 4 + idx, peer).wait_recv()
    for idx in range(3):
        total = total + cross_in[idx].astype(jnp.float32)
    out_ref[...] = total
    for copy in sends:
        copy.wait_send()


def scatter_over_tok(partial, tok_count, collective_id):
    assert tok_count == 8
    rows, cols = partial.shape
    share = rows // tok_count
    vmem = pltpu.MemorySpace.VMEM
    return pl.pallas_call(
        lambda *refs: scatter_tok_kernel(tok_count, *refs),
        out_shape=jax.ShapeDtypeStruct((share, cols), jnp.float32),
        in_specs=[pl.BlockSpec(memory_space=vmem)],
        out_specs=pl.BlockSpec(memory_space=vmem),
        scratch_shapes=[
            pltpu.VMEM((4, share, cols), jnp.float32),
            pltpu.VMEM((3, share, cols), jnp.bfloat16),
            pltpu.VMEM((3, share, cols), jnp.bfloat16),
            pltpu.SemaphoreType.DMA((7,)),
            pltpu.SemaphoreType.DMA((7,)),
        ],
        compiler_params=pltpu.CompilerParams(
            collective_id=collective_id, has_side_effects=True, vmem_limit_bytes=48 * 1024 * 1024
        ),
        cost_estimate=pl.CostEstimate(
            flops=8 * share * cols, transcendentals=0, bytes_accessed=rows * cols * 4 * 2
        ),
    )(partial)


def local(
    queries,
    suffix_kv,
    prefix_cache,
    q_gain,
    k_gain,
    lengths,
    group_of,
    owner_order,
    residual,
    w_out,
    attn_gain,
    ffn_in_gain,
    ffn_out_gain,
    w_gate,
    w_up,
    w_down,
):
    req_count = lax.axis_size("req")
    tok_count = lax.axis_size("tok")
    req_index = lax.axis_index("req")
    tok_index = lax.axis_index("tok")
    row_count = queries.shape[0]
    heads_here = queries.shape[1] // HD
    head_ratio = H // KVH
    kv_first = tok_index * heads_here // head_ratio
    kv_width = KVH * HD
    own_count = req_count // GROUPS

    with jax.named_scope("prefix_gather"):
        pref_keys = lax.dynamic_slice_in_dim(prefix_cache, kv_first * HD, HD, 1)
        pref_vals = lax.dynamic_slice_in_dim(prefix_cache, kv_width + kv_first * HD, HD, 1)
        pref_kv = jnp.concatenate([pref_keys, pref_vals], axis=1)
        half_rows = pref_kv.shape[0] // 2
        core = tok_index % 2
        my_half = lax.dynamic_slice_in_dim(pref_kv, core * half_rows, half_rows, 0)
        gathered = lax.all_gather(my_half, "req", axis=0, tiled=False)
        w_out_all = gather_over_tok(w_out, tok_count, 0)
        gathered, w_out_all = lax.optimization_barrier((gathered, w_out_all))
        own_group = group_of[req_index]
        owner_ids = lax.dynamic_slice_in_dim(owner_order, own_group * own_count, own_count)
        picked = jnp.take(gathered, owner_ids, axis=0).reshape(-1, 2 * HD)
        partner = [(t, t ^ 1) for t in range(tok_count)]
        swapped = lax.ppermute(picked, "tok", perm=partner)
        shared = jnp.concatenate([picked, swapped], axis=0)

    with jax.named_scope("attention"):
        query_normed = norm_heads(queries, q_gain, heads_here)
        suf_keys = norm_heads(
            lax.dynamic_slice_in_dim(suffix_kv, kv_first * HD, HD, 1), k_gain, 1
        )
        suf_vals = lax.dynamic_slice_in_dim(suffix_kv, kv_width + kv_first * HD, HD, 1)
        all_keys = jnp.concatenate([shared[:, :HD], suf_keys], axis=0)
        all_vals = jnp.concatenate([shared[:, HD:], suf_vals], axis=0)
        seg_ends = jnp.cumsum(lengths[0])
        positions = jnp.arange(row_count, dtype=jnp.int32)
        segment = jnp.sum((positions[:, None] >= seg_ends[None, :]).astype(jnp.int32), axis=1)
        causal = (segment[:, None] == segment[None, :]) & (positions[None, :] <= positions[:, None])
        visible = jnp.concatenate(
            [jnp.ones((row_count, shared.shape[0]), jnp.bool_), causal], axis=1
        )
        outputs = []
        for head_idx in range(heads_here):
            head_q = query_normed[:, head_idx * HD:(head_idx + 1) * HD]
            scores = jnp.dot(head_q, all_keys.T, preferred_element_type=jnp.float32) * HD ** (-0.5)
            scores = jnp.where(visible, scores, MASKED)
            row_max = jnp.max(scores, axis=-1, keepdims=True)
            weights = jnp.exp(scores - row_max)
            row_sum = jnp.sum(weights, axis=-1, keepdims=True)
            head_out = jnp.dot(
                weights.astype(jnp.bfloat16), all_vals, preferred_element_type=jnp.float32
            ) / row_sum
            outputs.append(head_out)
        attention = jnp.concatenate(outputs, axis=1).astype(jnp.bfloat16)

    share = row_count // tok_count
    first_row = tok_index * share
    with jax.named_scope("out_projection"):
        attention_all = gather_over_tok(attention, tok_count, 1)
        projected = jnp.einsum(
            "srd,sdc->rc", attention_all, w_out_all, preferred_element_type=jnp.float32
        )
        mixed_rows = residual.astype(jnp.float32) + rms_scale(projected, attn_gain)
        normed = rms_scale(mixed_rows, ffn_in_gain).astype(jnp.bfloat16)
        mixed_share = lax.dynamic_slice_in_dim(mixed_rows, first_row, share, 0)
    with jax.named_scope("feed_forward"):
        gate = jnp.dot(normed, w_gate, preferred_element_type=jnp.float32)
        upward = jnp.dot(normed, w_up, preferred_element_type=jnp.float32)
        hidden = (jax.nn.gelu(gate, approximate=True) * upward).astype(jnp.bfloat16)
        down_share = scatter_over_tok(
            jnp.dot(hidden, w_down, preferred_element_type=jnp.float32), tok_count, 2
        )
    return (mixed_share + rms_scale(down_share.astype(jnp.float32), ffn_out_gain)).astype(
        jnp.bfloat16
    )


def solution(mesh):
    in_specs = (
        P("req", "tok"),
        P("req", None),
        P("req", None),
        P(),
        P(),
        P("req", None),
        P(),
        P(),
        P("req", None),
        P("tok", None),
        P(),
        P(),
        P(),
        P(None, "tok"),
        P(None, "tok"),
        P("tok", None),
    )
    out_specs = P(("req", "tok"), None)
    return jax.shard_map(local, mesh=mesh, in_specs=in_specs, out_specs=out_specs, check_vma=False)
```

```python
import jax
import jax.numpy as jnp
from jax import lax
from jax.sharding import PartitionSpec as P
from jax.experimental import pallas as pl
from jax.experimental.pallas import tpu as pltpu

H = 8
KVH = 4
HD = 256
GROUPS = 2


EPSILON = 1e-06
MASKED = -1e30


def rms_scale(values_in, gain_vec):
    return (
        values_in
        * lax.rsqrt(jnp.mean(values_in * values_in, axis=-1, keepdims=True) + EPSILON)
        * gain_vec
    )


def norm_heads(values_in, gain_vec, head_count):
    row_count = values_in.shape[0]
    shaped = values_in.astype(jnp.float32).reshape(row_count, head_count, HD)
    return rms_scale(shaped, gain_vec).astype(jnp.bfloat16).reshape(row_count, head_count * HD)


def gather_tok_kernel(tok_count, w_ref, out_ref, send_sem, recv_sem, local_sem):
    mesh_ids = pl.DeviceIdType.MESH
    me = lax.axis_index("tok")
    up = lax.rem(me + 2, tok_count)
    down = lax.rem(me + tok_count - 2, tok_count)
    far = lax.rem(me + 4, tok_count)
    partner = me + 1 - 2 * lax.rem(me, 2)
    half = w_ref.shape[0] // 2

    barrier = pltpu.get_barrier_semaphore()
    for peer in (up, down, partner):
        pl.semaphore_signal(barrier, inc=1, device_id={"tok": peer}, device_id_type=mesh_ids)
    pl.semaphore_wait(barrier, 3)

    def remote(src, dst, slot, peer):
        return pltpu.make_async_remote_copy(
            src_ref=src,
            dst_ref=dst,
            send_sem=send_sem.at[slot],
            recv_sem=recv_sem.at[slot],
            device_id={"tok": peer},
            device_id_type=mesh_ids,
        )

    local = pltpu.make_async_copy(w_ref, out_ref.at[me], local_sem.at[0])
    local.start()
    to_up = remote(w_ref, out_ref.at[me], 0, up)
    to_down = remote(w_ref, out_ref.at[me], 1, down)
    to_up.start()
    to_down.start()
    remote(w_ref, out_ref.at[down], 0, down).wait_recv()
    remote(w_ref, out_ref.at[up], 1, up).wait_recv()

    first = pl.ds(0, half)
    second = pl.ds(half, half)
    fwd_up = remote(out_ref.at[down, first], out_ref.at[down, first], 2, up)
    fwd_down = remote(out_ref.at[up, second], out_ref.at[up, second], 3, down)
    fwd_up.start()
    fwd_down.start()
    remote(out_ref.at[far, first], out_ref.at[far, first], 2, down).wait_recv()
    remote(out_ref.at[far, second], out_ref.at[far, second], 3, up).wait_recv()
    local.wait()

    mine = (me, up, down, far)
    theirs = (
        partner,
        lax.rem(partner + 2, tok_count),
        lax.rem(partner + tok_count - 2, tok_count),
        lax.rem(partner + 4, tok_count),
    )
    to_partner = []
    for idx, slot in enumerate(mine):
        copy = remote(out_ref.at[slot], out_ref.at[slot], 4 + idx, partner)
        copy.start()
        to_partner.append(copy)
    for idx, slot in enumerate(theirs):
        remote(out_ref.at[slot], out_ref.at[slot], 4 + idx, partner).wait_recv()
    for copy in [to_up, to_down, fwd_up, fwd_down] + to_partner:
        copy.wait_send()


def gather_req_kernel(line, block_ref, out_ref, send_sem, recv_sem, local_sem):
    mesh_ids = pl.DeviceIdType.MESH
    me = lax.axis_index("req")
    core = lax.rem(lax.axis_index("tok"), 2)
    first_stride = 1 + (line - 1) * core
    second_stride = line - (line - 1) * core
    half = block_ref.shape[0] // 2
    top = pl.ds(0, half)
    bottom = pl.ds(half, half)

    def step(index, stride, offset):
        pos = lax.rem(index // stride, line)
        return index + (lax.rem(pos + offset + line, line) - pos) * stride

    plus1, minus1, far1 = (step(me, first_stride, d) for d in (1, -1, 2))
    plus2, minus2, far2 = (step(me, second_stride, d) for d in (1, -1, 2))

    barrier = pltpu.get_barrier_semaphore()
    for peer in (plus1, minus1, plus2, minus2):
        pl.semaphore_signal(barrier, inc=1, device_id={"req": peer}, device_id_type=mesh_ids)
    pl.semaphore_wait(barrier, 4)

    def remote(src, dst, slot, peer):
        return pltpu.make_async_remote_copy(
            src_ref=src,
            dst_ref=dst,
            send_sem=send_sem.at[slot],
            recv_sem=recv_sem.at[slot],
            device_id={"req": peer},
            device_id_type=mesh_ids,
        )

    sends = []

    def send(src, dst, slot, peer):
        copy = remote(src, dst, slot, peer)
        copy.start()
        sends.append(copy)

    local = pltpu.make_async_copy(block_ref, out_ref.at[me], local_sem.at[0])
    local.start()
    send(block_ref, out_ref.at[me], 0, plus1)
    send(block_ref, out_ref.at[me], 1, minus1)
    remote(block_ref, out_ref.at[minus1], 0, minus1).wait_recv()
    remote(block_ref, out_ref.at[plus1], 1, plus1).wait_recv()
    send(out_ref.at[minus1, top], out_ref.at[minus1, top], 2, plus1)
    send(out_ref.at[plus1, bottom], out_ref.at[plus1, bottom], 3, minus1)
    remote(out_ref.at[far1, top], out_ref.at[far1, top], 2, minus1).wait_recv()
    remote(out_ref.at[far1, bottom], out_ref.at[far1, bottom], 3, plus1).wait_recv()
    local.wait()

    offsets = (0, 1, -1, 2)

    def line_of(index):
        return [step(index, first_stride, d) for d in offsets]

    for idx, slot in enumerate(line_of(me)):
        send(out_ref.at[slot], out_ref.at[slot], 4 + idx, plus2)
        send(out_ref.at[slot], out_ref.at[slot], 8 + idx, minus2)
    from_minus = line_of(minus2)
    from_plus = line_of(plus2)
    for idx in range(len(offsets)):
        remote(out_ref.at[from_minus[idx]], out_ref.at[from_minus[idx]], 4 + idx, minus2).wait_recv()
        remote(out_ref.at[from_plus[idx]], out_ref.at[from_plus[idx]], 8 + idx, plus2).wait_recv()
    for idx in range(len(offsets)):
        send(out_ref.at[from_minus[idx], top], out_ref.at[from_minus[idx], top], 12 + idx, plus2)
        send(out_ref.at[from_plus[idx], bottom], out_ref.at[from_plus[idx], bottom], 16 + idx, minus2)
    from_far = line_of(far2)
    for idx in range(len(offsets)):
        slot = from_far[idx]
        remote(out_ref.at[slot, top], out_ref.at[slot, top], 12 + idx, minus2).wait_recv()
        remote(out_ref.at[slot, bottom], out_ref.at[slot, bottom], 16 + idx, plus2).wait_recv()
    for copy in sends:
        copy.wait_send()


def gather_over_req(block, req_count, collective_id):
    line = 4
    assert req_count == line * line
    rows, cols = block.shape
    return pl.pallas_call(
        lambda *refs: gather_req_kernel(line, *refs),
        out_shape=jax.ShapeDtypeStruct((req_count, rows, cols), block.dtype),
        in_specs=[pl.BlockSpec(memory_space=pl.ANY)],
        out_specs=pl.BlockSpec(memory_space=pl.ANY),
        scratch_shapes=[
            pltpu.SemaphoreType.DMA((20,)),
            pltpu.SemaphoreType.DMA((20,)),
            pltpu.SemaphoreType.DMA((1,)),
        ],
        compiler_params=pltpu.CompilerParams(collective_id=collective_id, has_side_effects=True),
        cost_estimate=pl.CostEstimate(
            flops=0, transcendentals=0, bytes_accessed=2 * req_count * rows * cols * 2
        ),
    )(block)


def gather_over_tok(block, tok_count, collective_id):
    assert tok_count == 8
    rows, cols = block.shape
    return pl.pallas_call(
        lambda *refs: gather_tok_kernel(tok_count, *refs),
        out_shape=jax.ShapeDtypeStruct((tok_count, rows, cols), block.dtype),
        in_specs=[pl.BlockSpec(memory_space=pl.ANY)],
        out_specs=pl.BlockSpec(memory_space=pl.ANY),
        scratch_shapes=[
            pltpu.SemaphoreType.DMA((8,)),
            pltpu.SemaphoreType.DMA((8,)),
            pltpu.SemaphoreType.DMA((1,)),
        ],
        compiler_params=pltpu.CompilerParams(collective_id=collective_id, has_side_effects=True),
        cost_estimate=pl.CostEstimate(
            flops=0, transcendentals=0, bytes_accessed=2 * tok_count * rows * cols * 2
        ),
    )(block)


def scatter_tok_kernel(tok_count, part_ref, out_ref, chip_in, cross_out, cross_in, send_sem, recv_sem):
    mesh_ids = pl.DeviceIdType.MESH
    me = lax.axis_index("tok")
    up = lax.rem(me + 2, tok_count)
    down = lax.rem(me + tok_count - 2, tok_count)
    far = lax.rem(me + 4, tok_count)
    partner = me + 1 - 2 * lax.rem(me, 2)
    share = out_ref.shape[0]

    barrier = pltpu.get_barrier_semaphore()
    for peer in (up, down, far, partner):
        pl.semaphore_signal(barrier, inc=1, device_id={"tok": peer}, device_id_type=mesh_ids)
    pl.semaphore_wait(barrier, 4)

    def remote(src, dst, slot, peer):
        return pltpu.make_async_remote_copy(
            src_ref=src,
            dst_ref=dst,
            send_sem=send_sem.at[slot],
            recv_sem=recv_sem.at[slot],
            device_id={"tok": peer},
            device_id_type=mesh_ids,
        )

    def family(base):
        return (
            base,
            lax.rem(base + 2, tok_count),
            lax.rem(base + tok_count - 2, tok_count),
            lax.rem(base + 4, tok_count),
        )

    def rows_of(block):
        return pl.ds(pl.multiple_of(block * share, share), share)

    sends = []
    for idx, block in enumerate(family(partner)):
        copy = remote(part_ref.at[rows_of(block)], chip_in.at[idx], idx, partner)
        copy.start()
        sends.append(copy)
    mine = family(me)
    for idx in range(4):
        remote(part_ref.at[rows_of(mine[idx])], chip_in.at[idx], idx, partner).wait_recv()

    for idx in range(1, 4):
        summed = part_ref[rows_of(mine[idx]), :] + chip_in[idx]
        cross_out[idx - 1] = summed.astype(cross_out.dtype)
    for src_idx, dst_idx, peer in ((0, 1, up), (1, 0, down), (2, 2, far)):
        copy = remote(cross_out.at[src_idx], cross_in.at[dst_idx], 4 + dst_idx, peer)
        copy.start()
        sends.append(copy)
    total = part_ref[rows_of(me), :] + chip_in[0]
    for idx, peer in ((0, up), (1, down), (2, far)):
        remote(cross_out.at[idx], cross_in.at[idx], 4 + idx, peer).wait_recv()
    for idx in range(3):
        total = total + cross_in[idx].astype(jnp.float32)
    out_ref[...] = total
    for copy in sends:
        copy.wait_send()


def scatter_over_tok(partial, tok_count, collective_id):
    assert tok_count == 8
    rows, cols = partial.shape
    share = rows // tok_count
    vmem = pltpu.MemorySpace.VMEM
    return pl.pallas_call(
        lambda *refs: scatter_tok_kernel(tok_count, *refs),
        out_shape=jax.ShapeDtypeStruct((share, cols), jnp.float32),
        in_specs=[pl.BlockSpec(memory_space=vmem)],
        out_specs=pl.BlockSpec(memory_space=vmem),
        scratch_shapes=[
            pltpu.VMEM((4, share, cols), jnp.float32),
            pltpu.VMEM((3, share, cols), jnp.bfloat16),
            pltpu.VMEM((3, share, cols), jnp.bfloat16),
            pltpu.SemaphoreType.DMA((7,)),
            pltpu.SemaphoreType.DMA((7,)),
        ],
        compiler_params=pltpu.CompilerParams(
            collective_id=collective_id, has_side_effects=True, vmem_limit_bytes=48 * 1024 * 1024
        ),
        cost_estimate=pl.CostEstimate(
            flops=8 * share * cols, transcendentals=0, bytes_accessed=rows * cols * 4 * 2
        ),
    )(partial)


def local(
    queries,
    suffix_kv,
    prefix_cache,
    q_gain,
    k_gain,
    lengths,
    group_of,
    owner_order,
    residual,
    w_out,
    attn_gain,
    ffn_in_gain,
    ffn_out_gain,
    w_gate,
    w_up,
    w_down,
):
    req_count = lax.axis_size("req")
    tok_count = lax.axis_size("tok")
    req_index = lax.axis_index("req")
    tok_index = lax.axis_index("tok")
    row_count = queries.shape[0]
    heads_here = queries.shape[1] // HD
    head_ratio = H // KVH
    kv_first = tok_index * heads_here // head_ratio
    kv_width = KVH * HD
    own_count = req_count // GROUPS

    with jax.named_scope("prefix_gather"):
        pref_keys = lax.dynamic_slice_in_dim(prefix_cache, kv_first * HD, HD, 1)
        pref_vals = lax.dynamic_slice_in_dim(prefix_cache, kv_width + kv_first * HD, HD, 1)
        pref_kv = jnp.concatenate([pref_keys, pref_vals], axis=1)
        half_rows = pref_kv.shape[0] // 2
        core = tok_index % 2
        my_half = lax.dynamic_slice_in_dim(pref_kv, core * half_rows, half_rows, 0)
        gathered = gather_over_req(my_half, req_count, 0)
        own_group = group_of[req_index]
        owner_ids = lax.dynamic_slice_in_dim(owner_order, own_group * own_count, own_count)
        picked = jnp.take(gathered, owner_ids, axis=0).reshape(-1, 2 * HD)
        partner = [(t, t ^ 1) for t in range(tok_count)]
        swapped = lax.ppermute(picked, "tok", perm=partner)
        shared = jnp.concatenate([picked, swapped], axis=0)

    with jax.named_scope("attention"):
        query_normed = norm_heads(queries, q_gain, heads_here)
        suf_keys = norm_heads(
            lax.dynamic_slice_in_dim(suffix_kv, kv_first * HD, HD, 1), k_gain, 1
        )
        suf_vals = lax.dynamic_slice_in_dim(suffix_kv, kv_width + kv_first * HD, HD, 1)
        all_keys = jnp.concatenate([shared[:, :HD], suf_keys], axis=0)
        all_vals = jnp.concatenate([shared[:, HD:], suf_vals], axis=0)
        seg_ends = jnp.cumsum(lengths[0])
        positions = jnp.arange(row_count, dtype=jnp.int32)
        segment = jnp.sum((positions[:, None] >= seg_ends[None, :]).astype(jnp.int32), axis=1)
        causal = (segment[:, None] == segment[None, :]) & (positions[None, :] <= positions[:, None])
        visible = jnp.concatenate(
            [jnp.ones((row_count, shared.shape[0]), jnp.bool_), causal], axis=1
        )
        outputs = []
        for head_idx in range(heads_here):
            head_q = query_normed[:, head_idx * HD:(head_idx + 1) * HD]
            scores = jnp.dot(head_q, all_keys.T, preferred_element_type=jnp.float32) * HD ** (-0.5)
            scores = jnp.where(visible, scores, MASKED)
            row_max = jnp.max(scores, axis=-1, keepdims=True)
            weights = jnp.exp(scores - row_max)
            row_sum = jnp.sum(weights, axis=-1, keepdims=True)
            head_out = jnp.dot(
                weights.astype(jnp.bfloat16), all_vals, preferred_element_type=jnp.float32
            ) / row_sum
            outputs.append(head_out)
        attention = jnp.concatenate(outputs, axis=1).astype(jnp.bfloat16)

    share = row_count // tok_count
    first_row = tok_index * share
    with jax.named_scope("out_projection"):
        projected = scatter_over_tok(
            jnp.dot(attention, w_out, preferred_element_type=jnp.float32), tok_count, 3
        )
        residual_share = lax.dynamic_slice_in_dim(residual, first_row, share, 0)
        mixed_share = residual_share.astype(jnp.float32) + rms_scale(projected, attn_gain)
        normed_share = rms_scale(mixed_share, ffn_in_gain).astype(jnp.bfloat16)
        normed = gather_over_tok(normed_share, tok_count, 1).reshape(row_count, -1)
    with jax.named_scope("feed_forward"):
        gate = jnp.dot(normed, w_gate, preferred_element_type=jnp.float32)
        upward = jnp.dot(normed, w_up, preferred_element_type=jnp.float32)
        hidden = (jax.nn.gelu(gate, approximate=True) * upward).astype(jnp.bfloat16)
        down_share = scatter_over_tok(
            jnp.dot(hidden, w_down, preferred_element_type=jnp.float32), tok_count, 2
        )
    return (mixed_share + rms_scale(down_share.astype(jnp.float32), ffn_out_gain)).astype(
        jnp.bfloat16
    )


def solution(mesh):
    in_specs = (
        P("req", "tok"),
        P("req", None),
        P("req", None),
        P(),
        P(),
        P("req", None),
        P(),
        P(),
        P("req", None),
        P("tok", None),
        P(),
        P(),
        P(),
        P(None, "tok"),
        P(None, "tok"),
        P("tok", None),
    )
    out_specs = P(("req", "tok"), None)
    return jax.shard_map(local, mesh=mesh, in_specs=in_specs, out_specs=out_specs, check_vma=False)
```

```python
import jax
import jax.numpy as jnp
from jax import lax
from jax.sharding import PartitionSpec as P
from jax.experimental import pallas as pl
from jax.experimental.pallas import tpu as pltpu

H = 8
KVH = 4
HD = 256
GROUPS = 2


EPSILON = 1e-06
MASKED = -1e30


def rms_scale(values_in, gain_vec):
    return (
        values_in
        * lax.rsqrt(jnp.mean(values_in * values_in, axis=-1, keepdims=True) + EPSILON)
        * gain_vec
    )


def norm_heads(values_in, gain_vec, head_count):
    row_count = values_in.shape[0]
    shaped = values_in.astype(jnp.float32).reshape(row_count, head_count, HD)
    return rms_scale(shaped, gain_vec).astype(jnp.bfloat16).reshape(row_count, head_count * HD)


def req_ring(line, block_ref, out_ref, send_sem, recv_sem, local_sem, sends):
    mesh_ids = pl.DeviceIdType.MESH
    me = lax.axis_index("req")
    core = lax.rem(lax.axis_index("tok"), 2)
    first_stride = 1 + (line - 1) * core
    second_stride = line - (line - 1) * core
    half = block_ref.shape[0] // 2
    top = pl.ds(0, half)
    bottom = pl.ds(half, half)

    def step(index, stride, offset):
        pos = lax.rem(index // stride, line)
        return index + (lax.rem(pos + offset + line, line) - pos) * stride

    plus1, minus1, far1 = (step(me, first_stride, d) for d in (1, -1, 2))
    plus2, minus2, far2 = (step(me, second_stride, d) for d in (1, -1, 2))

    def remote(src, dst, slot, peer):
        return pltpu.make_async_remote_copy(
            src_ref=src,
            dst_ref=dst,
            send_sem=send_sem.at[slot],
            recv_sem=recv_sem.at[slot],
            device_id={"req": peer},
            device_id_type=mesh_ids,
        )

    def send(src, dst, slot, peer):
        copy = remote(src, dst, slot, peer)
        copy.start()
        sends.append(copy)

    local = pltpu.make_async_copy(block_ref, out_ref.at[me], local_sem.at[0])
    local.start()
    send(block_ref, out_ref.at[me], 0, plus1)
    send(block_ref, out_ref.at[me], 1, minus1)
    yield
    remote(block_ref, out_ref.at[minus1], 0, minus1).wait_recv()
    remote(block_ref, out_ref.at[plus1], 1, plus1).wait_recv()
    send(out_ref.at[minus1, top], out_ref.at[minus1, top], 2, plus1)
    send(out_ref.at[plus1, bottom], out_ref.at[plus1, bottom], 3, minus1)
    remote(out_ref.at[far1, top], out_ref.at[far1, top], 2, minus1).wait_recv()
    remote(out_ref.at[far1, bottom], out_ref.at[far1, bottom], 3, plus1).wait_recv()
    yield
    local.wait()

    offsets = (0, 1, -1, 2)

    def line_of(index):
        return [step(index, first_stride, d) for d in offsets]

    for idx, slot in enumerate(line_of(me)):
        send(out_ref.at[slot], out_ref.at[slot], 4 + idx, plus2)
        send(out_ref.at[slot], out_ref.at[slot], 8 + idx, minus2)
    from_minus = line_of(minus2)
    from_plus = line_of(plus2)
    yield
    for idx in range(len(offsets)):
        remote(out_ref.at[from_minus[idx]], out_ref.at[from_minus[idx]], 4 + idx, minus2).wait_recv()
        remote(out_ref.at[from_plus[idx]], out_ref.at[from_plus[idx]], 8 + idx, plus2).wait_recv()
    for idx in range(len(offsets)):
        send(out_ref.at[from_minus[idx], top], out_ref.at[from_minus[idx], top], 12 + idx, plus2)
        send(out_ref.at[from_plus[idx], bottom], out_ref.at[from_plus[idx], bottom], 16 + idx, minus2)
    yield
    from_far = line_of(far2)
    for idx in range(len(offsets)):
        slot = from_far[idx]
        remote(out_ref.at[slot, top], out_ref.at[slot, top], 12 + idx, minus2).wait_recv()
        remote(out_ref.at[slot, bottom], out_ref.at[slot, bottom], 16 + idx, plus2).wait_recv()
    yield


def tok_peers(tok_count):
    me = lax.axis_index("tok")
    up = lax.rem(me + 2, tok_count)
    down = lax.rem(me + tok_count - 2, tok_count)
    partner = me + 1 - 2 * lax.rem(me, 2)
    return up, down, partner


def tok_ring(tok_count, w_ref, out_ref, send_sem, recv_sem, local_sem, sends):
    mesh_ids = pl.DeviceIdType.MESH
    me = lax.axis_index("tok")
    up = lax.rem(me + 2, tok_count)
    down = lax.rem(me + tok_count - 2, tok_count)
    far = lax.rem(me + 4, tok_count)
    partner = me + 1 - 2 * lax.rem(me, 2)
    half = w_ref.shape[0] // 2

    def remote(src, dst, slot, peer):
        return pltpu.make_async_remote_copy(
            src_ref=src,
            dst_ref=dst,
            send_sem=send_sem.at[slot],
            recv_sem=recv_sem.at[slot],
            device_id={"tok": peer},
            device_id_type=mesh_ids,
        )

    local = pltpu.make_async_copy(w_ref, out_ref.at[me], local_sem.at[0])
    local.start()
    to_up = remote(w_ref, out_ref.at[me], 0, up)
    to_down = remote(w_ref, out_ref.at[me], 1, down)
    to_up.start()
    to_down.start()
    yield
    remote(w_ref, out_ref.at[down], 0, down).wait_recv()
    remote(w_ref, out_ref.at[up], 1, up).wait_recv()

    first = pl.ds(0, half)
    second = pl.ds(half, half)
    fwd_up = remote(out_ref.at[down, first], out_ref.at[down, first], 2, up)
    fwd_down = remote(out_ref.at[up, second], out_ref.at[up, second], 3, down)
    fwd_up.start()
    fwd_down.start()
    yield
    remote(out_ref.at[far, first], out_ref.at[far, first], 2, down).wait_recv()
    remote(out_ref.at[far, second], out_ref.at[far, second], 3, up).wait_recv()
    local.wait()

    mine = (me, up, down, far)
    theirs = (
        partner,
        lax.rem(partner + 2, tok_count),
        lax.rem(partner + tok_count - 2, tok_count),
        lax.rem(partner + 4, tok_count),
    )
    to_partner = []
    for idx, slot in enumerate(mine):
        copy = remote(out_ref.at[slot], out_ref.at[slot], 4 + idx, partner)
        copy.start()
        to_partner.append(copy)
    yield
    for idx, slot in enumerate(theirs):
        remote(out_ref.at[slot], out_ref.at[slot], 4 + idx, partner).wait_recv()
    sends.extend([to_up, to_down, fwd_up, fwd_down] + to_partner)
    yield


def gather_tok_kernel(tok_count, w_ref, out_ref, send_sem, recv_sem, local_sem):
    mesh_ids = pl.DeviceIdType.MESH
    barrier = pltpu.get_barrier_semaphore()
    for peer in tok_peers(tok_count):
        pl.semaphore_signal(barrier, inc=1, device_id={"tok": peer}, device_id_type=mesh_ids)
    pl.semaphore_wait(barrier, 3)
    sends = []
    for _ in tok_ring(tok_count, w_ref, out_ref, send_sem, recv_sem, local_sem, sends):
        pass
    for copy in sends:
        copy.wait_send()


def prefetch_kernel(
    line, tok_count, w_ref, kv_ref, w_all, kv_all, w_send, w_recv, w_local, kv_send, kv_recv, kv_local
):
    mesh_ids = pl.DeviceIdType.MESH
    me = lax.axis_index("req")
    core = lax.rem(lax.axis_index("tok"), 2)
    barrier = pltpu.get_barrier_semaphore()
    for peer in tok_peers(tok_count):
        pl.semaphore_signal(barrier, inc=1, device_id={"tok": peer}, device_id_type=mesh_ids)
    for stride in (1 + (line - 1) * core, line - (line - 1) * core):
        pos = lax.rem(me // stride, line)
        for offset in (1, line - 1):
            peer = me + (lax.rem(pos + offset, line) - pos) * stride
            pl.semaphore_signal(barrier, inc=1, device_id={"req": peer}, device_id_type=mesh_ids)
    pl.semaphore_wait(barrier, 7)
    sends = []
    w_steps = tok_ring(tok_count, w_ref, w_all, w_send, w_recv, w_local, sends)
    kv_steps = req_ring(line, kv_ref, kv_all, kv_send, kv_recv, kv_local, sends)
    for steps in (w_steps, kv_steps, kv_steps, kv_steps, w_steps, kv_steps, w_steps, kv_steps, w_steps):
        next(steps)
    for steps in (w_steps, kv_steps):
        for _ in steps:
            pass
    for copy in sends:
        copy.wait_send()


def prefetch(w_block, kv_block, tok_count, req_count, collective_id):
    line = 4
    assert tok_count == 8 and req_count == line * line
    w_rows, w_cols = w_block.shape
    kv_rows, kv_cols = kv_block.shape
    any_space = pl.BlockSpec(memory_space=pl.ANY)
    return pl.pallas_call(
        lambda *refs: prefetch_kernel(line, tok_count, *refs),
        out_shape=(
            jax.ShapeDtypeStruct((tok_count, w_rows, w_cols), w_block.dtype),
            jax.ShapeDtypeStruct((req_count, kv_rows, kv_cols), kv_block.dtype),
        ),
        in_specs=[any_space, any_space],
        out_specs=(any_space, any_space),
        scratch_shapes=[
            pltpu.SemaphoreType.DMA((8,)),
            pltpu.SemaphoreType.DMA((8,)),
            pltpu.SemaphoreType.DMA((1,)),
            pltpu.SemaphoreType.DMA((20,)),
            pltpu.SemaphoreType.DMA((20,)),
            pltpu.SemaphoreType.DMA((1,)),
        ],
        compiler_params=pltpu.CompilerParams(collective_id=collective_id, has_side_effects=True),
        cost_estimate=pl.CostEstimate(
            flops=0,
            transcendentals=0,
            bytes_accessed=2 * (tok_count * w_rows * w_cols + req_count * kv_rows * kv_cols) * 2,
        ),
    )(w_block, kv_block)


def gather_over_tok(block, tok_count, collective_id):
    assert tok_count == 8
    rows, cols = block.shape
    return pl.pallas_call(
        lambda *refs: gather_tok_kernel(tok_count, *refs),
        out_shape=jax.ShapeDtypeStruct((tok_count, rows, cols), block.dtype),
        in_specs=[pl.BlockSpec(memory_space=pl.ANY)],
        out_specs=pl.BlockSpec(memory_space=pl.ANY),
        scratch_shapes=[
            pltpu.SemaphoreType.DMA((8,)),
            pltpu.SemaphoreType.DMA((8,)),
            pltpu.SemaphoreType.DMA((1,)),
        ],
        compiler_params=pltpu.CompilerParams(collective_id=collective_id, has_side_effects=True),
        cost_estimate=pl.CostEstimate(
            flops=0, transcendentals=0, bytes_accessed=2 * tok_count * rows * cols * 2
        ),
    )(block)


def scatter_tok_kernel(tok_count, part_ref, out_ref, chip_in, cross_out, cross_in, send_sem, recv_sem):
    mesh_ids = pl.DeviceIdType.MESH
    me = lax.axis_index("tok")
    up = lax.rem(me + 2, tok_count)
    down = lax.rem(me + tok_count - 2, tok_count)
    far = lax.rem(me + 4, tok_count)
    partner = me + 1 - 2 * lax.rem(me, 2)
    share = out_ref.shape[0]

    barrier = pltpu.get_barrier_semaphore()
    for peer in (up, down, far, partner):
        pl.semaphore_signal(barrier, inc=1, device_id={"tok": peer}, device_id_type=mesh_ids)
    pl.semaphore_wait(barrier, 4)

    def remote(src, dst, slot, peer):
        return pltpu.make_async_remote_copy(
            src_ref=src,
            dst_ref=dst,
            send_sem=send_sem.at[slot],
            recv_sem=recv_sem.at[slot],
            device_id={"tok": peer},
            device_id_type=mesh_ids,
        )

    def family(base):
        return (
            base,
            lax.rem(base + 2, tok_count),
            lax.rem(base + tok_count - 2, tok_count),
            lax.rem(base + 4, tok_count),
        )

    def rows_of(block):
        return pl.ds(pl.multiple_of(block * share, share), share)

    sends = []
    for idx, block in enumerate(family(partner)):
        copy = remote(part_ref.at[rows_of(block)], chip_in.at[idx], idx, partner)
        copy.start()
        sends.append(copy)
    mine = family(me)
    for idx in range(4):
        remote(part_ref.at[rows_of(mine[idx])], chip_in.at[idx], idx, partner).wait_recv()

    for idx in range(1, 4):
        summed = part_ref[rows_of(mine[idx]), :] + chip_in[idx]
        cross_out[idx - 1] = summed.astype(cross_out.dtype)
    for src_idx, dst_idx, peer in ((0, 1, up), (1, 0, down), (2, 2, far)):
        copy = remote(cross_out.at[src_idx], cross_in.at[dst_idx], 4 + dst_idx, peer)
        copy.start()
        sends.append(copy)
    total = part_ref[rows_of(me), :] + chip_in[0]
    for idx, peer in ((0, up), (1, down), (2, far)):
        remote(cross_out.at[idx], cross_in.at[idx], 4 + idx, peer).wait_recv()
    for idx in range(3):
        total = total + cross_in[idx].astype(jnp.float32)
    out_ref[...] = total
    for copy in sends:
        copy.wait_send()


def scatter_over_tok(partial, tok_count, collective_id):
    assert tok_count == 8
    rows, cols = partial.shape
    share = rows // tok_count
    vmem = pltpu.MemorySpace.VMEM
    return pl.pallas_call(
        lambda *refs: scatter_tok_kernel(tok_count, *refs),
        out_shape=jax.ShapeDtypeStruct((share, cols), jnp.float32),
        in_specs=[pl.BlockSpec(memory_space=vmem)],
        out_specs=pl.BlockSpec(memory_space=vmem),
        scratch_shapes=[
            pltpu.VMEM((4, share, cols), jnp.float32),
            pltpu.VMEM((3, share, cols), jnp.bfloat16),
            pltpu.VMEM((3, share, cols), jnp.bfloat16),
            pltpu.SemaphoreType.DMA((7,)),
            pltpu.SemaphoreType.DMA((7,)),
        ],
        compiler_params=pltpu.CompilerParams(
            collective_id=collective_id, has_side_effects=True, vmem_limit_bytes=48 * 1024 * 1024
        ),
        cost_estimate=pl.CostEstimate(
            flops=8 * share * cols, transcendentals=0, bytes_accessed=rows * cols * 4 * 2
        ),
    )(partial)


def local(
    queries,
    suffix_kv,
    prefix_cache,
    q_gain,
    k_gain,
    lengths,
    group_of,
    owner_order,
    residual,
    w_out,
    attn_gain,
    ffn_in_gain,
    ffn_out_gain,
    w_gate,
    w_up,
    w_down,
):
    req_count = lax.axis_size("req")
    tok_count = lax.axis_size("tok")
    req_index = lax.axis_index("req")
    tok_index = lax.axis_index("tok")
    row_count = queries.shape[0]
    heads_here = queries.shape[1] // HD
    head_ratio = H // KVH
    kv_first = tok_index * heads_here // head_ratio
    kv_width = KVH * HD
    own_count = req_count // GROUPS

    with jax.named_scope("prefix_gather"):
        pref_keys = lax.dynamic_slice_in_dim(prefix_cache, kv_first * HD, HD, 1)
        pref_vals = lax.dynamic_slice_in_dim(prefix_cache, kv_width + kv_first * HD, HD, 1)
        pref_kv = jnp.concatenate([pref_keys, pref_vals], axis=1)
        half_rows = pref_kv.shape[0] // 2
        core = tok_index % 2
        my_half = lax.dynamic_slice_in_dim(pref_kv, core * half_rows, half_rows, 0)
        w_out_all, gathered = prefetch(w_out, my_half, tok_count, req_count, 0)
        own_group = group_of[req_index]
        owner_ids = lax.dynamic_slice_in_dim(owner_order, own_group * own_count, own_count)
        picked = jnp.take(gathered, owner_ids, axis=0).reshape(-1, 2 * HD)
        partner = [(t, t ^ 1) for t in range(tok_count)]
        swapped = lax.ppermute(picked, "tok", perm=partner)
        shared = jnp.concatenate([picked, swapped], axis=0)

    with jax.named_scope("attention"):
        query_normed = norm_heads(queries, q_gain, heads_here)
        suf_keys = norm_heads(
            lax.dynamic_slice_in_dim(suffix_kv, kv_first * HD, HD, 1), k_gain, 1
        )
        suf_vals = lax.dynamic_slice_in_dim(suffix_kv, kv_width + kv_first * HD, HD, 1)
        all_keys = jnp.concatenate([shared[:, :HD], suf_keys], axis=0)
        all_vals = jnp.concatenate([shared[:, HD:], suf_vals], axis=0)
        seg_ends = jnp.cumsum(lengths[0])
        positions = jnp.arange(row_count, dtype=jnp.int32)
        segment = jnp.sum((positions[:, None] >= seg_ends[None, :]).astype(jnp.int32), axis=1)
        causal = (segment[:, None] == segment[None, :]) & (positions[None, :] <= positions[:, None])
        visible = jnp.concatenate(
            [jnp.ones((row_count, shared.shape[0]), jnp.bool_), causal], axis=1
        )
        outputs = []
        for head_idx in range(heads_here):
            head_q = query_normed[:, head_idx * HD:(head_idx + 1) * HD]
            scores = jnp.dot(head_q, all_keys.T, preferred_element_type=jnp.float32) * HD ** (-0.5)
            scores = jnp.where(visible, scores, MASKED)
            row_max = jnp.max(scores, axis=-1, keepdims=True)
            weights = jnp.exp(scores - row_max)
            row_sum = jnp.sum(weights, axis=-1, keepdims=True)
            head_out = jnp.dot(
                weights.astype(jnp.bfloat16), all_vals, preferred_element_type=jnp.float32
            ) / row_sum
            outputs.append(head_out)
        attention = jnp.concatenate(outputs, axis=1).astype(jnp.bfloat16)

    share = row_count // tok_count
    first_row = tok_index * share
    with jax.named_scope("out_projection"):
        attention_all = gather_over_tok(attention, tok_count, 1)
        projected = jnp.einsum(
            "srd,sdc->rc", attention_all, w_out_all, preferred_element_type=jnp.float32
        )
        mixed_rows = residual.astype(jnp.float32) + rms_scale(projected, attn_gain)
        normed = rms_scale(mixed_rows, ffn_in_gain).astype(jnp.bfloat16)
        mixed_share = lax.dynamic_slice_in_dim(mixed_rows, first_row, share, 0)
    with jax.named_scope("feed_forward"):
        gate = jnp.dot(normed, w_gate, preferred_element_type=jnp.float32)
        upward = jnp.dot(normed, w_up, preferred_element_type=jnp.float32)
        hidden = (jax.nn.gelu(gate, approximate=True) * upward).astype(jnp.bfloat16)
        down_share = scatter_over_tok(
            jnp.dot(hidden, w_down, preferred_element_type=jnp.float32), tok_count, 2
        )
    return (mixed_share + rms_scale(down_share.astype(jnp.float32), ffn_out_gain)).astype(
        jnp.bfloat16
    )


def solution(mesh):
    in_specs = (
        P("req", "tok"),
        P("req", None),
        P("req", None),
        P(),
        P(),
        P("req", None),
        P(),
        P(),
        P("req", None),
        P("tok", None),
        P(),
        P(),
        P(),
        P(None, "tok"),
        P(None, "tok"),
        P("tok", None),
    )
    out_specs = P(("req", "tok"), None)
    return jax.shard_map(local, mesh=mesh, in_specs=in_specs, out_specs=out_specs, check_vma=False)
```

```python
import jax
import jax.numpy as jnp
from jax import lax
from jax.sharding import PartitionSpec as P
from jax.experimental import pallas as pl
from jax.experimental.pallas import tpu as pltpu

H = 8
KVH = 4
HD = 256
GROUPS = 2


EPSILON = 1e-06
MASKED = -1e30


def rms_scale(values_in, gain_vec):
    return (
        values_in
        * lax.rsqrt(jnp.mean(values_in * values_in, axis=-1, keepdims=True) + EPSILON)
        * gain_vec
    )


def norm_heads(values_in, gain_vec, head_count):
    row_count = values_in.shape[0]
    shaped = values_in.astype(jnp.float32).reshape(row_count, head_count, HD)
    return rms_scale(shaped, gain_vec).astype(jnp.bfloat16).reshape(row_count, head_count * HD)


def gather_tok_kernel(tok_count, w_ref, out_ref, send_sem, recv_sem, local_sem):
    mesh_ids = pl.DeviceIdType.MESH
    me = lax.axis_index("tok")
    up = lax.rem(me + 2, tok_count)
    down = lax.rem(me + tok_count - 2, tok_count)
    far = lax.rem(me + 4, tok_count)
    partner = me + 1 - 2 * lax.rem(me, 2)
    half = w_ref.shape[0] // 2

    barrier = pltpu.get_barrier_semaphore()
    for peer in (up, down, partner):
        pl.semaphore_signal(barrier, inc=1, device_id={"tok": peer}, device_id_type=mesh_ids)
    pl.semaphore_wait(barrier, 3)

    def remote(src, dst, slot, peer):
        return pltpu.make_async_remote_copy(
            src_ref=src,
            dst_ref=dst,
            send_sem=send_sem.at[slot],
            recv_sem=recv_sem.at[slot],
            device_id={"tok": peer},
            device_id_type=mesh_ids,
        )

    local = pltpu.make_async_copy(w_ref, out_ref.at[me], local_sem.at[0])
    local.start()
    to_up = remote(w_ref, out_ref.at[me], 0, up)
    to_down = remote(w_ref, out_ref.at[me], 1, down)
    to_up.start()
    to_down.start()
    remote(w_ref, out_ref.at[down], 0, down).wait_recv()
    remote(w_ref, out_ref.at[up], 1, up).wait_recv()

    first = pl.ds(0, half)
    second = pl.ds(half, half)
    fwd_up = remote(out_ref.at[down, first], out_ref.at[down, first], 2, up)
    fwd_down = remote(out_ref.at[up, second], out_ref.at[up, second], 3, down)
    fwd_up.start()
    fwd_down.start()
    remote(out_ref.at[far, first], out_ref.at[far, first], 2, down).wait_recv()
    remote(out_ref.at[far, second], out_ref.at[far, second], 3, up).wait_recv()
    local.wait()

    mine = (me, up, down, far)
    theirs = (
        partner,
        lax.rem(partner + 2, tok_count),
        lax.rem(partner + tok_count - 2, tok_count),
        lax.rem(partner + 4, tok_count),
    )
    to_partner = []
    for idx, slot in enumerate(mine):
        copy = remote(out_ref.at[slot], out_ref.at[slot], 4 + idx, partner)
        copy.start()
        to_partner.append(copy)
    for idx, slot in enumerate(theirs):
        remote(out_ref.at[slot], out_ref.at[slot], 4 + idx, partner).wait_recv()
    for copy in [to_up, to_down, fwd_up, fwd_down] + to_partner:
        copy.wait_send()


def gather_over_tok(block, tok_count, collective_id):
    assert tok_count == 8
    rows, cols = block.shape
    return pl.pallas_call(
        lambda *refs: gather_tok_kernel(tok_count, *refs),
        out_shape=jax.ShapeDtypeStruct((tok_count, rows, cols), block.dtype),
        in_specs=[pl.BlockSpec(memory_space=pl.ANY)],
        out_specs=pl.BlockSpec(memory_space=pl.ANY),
        scratch_shapes=[
            pltpu.SemaphoreType.DMA((8,)),
            pltpu.SemaphoreType.DMA((8,)),
            pltpu.SemaphoreType.DMA((1,)),
        ],
        compiler_params=pltpu.CompilerParams(collective_id=collective_id, has_side_effects=True),
        cost_estimate=pl.CostEstimate(
            flops=0, transcendentals=0, bytes_accessed=2 * tok_count * rows * cols * 2
        ),
    )(block)


def project_tok_kernel(
    tok_count, att_ref, w_hbm, out_ref, att_all, w_buf, send_sem, recv_sem, load_sem
):
    mesh_ids = pl.DeviceIdType.MESH
    me = lax.axis_index("tok")
    up = lax.rem(me + 2, tok_count)
    down = lax.rem(me + tok_count - 2, tok_count)
    far = lax.rem(me + 4, tok_count)
    partner = me + 1 - 2 * lax.rem(me, 2)
    half = att_ref.shape[0] // 2
    cols = out_ref.shape[1]
    tile = 512
    tiles = cols // tile

    barrier = pltpu.get_barrier_semaphore()
    for peer in (up, down, partner):
        pl.semaphore_signal(barrier, inc=1, device_id={"tok": peer}, device_id_type=mesh_ids)
    pl.semaphore_wait(barrier, 3)

    def remote(src, dst, slot, peer):
        return pltpu.make_async_remote_copy(
            src_ref=src,
            dst_ref=dst,
            send_sem=send_sem.at[slot],
            recv_sem=recv_sem.at[slot],
            device_id={"tok": peer},
            device_id_type=mesh_ids,
        )

    theirs = (
        partner,
        lax.rem(partner + 2, tok_count),
        lax.rem(partner + tok_count - 2, tok_count),
        lax.rem(partner + 4, tok_count),
    )
    order = (me, down, up, far) + theirs

    def load(idx):
        return pltpu.make_async_copy(w_hbm.at[order[idx]], w_buf.at[idx % 2], load_sem.at[idx % 2])

    def accumulate(idx, source, first):
        load(idx).wait()
        if idx + 1 < len(order):
            load(idx + 1).start()
        weights = w_buf.at[idx % 2]

        def one_tile(col):
            span = pl.ds(pl.multiple_of(col * tile, tile), tile)
            term = jnp.dot(source[...], weights[:, span], preferred_element_type=jnp.float32)
            if first:
                out_ref[:, span] = term
            else:
                out_ref[:, span] = out_ref[:, span] + term

        pl.loop(0, tiles)(one_tile)

    load(0).start()
    sends = []
    to_up = remote(att_ref, att_all.at[me], 0, up)
    to_down = remote(att_ref, att_all.at[me], 1, down)
    to_up.start()
    to_down.start()
    sends += [to_up, to_down]
    accumulate(0, att_ref, True)
    remote(att_ref, att_all.at[down], 0, down).wait_recv()
    remote(att_ref, att_all.at[up], 1, up).wait_recv()
    first = pl.ds(0, half)
    second = pl.ds(half, half)
    fwd_up = remote(att_all.at[down, first], att_all.at[down, first], 2, up)
    fwd_down = remote(att_all.at[up, second], att_all.at[up, second], 3, down)
    fwd_up.start()
    fwd_down.start()
    sends += [fwd_up, fwd_down]
    accumulate(1, att_all.at[down], False)
    accumulate(2, att_all.at[up], False)
    remote(att_all.at[far, first], att_all.at[far, first], 2, down).wait_recv()
    remote(att_all.at[far, second], att_all.at[far, second], 3, up).wait_recv()
    for idx, (src, slot) in enumerate(
        ((att_ref, me), (att_all.at[up], up), (att_all.at[down], down), (att_all.at[far], far))
    ):
        copy = remote(src, att_all.at[slot], 4 + idx, partner)
        copy.start()
        sends.append(copy)
    accumulate(3, att_all.at[far], False)
    for idx, slot in enumerate(theirs):
        remote(att_all.at[slot], att_all.at[slot], 4 + idx, partner).wait_recv()
        accumulate(4 + idx, att_all.at[slot], False)
    for copy in sends:
        copy.wait_send()


def project_over_tok(attention, w_all, tok_count, collective_id):
    assert tok_count == 8
    rows, width = attention.shape
    cols = w_all.shape[2]
    vmem = pltpu.MemorySpace.VMEM
    return pl.pallas_call(
        lambda *refs: project_tok_kernel(tok_count, *refs),
        out_shape=jax.ShapeDtypeStruct((rows, cols), jnp.float32),
        in_specs=[pl.BlockSpec(memory_space=vmem), pl.BlockSpec(memory_space=pl.ANY)],
        out_specs=pl.BlockSpec(memory_space=vmem),
        scratch_shapes=[
            pltpu.VMEM((tok_count, rows, width), attention.dtype),
            pltpu.VMEM((2, width, cols), w_all.dtype),
            pltpu.SemaphoreType.DMA((8,)),
            pltpu.SemaphoreType.DMA((8,)),
            pltpu.SemaphoreType.DMA((2,)),
        ],
        compiler_params=pltpu.CompilerParams(
            collective_id=collective_id, has_side_effects=True, vmem_limit_bytes=48 * 1024 * 1024
        ),
        cost_estimate=pl.CostEstimate(
            flops=2 * rows * width * tok_count * cols,
            transcendentals=0,
            bytes_accessed=tok_count * width * cols * 2 + rows * cols * 4,
        ),
    )(attention, w_all)


def scatter_tok_kernel(tok_count, part_ref, out_ref, chip_in, cross_out, cross_in, send_sem, recv_sem):
    mesh_ids = pl.DeviceIdType.MESH
    me = lax.axis_index("tok")
    up = lax.rem(me + 2, tok_count)
    down = lax.rem(me + tok_count - 2, tok_count)
    far = lax.rem(me + 4, tok_count)
    partner = me + 1 - 2 * lax.rem(me, 2)
    share = out_ref.shape[0]

    barrier = pltpu.get_barrier_semaphore()
    for peer in (up, down, far, partner):
        pl.semaphore_signal(barrier, inc=1, device_id={"tok": peer}, device_id_type=mesh_ids)
    pl.semaphore_wait(barrier, 4)

    def remote(src, dst, slot, peer):
        return pltpu.make_async_remote_copy(
            src_ref=src,
            dst_ref=dst,
            send_sem=send_sem.at[slot],
            recv_sem=recv_sem.at[slot],
            device_id={"tok": peer},
            device_id_type=mesh_ids,
        )

    def family(base):
        return (
            base,
            lax.rem(base + 2, tok_count),
            lax.rem(base + tok_count - 2, tok_count),
            lax.rem(base + 4, tok_count),
        )

    def rows_of(block):
        return pl.ds(pl.multiple_of(block * share, share), share)

    sends = []
    for idx, block in enumerate(family(partner)):
        copy = remote(part_ref.at[rows_of(block)], chip_in.at[idx], idx, partner)
        copy.start()
        sends.append(copy)
    mine = family(me)
    for idx in range(4):
        remote(part_ref.at[rows_of(mine[idx])], chip_in.at[idx], idx, partner).wait_recv()

    for idx in range(1, 4):
        summed = part_ref[rows_of(mine[idx]), :] + chip_in[idx]
        cross_out[idx - 1] = summed.astype(cross_out.dtype)
    for src_idx, dst_idx, peer in ((0, 1, up), (1, 0, down), (2, 2, far)):
        copy = remote(cross_out.at[src_idx], cross_in.at[dst_idx], 4 + dst_idx, peer)
        copy.start()
        sends.append(copy)
    total = part_ref[rows_of(me), :] + chip_in[0]
    for idx, peer in ((0, up), (1, down), (2, far)):
        remote(cross_out.at[idx], cross_in.at[idx], 4 + idx, peer).wait_recv()
    for idx in range(3):
        total = total + cross_in[idx].astype(jnp.float32)
    out_ref[...] = total
    for copy in sends:
        copy.wait_send()


def scatter_over_tok(partial, tok_count, collective_id):
    assert tok_count == 8
    rows, cols = partial.shape
    share = rows // tok_count
    vmem = pltpu.MemorySpace.VMEM
    return pl.pallas_call(
        lambda *refs: scatter_tok_kernel(tok_count, *refs),
        out_shape=jax.ShapeDtypeStruct((share, cols), jnp.float32),
        in_specs=[pl.BlockSpec(memory_space=vmem)],
        out_specs=pl.BlockSpec(memory_space=vmem),
        scratch_shapes=[
            pltpu.VMEM((4, share, cols), jnp.float32),
            pltpu.VMEM((3, share, cols), jnp.bfloat16),
            pltpu.VMEM((3, share, cols), jnp.bfloat16),
            pltpu.SemaphoreType.DMA((7,)),
            pltpu.SemaphoreType.DMA((7,)),
        ],
        compiler_params=pltpu.CompilerParams(
            collective_id=collective_id, has_side_effects=True, vmem_limit_bytes=48 * 1024 * 1024
        ),
        cost_estimate=pl.CostEstimate(
            flops=8 * share * cols, transcendentals=0, bytes_accessed=rows * cols * 4 * 2
        ),
    )(partial)


def local(
    queries,
    suffix_kv,
    prefix_cache,
    q_gain,
    k_gain,
    lengths,
    group_of,
    owner_order,
    residual,
    w_out,
    attn_gain,
    ffn_in_gain,
    ffn_out_gain,
    w_gate,
    w_up,
    w_down,
):
    req_count = lax.axis_size("req")
    tok_count = lax.axis_size("tok")
    req_index = lax.axis_index("req")
    tok_index = lax.axis_index("tok")
    row_count = queries.shape[0]
    heads_here = queries.shape[1] // HD
    head_ratio = H // KVH
    kv_first = tok_index * heads_here // head_ratio
    kv_width = KVH * HD
    own_count = req_count // GROUPS

    with jax.named_scope("prefix_gather"):
        pref_keys = lax.dynamic_slice_in_dim(prefix_cache, kv_first * HD, HD, 1)
        pref_vals = lax.dynamic_slice_in_dim(prefix_cache, kv_width + kv_first * HD, HD, 1)
        pref_kv = jnp.concatenate([pref_keys, pref_vals], axis=1)
        half_rows = pref_kv.shape[0] // 2
        core = tok_index % 2
        my_half = lax.dynamic_slice_in_dim(pref_kv, core * half_rows, half_rows, 0)
        gathered = lax.all_gather(my_half, "req", axis=0, tiled=False)
        w_out_all = gather_over_tok(w_out, tok_count, 0)
        gathered, w_out_all = lax.optimization_barrier((gathered, w_out_all))
        own_group = group_of[req_index]
        owner_ids = lax.dynamic_slice_in_dim(owner_order, own_group * own_count, own_count)
        picked = jnp.take(gathered, owner_ids, axis=0).reshape(-1, 2 * HD)
        partner = [(t, t ^ 1) for t in range(tok_count)]
        swapped = lax.ppermute(picked, "tok", perm=partner)
        shared = jnp.concatenate([picked, swapped], axis=0)

    with jax.named_scope("attention"):
        query_normed = norm_heads(queries, q_gain, heads_here)
        suf_keys = norm_heads(
            lax.dynamic_slice_in_dim(suffix_kv, kv_first * HD, HD, 1), k_gain, 1
        )
        suf_vals = lax.dynamic_slice_in_dim(suffix_kv, kv_width + kv_first * HD, HD, 1)
        all_keys = jnp.concatenate([shared[:, :HD], suf_keys], axis=0)
        all_vals = jnp.concatenate([shared[:, HD:], suf_vals], axis=0)
        seg_ends = jnp.cumsum(lengths[0])
        positions = jnp.arange(row_count, dtype=jnp.int32)
        segment = jnp.sum((positions[:, None] >= seg_ends[None, :]).astype(jnp.int32), axis=1)
        causal = (segment[:, None] == segment[None, :]) & (positions[None, :] <= positions[:, None])
        visible = jnp.concatenate(
            [jnp.ones((row_count, shared.shape[0]), jnp.bool_), causal], axis=1
        )
        outputs = []
        for head_idx in range(heads_here):
            head_q = query_normed[:, head_idx * HD:(head_idx + 1) * HD]
            scores = jnp.dot(head_q, all_keys.T, preferred_element_type=jnp.float32) * HD ** (-0.5)
            scores = jnp.where(visible, scores, MASKED)
            row_max = jnp.max(scores, axis=-1, keepdims=True)
            weights = jnp.exp(scores - row_max)
            row_sum = jnp.sum(weights, axis=-1, keepdims=True)
            head_out = jnp.dot(
                weights.astype(jnp.bfloat16), all_vals, preferred_element_type=jnp.float32
            ) / row_sum
            outputs.append(head_out)
        attention = jnp.concatenate(outputs, axis=1).astype(jnp.bfloat16)

    share = row_count // tok_count
    first_row = tok_index * share
    with jax.named_scope("out_projection"):
        projected = project_over_tok(attention, w_out_all, tok_count, 1)
        mixed_rows = residual.astype(jnp.float32) + rms_scale(projected, attn_gain)
        normed = rms_scale(mixed_rows, ffn_in_gain).astype(jnp.bfloat16)
        mixed_share = lax.dynamic_slice_in_dim(mixed_rows, first_row, share, 0)
    with jax.named_scope("feed_forward"):
        gate = jnp.dot(normed, w_gate, preferred_element_type=jnp.float32)
        upward = jnp.dot(normed, w_up, preferred_element_type=jnp.float32)
        hidden = (jax.nn.gelu(gate, approximate=True) * upward).astype(jnp.bfloat16)
        down_share = scatter_over_tok(
            jnp.dot(hidden, w_down, preferred_element_type=jnp.float32), tok_count, 2
        )
    return (mixed_share + rms_scale(down_share.astype(jnp.float32), ffn_out_gain)).astype(
        jnp.bfloat16
    )


def solution(mesh):
    in_specs = (
        P("req", "tok"),
        P("req", None),
        P("req", None),
        P(),
        P(),
        P("req", None),
        P(),
        P(),
        P("req", None),
        P("tok", None),
        P(),
        P(),
        P(),
        P(None, "tok"),
        P(None, "tok"),
        P("tok", None),
    )
    out_specs = P(("req", "tok"), None)
    return jax.shard_map(local, mesh=mesh, in_specs=in_specs, out_specs=out_specs, check_vma=False)
```

```python
import jax
import jax.numpy as jnp
from jax import lax
from jax.sharding import PartitionSpec as P
from jax.experimental import pallas as pl
from jax.experimental.pallas import tpu as pltpu

H = 8
KVH = 4
HD = 256
GROUPS = 2


EPSILON = 1e-06
MASKED = -1e30


def rms_scale(values_in, gain_vec):
    return (
        values_in
        * lax.rsqrt(jnp.mean(values_in * values_in, axis=-1, keepdims=True) + EPSILON)
        * gain_vec
    )


def norm_heads(values_in, gain_vec, head_count):
    row_count = values_in.shape[0]
    shaped = values_in.astype(jnp.float32).reshape(row_count, head_count, HD)
    return rms_scale(shaped, gain_vec).astype(jnp.bfloat16).reshape(row_count, head_count * HD)


def gather_tok_kernel(tok_count, w_ref, out_ref, send_sem, recv_sem, local_sem):
    mesh_ids = pl.DeviceIdType.MESH
    me = lax.axis_index("tok")
    up = lax.rem(me + 2, tok_count)
    down = lax.rem(me + tok_count - 2, tok_count)
    far = lax.rem(me + 4, tok_count)
    partner = me + 1 - 2 * lax.rem(me, 2)
    half = w_ref.shape[0] // 2

    barrier = pltpu.get_barrier_semaphore()
    for peer in (up, down, partner):
        pl.semaphore_signal(barrier, inc=1, device_id={"tok": peer}, device_id_type=mesh_ids)
    pl.semaphore_wait(barrier, 3)

    def remote(src, dst, slot, peer):
        return pltpu.make_async_remote_copy(
            src_ref=src,
            dst_ref=dst,
            send_sem=send_sem.at[slot],
            recv_sem=recv_sem.at[slot],
            device_id={"tok": peer},
            device_id_type=mesh_ids,
        )

    local = pltpu.make_async_copy(w_ref, out_ref.at[me], local_sem.at[0])
    local.start()
    to_up = remote(w_ref, out_ref.at[me], 0, up)
    to_down = remote(w_ref, out_ref.at[me], 1, down)
    to_up.start()
    to_down.start()
    remote(w_ref, out_ref.at[down], 0, down).wait_recv()
    remote(w_ref, out_ref.at[up], 1, up).wait_recv()

    first = pl.ds(0, half)
    second = pl.ds(half, half)
    fwd_up = remote(out_ref.at[down, first], out_ref.at[down, first], 2, up)
    fwd_down = remote(out_ref.at[up, second], out_ref.at[up, second], 3, down)
    fwd_up.start()
    fwd_down.start()
    remote(out_ref.at[far, first], out_ref.at[far, first], 2, down).wait_recv()
    remote(out_ref.at[far, second], out_ref.at[far, second], 3, up).wait_recv()
    local.wait()

    mine = (me, up, down, far)
    theirs = (
        partner,
        lax.rem(partner + 2, tok_count),
        lax.rem(partner + tok_count - 2, tok_count),
        lax.rem(partner + 4, tok_count),
    )
    to_partner = []
    for idx, slot in enumerate(mine):
        copy = remote(out_ref.at[slot], out_ref.at[slot], 4 + idx, partner)
        copy.start()
        to_partner.append(copy)
    for idx, slot in enumerate(theirs):
        remote(out_ref.at[slot], out_ref.at[slot], 4 + idx, partner).wait_recv()
    for copy in [to_up, to_down, fwd_up, fwd_down] + to_partner:
        copy.wait_send()


def gather_over_tok(block, tok_count, collective_id):
    assert tok_count == 8
    rows, cols = block.shape
    return pl.pallas_call(
        lambda *refs: gather_tok_kernel(tok_count, *refs),
        out_shape=jax.ShapeDtypeStruct((tok_count, rows, cols), block.dtype),
        in_specs=[pl.BlockSpec(memory_space=pl.ANY)],
        out_specs=pl.BlockSpec(memory_space=pl.ANY),
        scratch_shapes=[
            pltpu.SemaphoreType.DMA((8,)),
            pltpu.SemaphoreType.DMA((8,)),
            pltpu.SemaphoreType.DMA((1,)),
        ],
        compiler_params=pltpu.CompilerParams(collective_id=collective_id, has_side_effects=True),
        cost_estimate=pl.CostEstimate(
            flops=0, transcendentals=0, bytes_accessed=2 * tok_count * rows * cols * 2
        ),
    )(block)


def project_tok_kernel(
    tok_count, att_ref, w_hbm, out_ref, att_all, w_buf, send_sem, recv_sem, load_sem
):
    mesh_ids = pl.DeviceIdType.MESH
    me = lax.axis_index("tok")
    up = lax.rem(me + 2, tok_count)
    down = lax.rem(me + tok_count - 2, tok_count)
    far = lax.rem(me + 4, tok_count)
    partner = me + 1 - 2 * lax.rem(me, 2)
    half = att_ref.shape[0] // 2
    cols = out_ref.shape[1]
    tile = 512
    tiles = cols // tile

    barrier = pltpu.get_barrier_semaphore()
    for peer in (up, down, partner):
        pl.semaphore_signal(barrier, inc=1, device_id={"tok": peer}, device_id_type=mesh_ids)
    pl.semaphore_wait(barrier, 3)

    def remote(src, dst, slot, peer):
        return pltpu.make_async_remote_copy(
            src_ref=src,
            dst_ref=dst,
            send_sem=send_sem.at[slot],
            recv_sem=recv_sem.at[slot],
            device_id={"tok": peer},
            device_id_type=mesh_ids,
        )

    theirs = (
        partner,
        lax.rem(partner + 2, tok_count),
        lax.rem(partner + tok_count - 2, tok_count),
        lax.rem(partner + 4, tok_count),
    )
    order = (me, down, up, far) + theirs

    def load(idx):
        return pltpu.make_async_copy(w_hbm.at[order[idx]], w_buf.at[idx % 2], load_sem.at[idx % 2])

    def accumulate(idx, source, first):
        load(idx).wait()
        if idx + 1 < len(order):
            load(idx + 1).start()
        weights = w_buf.at[idx % 2]

        def one_tile(col):
            span = pl.ds(pl.multiple_of(col * tile, tile), tile)
            term = jnp.dot(source[...], weights[:, span], preferred_element_type=jnp.float32)
            if first:
                out_ref[:, span] = term
            else:
                out_ref[:, span] = out_ref[:, span] + term

        pl.loop(0, tiles)(one_tile)

    load(0).start()
    sends = []
    to_up = remote(att_ref, att_all.at[me], 0, up)
    to_down = remote(att_ref, att_all.at[me], 1, down)
    to_up.start()
    to_down.start()
    sends += [to_up, to_down]
    accumulate(0, att_ref, True)
    remote(att_ref, att_all.at[down], 0, down).wait_recv()
    remote(att_ref, att_all.at[up], 1, up).wait_recv()
    first = pl.ds(0, half)
    second = pl.ds(half, half)
    fwd_up = remote(att_all.at[down, first], att_all.at[down, first], 2, up)
    fwd_down = remote(att_all.at[up, second], att_all.at[up, second], 3, down)
    fwd_up.start()
    fwd_down.start()
    sends += [fwd_up, fwd_down]
    accumulate(1, att_all.at[down], False)
    accumulate(2, att_all.at[up], False)
    remote(att_all.at[far, first], att_all.at[far, first], 2, down).wait_recv()
    remote(att_all.at[far, second], att_all.at[far, second], 3, up).wait_recv()
    for idx, (src, slot) in enumerate(
        ((att_ref, me), (att_all.at[up], up), (att_all.at[down], down), (att_all.at[far], far))
    ):
        copy = remote(src, att_all.at[slot], 4 + idx, partner)
        copy.start()
        sends.append(copy)
    accumulate(3, att_all.at[far], False)
    for idx, slot in enumerate(theirs):
        remote(att_all.at[slot], att_all.at[slot], 4 + idx, partner).wait_recv()
        accumulate(4 + idx, att_all.at[slot], False)
    for copy in sends:
        copy.wait_send()


def project_over_tok(attention, w_all, tok_count, collective_id):
    assert tok_count == 8
    rows, width = attention.shape
    cols = w_all.shape[2]
    vmem = pltpu.MemorySpace.VMEM
    return pl.pallas_call(
        lambda *refs: project_tok_kernel(tok_count, *refs),
        out_shape=jax.ShapeDtypeStruct((rows, cols), jnp.float32),
        in_specs=[pl.BlockSpec(memory_space=vmem), pl.BlockSpec(memory_space=pl.ANY)],
        out_specs=pl.BlockSpec(memory_space=vmem),
        scratch_shapes=[
            pltpu.VMEM((tok_count, rows, width), attention.dtype),
            pltpu.VMEM((2, width, cols), w_all.dtype),
            pltpu.SemaphoreType.DMA((8,)),
            pltpu.SemaphoreType.DMA((8,)),
            pltpu.SemaphoreType.DMA((2,)),
        ],
        compiler_params=pltpu.CompilerParams(
            collective_id=collective_id, has_side_effects=True, vmem_limit_bytes=48 * 1024 * 1024
        ),
        cost_estimate=pl.CostEstimate(
            flops=2 * rows * width * tok_count * cols,
            transcendentals=0,
            bytes_accessed=tok_count * width * cols * 2 + rows * cols * 4,
        ),
    )(attention, w_all)


def cross_tok_kernel(tok_count, sums_ref, out_ref, cross_out, cross_in, send_sem, recv_sem):
    mesh_ids = pl.DeviceIdType.MESH
    me = lax.axis_index("tok")
    up = lax.rem(me + 2, tok_count)
    down = lax.rem(me + tok_count - 2, tok_count)
    far = lax.rem(me + 4, tok_count)
    lines = tok_count // 2

    barrier = pltpu.get_barrier_semaphore()
    for peer in (up, down, far):
        pl.semaphore_signal(barrier, inc=1, device_id={"tok": peer}, device_id_type=mesh_ids)
    pl.semaphore_wait(barrier, 3)

    def remote(src, dst, slot, peer):
        return pltpu.make_async_remote_copy(
            src_ref=src,
            dst_ref=dst,
            send_sem=send_sem.at[slot],
            recv_sem=recv_sem.at[slot],
            device_id={"tok": peer},
            device_id_type=mesh_ids,
        )

    sends = []
    for src_idx, peer, dst_idx in ((0, up, 1), (1, down, 0), (2, far, 2)):
        cross_out[src_idx] = sums_ref[lax.rem(peer // 2, lines)].astype(cross_out.dtype)
        copy = remote(cross_out.at[src_idx], cross_in.at[dst_idx], dst_idx, peer)
        copy.start()
        sends.append(copy)
    total = sums_ref[me // 2]
    for idx, peer in ((0, up), (1, down), (2, far)):
        remote(cross_out.at[idx], cross_in.at[idx], idx, peer).wait_recv()
    for idx in range(3):
        total = total + cross_in[idx].astype(jnp.float32)
    out_ref[...] = total
    for copy in sends:
        copy.wait_send()


def cross_over_tok(sums, tok_count, collective_id):
    assert tok_count == 8
    lines, share, cols = sums.shape
    vmem = pltpu.MemorySpace.VMEM
    return pl.pallas_call(
        lambda *refs: cross_tok_kernel(tok_count, *refs),
        out_shape=jax.ShapeDtypeStruct((share, cols), jnp.float32),
        in_specs=[pl.BlockSpec(memory_space=vmem)],
        out_specs=pl.BlockSpec(memory_space=vmem),
        scratch_shapes=[
            pltpu.VMEM((3, share, cols), jnp.bfloat16),
            pltpu.VMEM((3, share, cols), jnp.bfloat16),
            pltpu.SemaphoreType.DMA((3,)),
            pltpu.SemaphoreType.DMA((3,)),
        ],
        compiler_params=pltpu.CompilerParams(
            collective_id=collective_id, has_side_effects=True, vmem_limit_bytes=32 * 1024 * 1024
        ),
        cost_estimate=pl.CostEstimate(
            flops=4 * share * cols, transcendentals=0, bytes_accessed=lines * share * cols * 4 * 2
        ),
    )(sums)


def scatter_tok_kernel(tok_count, part_ref, out_ref, chip_in, cross_out, cross_in, send_sem, recv_sem):
    mesh_ids = pl.DeviceIdType.MESH
    me = lax.axis_index("tok")
    up = lax.rem(me + 2, tok_count)
    down = lax.rem(me + tok_count - 2, tok_count)
    far = lax.rem(me + 4, tok_count)
    partner = me + 1 - 2 * lax.rem(me, 2)
    share = out_ref.shape[0]

    barrier = pltpu.get_barrier_semaphore()
    for peer in (up, down, far, partner):
        pl.semaphore_signal(barrier, inc=1, device_id={"tok": peer}, device_id_type=mesh_ids)
    pl.semaphore_wait(barrier, 4)

    def remote(src, dst, slot, peer):
        return pltpu.make_async_remote_copy(
            src_ref=src,
            dst_ref=dst,
            send_sem=send_sem.at[slot],
            recv_sem=recv_sem.at[slot],
            device_id={"tok": peer},
            device_id_type=mesh_ids,
        )

    def family(base):
        return (
            base,
            lax.rem(base + 2, tok_count),
            lax.rem(base + tok_count - 2, tok_count),
            lax.rem(base + 4, tok_count),
        )

    def rows_of(block):
        return pl.ds(pl.multiple_of(block * share, share), share)

    sends = []
    for idx, block in enumerate(family(partner)):
        copy = remote(part_ref.at[rows_of(block)], chip_in.at[idx], idx, partner)
        copy.start()
        sends.append(copy)
    mine = family(me)
    for idx in range(4):
        remote(part_ref.at[rows_of(mine[idx])], chip_in.at[idx], idx, partner).wait_recv()

    for idx in range(1, 4):
        summed = part_ref[rows_of(mine[idx]), :] + chip_in[idx]
        cross_out[idx - 1] = summed.astype(cross_out.dtype)
    for src_idx, dst_idx, peer in ((0, 1, up), (1, 0, down), (2, 2, far)):
        copy = remote(cross_out.at[src_idx], cross_in.at[dst_idx], 4 + dst_idx, peer)
        copy.start()
        sends.append(copy)
    total = part_ref[rows_of(me), :] + chip_in[0]
    for idx, peer in ((0, up), (1, down), (2, far)):
        remote(cross_out.at[idx], cross_in.at[idx], 4 + idx, peer).wait_recv()
    for idx in range(3):
        total = total + cross_in[idx].astype(jnp.float32)
    out_ref[...] = total
    for copy in sends:
        copy.wait_send()


def scatter_over_tok(partial, tok_count, collective_id):
    assert tok_count == 8
    rows, cols = partial.shape
    share = rows // tok_count
    vmem = pltpu.MemorySpace.VMEM
    return pl.pallas_call(
        lambda *refs: scatter_tok_kernel(tok_count, *refs),
        out_shape=jax.ShapeDtypeStruct((share, cols), jnp.float32),
        in_specs=[pl.BlockSpec(memory_space=vmem)],
        out_specs=pl.BlockSpec(memory_space=vmem),
        scratch_shapes=[
            pltpu.VMEM((4, share, cols), jnp.float32),
            pltpu.VMEM((3, share, cols), jnp.bfloat16),
            pltpu.VMEM((3, share, cols), jnp.bfloat16),
            pltpu.SemaphoreType.DMA((7,)),
            pltpu.SemaphoreType.DMA((7,)),
        ],
        compiler_params=pltpu.CompilerParams(
            collective_id=collective_id, has_side_effects=True, vmem_limit_bytes=48 * 1024 * 1024
        ),
        cost_estimate=pl.CostEstimate(
            flops=8 * share * cols, transcendentals=0, bytes_accessed=rows * cols * 4 * 2
        ),
    )(partial)


def local(
    queries,
    suffix_kv,
    prefix_cache,
    q_gain,
    k_gain,
    lengths,
    group_of,
    owner_order,
    residual,
    w_out,
    attn_gain,
    ffn_in_gain,
    ffn_out_gain,
    w_gate,
    w_up,
    w_down,
):
    req_count = lax.axis_size("req")
    tok_count = lax.axis_size("tok")
    req_index = lax.axis_index("req")
    tok_index = lax.axis_index("tok")
    row_count = queries.shape[0]
    heads_here = queries.shape[1] // HD
    head_ratio = H // KVH
    kv_first = tok_index * heads_here // head_ratio
    kv_width = KVH * HD
    own_count = req_count // GROUPS

    with jax.named_scope("prefix_gather"):
        pref_keys = lax.dynamic_slice_in_dim(prefix_cache, kv_first * HD, HD, 1)
        pref_vals = lax.dynamic_slice_in_dim(prefix_cache, kv_width + kv_first * HD, HD, 1)
        pref_kv = jnp.concatenate([pref_keys, pref_vals], axis=1)
        half_rows = pref_kv.shape[0] // 2
        core = tok_index % 2
        my_half = lax.dynamic_slice_in_dim(pref_kv, core * half_rows, half_rows, 0)
        gathered = lax.all_gather(my_half, "req", axis=0, tiled=False)
        w_out_all = gather_over_tok(w_out, tok_count, 0)
        gathered, w_out_all = lax.optimization_barrier((gathered, w_out_all))
        own_group = group_of[req_index]
        owner_ids = lax.dynamic_slice_in_dim(owner_order, own_group * own_count, own_count)
        picked = jnp.take(gathered, owner_ids, axis=0).reshape(-1, 2 * HD)
        partner = [(t, t ^ 1) for t in range(tok_count)]
        swapped = lax.ppermute(picked, "tok", perm=partner)
        shared = jnp.concatenate([picked, swapped], axis=0)

    with jax.named_scope("attention"):
        query_normed = norm_heads(queries, q_gain, heads_here)
        suf_keys = norm_heads(
            lax.dynamic_slice_in_dim(suffix_kv, kv_first * HD, HD, 1), k_gain, 1
        )
        suf_vals = lax.dynamic_slice_in_dim(suffix_kv, kv_width + kv_first * HD, HD, 1)
        all_keys = jnp.concatenate([shared[:, :HD], suf_keys], axis=0)
        all_vals = jnp.concatenate([shared[:, HD:], suf_vals], axis=0)
        seg_ends = jnp.cumsum(lengths[0])
        positions = jnp.arange(row_count, dtype=jnp.int32)
        segment = jnp.sum((positions[:, None] >= seg_ends[None, :]).astype(jnp.int32), axis=1)
        causal = (segment[:, None] == segment[None, :]) & (positions[None, :] <= positions[:, None])
        visible = jnp.concatenate(
            [jnp.ones((row_count, shared.shape[0]), jnp.bool_), causal], axis=1
        )
        outputs = []
        for head_idx in range(heads_here):
            head_q = query_normed[:, head_idx * HD:(head_idx + 1) * HD]
            scores = jnp.dot(head_q, all_keys.T, preferred_element_type=jnp.float32) * HD ** (-0.5)
            scores = jnp.where(visible, scores, MASKED)
            row_max = jnp.max(scores, axis=-1, keepdims=True)
            weights = jnp.exp(scores - row_max)
            row_sum = jnp.sum(weights, axis=-1, keepdims=True)
            head_out = jnp.dot(
                weights.astype(jnp.bfloat16), all_vals, preferred_element_type=jnp.float32
            ) / row_sum
            outputs.append(head_out)
        attention = jnp.concatenate(outputs, axis=1).astype(jnp.bfloat16)

    share = row_count // tok_count
    first_row = tok_index * share
    with jax.named_scope("out_projection"):
        projected = project_over_tok(attention, w_out_all, tok_count, 1)
        mixed_rows = residual.astype(jnp.float32) + rms_scale(projected, attn_gain)
        normed = rms_scale(mixed_rows, ffn_in_gain).astype(jnp.bfloat16)
        mixed_share = lax.dynamic_slice_in_dim(mixed_rows, first_row, share, 0)
    def feed_forward(rows_in):
        gate = jnp.dot(rows_in, w_gate, preferred_element_type=jnp.float32)
        upward = jnp.dot(rows_in, w_up, preferred_element_type=jnp.float32)
        hidden = (jax.nn.gelu(gate, approximate=True) * upward).astype(jnp.bfloat16)
        return jnp.dot(hidden, w_down, preferred_element_type=jnp.float32)

    with jax.named_scope("feed_forward"):
        core = tok_index % 2
        by_parity = normed.reshape(tok_count // 2, 2, share, normed.shape[1])
        theirs = lax.dynamic_index_in_dim(by_parity, 1 - core, axis=1, keepdims=False)
        mine = lax.dynamic_index_in_dim(by_parity, core, axis=1, keepdims=False)
        cols = normed.shape[1]
        partner = [(t, t ^ 1) for t in range(tok_count)]
        for_partner = feed_forward(theirs.reshape(-1, cols))
        from_partner = lax.ppermute(for_partner, "tok", perm=partner)
        chip_sums = feed_forward(mine.reshape(-1, cols)) + from_partner
        down_share = cross_over_tok(chip_sums.reshape(tok_count // 2, share, cols), tok_count, 2)
    return (mixed_share + rms_scale(down_share.astype(jnp.float32), ffn_out_gain)).astype(
        jnp.bfloat16
    )


def solution(mesh):
    in_specs = (
        P("req", "tok"),
        P("req", None),
        P("req", None),
        P(),
        P(),
        P("req", None),
        P(),
        P(),
        P("req", None),
        P("tok", None),
        P(),
        P(),
        P(),
        P(None, "tok"),
        P(None, "tok"),
        P("tok", None),
    )
    out_specs = P(("req", "tok"), None)
    return jax.shard_map(local, mesh=mesh, in_specs=in_specs, out_specs=out_specs, check_vma=False)
```

```python
import jax
import jax.numpy as jnp
from jax import lax
from jax.sharding import PartitionSpec as P
from jax.experimental import pallas as pl
from jax.experimental.pallas import tpu as pltpu

H = 8
KVH = 4
HD = 256
GROUPS = 2


EPSILON = 1e-06
MASKED = -1e30


def rms_scale(values_in, gain_vec):
    return (
        values_in
        * lax.rsqrt(jnp.mean(values_in * values_in, axis=-1, keepdims=True) + EPSILON)
        * gain_vec
    )


def norm_heads(values_in, gain_vec, head_count):
    row_count = values_in.shape[0]
    shaped = values_in.astype(jnp.float32).reshape(row_count, head_count, HD)
    return rms_scale(shaped, gain_vec).astype(jnp.bfloat16).reshape(row_count, head_count * HD)


def gather_tok_kernel(tok_count, w_ref, out_ref, send_sem, recv_sem, local_sem):
    mesh_ids = pl.DeviceIdType.MESH
    me = lax.axis_index("tok")
    up = lax.rem(me + 2, tok_count)
    down = lax.rem(me + tok_count - 2, tok_count)
    far = lax.rem(me + 4, tok_count)
    partner = me + 1 - 2 * lax.rem(me, 2)
    half = w_ref.shape[0] // 2

    barrier = pltpu.get_barrier_semaphore()
    for peer in (up, down, partner):
        pl.semaphore_signal(barrier, inc=1, device_id={"tok": peer}, device_id_type=mesh_ids)
    pl.semaphore_wait(barrier, 3)

    def remote(src, dst, slot, peer):
        return pltpu.make_async_remote_copy(
            src_ref=src,
            dst_ref=dst,
            send_sem=send_sem.at[slot],
            recv_sem=recv_sem.at[slot],
            device_id={"tok": peer},
            device_id_type=mesh_ids,
        )

    local = pltpu.make_async_copy(w_ref, out_ref.at[me], local_sem.at[0])
    local.start()
    to_up = remote(w_ref, out_ref.at[me], 0, up)
    to_down = remote(w_ref, out_ref.at[me], 1, down)
    to_up.start()
    to_down.start()
    remote(w_ref, out_ref.at[down], 0, down).wait_recv()
    remote(w_ref, out_ref.at[up], 1, up).wait_recv()

    first = pl.ds(0, half)
    second = pl.ds(half, half)
    fwd_up = remote(out_ref.at[down, first], out_ref.at[down, first], 2, up)
    fwd_down = remote(out_ref.at[up, second], out_ref.at[up, second], 3, down)
    fwd_up.start()
    fwd_down.start()
    remote(out_ref.at[far, first], out_ref.at[far, first], 2, down).wait_recv()
    remote(out_ref.at[far, second], out_ref.at[far, second], 3, up).wait_recv()
    local.wait()

    mine = (me, up, down, far)
    theirs = (
        partner,
        lax.rem(partner + 2, tok_count),
        lax.rem(partner + tok_count - 2, tok_count),
        lax.rem(partner + 4, tok_count),
    )
    to_partner = []
    for idx, slot in enumerate(mine):
        copy = remote(out_ref.at[slot], out_ref.at[slot], 4 + idx, partner)
        copy.start()
        to_partner.append(copy)
    for idx, slot in enumerate(theirs):
        remote(out_ref.at[slot], out_ref.at[slot], 4 + idx, partner).wait_recv()
    for copy in [to_up, to_down, fwd_up, fwd_down] + to_partner:
        copy.wait_send()


def gather_over_tok(block, tok_count, collective_id):
    assert tok_count == 8
    rows, cols = block.shape
    return pl.pallas_call(
        lambda *refs: gather_tok_kernel(tok_count, *refs),
        out_shape=jax.ShapeDtypeStruct((tok_count, rows, cols), block.dtype),
        in_specs=[pl.BlockSpec(memory_space=pl.ANY)],
        out_specs=pl.BlockSpec(memory_space=pl.ANY),
        scratch_shapes=[
            pltpu.SemaphoreType.DMA((8,)),
            pltpu.SemaphoreType.DMA((8,)),
            pltpu.SemaphoreType.DMA((1,)),
        ],
        compiler_params=pltpu.CompilerParams(collective_id=collective_id, has_side_effects=True),
        cost_estimate=pl.CostEstimate(
            flops=0, transcendentals=0, bytes_accessed=2 * tok_count * rows * cols * 2
        ),
    )(block)


def project_tok_kernel(
    tok_count, att_ref, w_hbm, out_ref, att_all, w_buf, send_sem, recv_sem, load_sem
):
    mesh_ids = pl.DeviceIdType.MESH
    me = lax.axis_index("tok")
    up = lax.rem(me + 2, tok_count)
    down = lax.rem(me + tok_count - 2, tok_count)
    far = lax.rem(me + 4, tok_count)
    partner = me + 1 - 2 * lax.rem(me, 2)
    half = att_ref.shape[0] // 2
    cols = out_ref.shape[1]
    tile = 512
    tiles = cols // tile

    barrier = pltpu.get_barrier_semaphore()
    for peer in (up, down, partner):
        pl.semaphore_signal(barrier, inc=1, device_id={"tok": peer}, device_id_type=mesh_ids)
    pl.semaphore_wait(barrier, 3)

    def remote(src, dst, slot, peer):
        return pltpu.make_async_remote_copy(
            src_ref=src,
            dst_ref=dst,
            send_sem=send_sem.at[slot],
            recv_sem=recv_sem.at[slot],
            device_id={"tok": peer},
            device_id_type=mesh_ids,
        )

    theirs = (
        partner,
        lax.rem(partner + 2, tok_count),
        lax.rem(partner + tok_count - 2, tok_count),
        lax.rem(partner + 4, tok_count),
    )
    order = (me, down, up, far) + theirs

    def load(idx):
        return pltpu.make_async_copy(w_hbm.at[order[idx]], w_buf.at[idx % 2], load_sem.at[idx % 2])

    def accumulate(idx, source, first):
        load(idx).wait()
        if idx + 1 < len(order):
            load(idx + 1).start()
        weights = w_buf.at[idx % 2]

        def one_tile(col):
            span = pl.ds(pl.multiple_of(col * tile, tile), tile)
            term = jnp.dot(source[...], weights[:, span], preferred_element_type=jnp.float32)
            if first:
                out_ref[:, span] = term
            else:
                out_ref[:, span] = out_ref[:, span] + term

        pl.loop(0, tiles)(one_tile)

    load(0).start()
    sends = []
    to_up = remote(att_ref, att_all.at[me], 0, up)
    to_down = remote(att_ref, att_all.at[me], 1, down)
    to_up.start()
    to_down.start()
    sends += [to_up, to_down]
    accumulate(0, att_ref, True)
    remote(att_ref, att_all.at[down], 0, down).wait_recv()
    remote(att_ref, att_all.at[up], 1, up).wait_recv()
    first = pl.ds(0, half)
    second = pl.ds(half, half)
    fwd_up = remote(att_all.at[down, first], att_all.at[down, first], 2, up)
    fwd_down = remote(att_all.at[up, second], att_all.at[up, second], 3, down)
    fwd_up.start()
    fwd_down.start()
    sends += [fwd_up, fwd_down]
    accumulate(1, att_all.at[down], False)
    accumulate(2, att_all.at[up], False)
    remote(att_all.at[far, first], att_all.at[far, first], 2, down).wait_recv()
    remote(att_all.at[far, second], att_all.at[far, second], 3, up).wait_recv()
    for idx, (src, slot) in enumerate(
        ((att_ref, me), (att_all.at[up], up), (att_all.at[down], down), (att_all.at[far], far))
    ):
        copy = remote(src, att_all.at[slot], 4 + idx, partner)
        copy.start()
        sends.append(copy)
    accumulate(3, att_all.at[far], False)
    for idx, slot in enumerate(theirs):
        remote(att_all.at[slot], att_all.at[slot], 4 + idx, partner).wait_recv()
        accumulate(4 + idx, att_all.at[slot], False)
    for copy in sends:
        copy.wait_send()


def project_over_tok(attention, w_all, tok_count, collective_id):
    assert tok_count == 8
    rows, width = attention.shape
    cols = w_all.shape[2]
    vmem = pltpu.MemorySpace.VMEM
    return pl.pallas_call(
        lambda *refs: project_tok_kernel(tok_count, *refs),
        out_shape=jax.ShapeDtypeStruct((rows, cols), jnp.float32),
        in_specs=[pl.BlockSpec(memory_space=vmem), pl.BlockSpec(memory_space=pl.ANY)],
        out_specs=pl.BlockSpec(memory_space=vmem),
        scratch_shapes=[
            pltpu.VMEM((tok_count, rows, width), attention.dtype),
            pltpu.VMEM((2, width, cols), w_all.dtype),
            pltpu.SemaphoreType.DMA((8,)),
            pltpu.SemaphoreType.DMA((8,)),
            pltpu.SemaphoreType.DMA((2,)),
        ],
        compiler_params=pltpu.CompilerParams(
            collective_id=collective_id, has_side_effects=True, vmem_limit_bytes=48 * 1024 * 1024
        ),
        cost_estimate=pl.CostEstimate(
            flops=2 * rows * width * tok_count * cols,
            transcendentals=0,
            bytes_accessed=tok_count * width * cols * 2 + rows * cols * 4,
        ),
    )(attention, w_all)


def scatter_tok_kernel(
    tok_count, part_hbm, out_ref, mine, chip_in, cross_out, cross_in, load_sem, send_sem, recv_sem
):
    mesh_ids = pl.DeviceIdType.MESH
    me = lax.axis_index("tok")
    up = lax.rem(me + 2, tok_count)
    down = lax.rem(me + tok_count - 2, tok_count)
    far = lax.rem(me + 4, tok_count)
    partner = me + 1 - 2 * lax.rem(me, 2)
    share = out_ref.shape[0]

    barrier = pltpu.get_barrier_semaphore()
    for peer in (up, down, far, partner):
        pl.semaphore_signal(barrier, inc=1, device_id={"tok": peer}, device_id_type=mesh_ids)
    pl.semaphore_wait(barrier, 4)

    def remote(src, dst, slot, peer):
        return pltpu.make_async_remote_copy(
            src_ref=src,
            dst_ref=dst,
            send_sem=send_sem.at[slot],
            recv_sem=recv_sem.at[slot],
            device_id={"tok": peer},
            device_id_type=mesh_ids,
        )

    def family(base):
        return (
            base,
            lax.rem(base + 2, tok_count),
            lax.rem(base + tok_count - 2, tok_count),
            lax.rem(base + 4, tok_count),
        )

    def rows_of(block):
        return pl.ds(pl.multiple_of(block * share, share), share)

    order = (3, 1, 2, 0)
    sends = []
    theirs = family(partner)
    for idx in order:
        copy = remote(part_hbm.at[rows_of(theirs[idx])], chip_in.at[idx], idx, partner)
        copy.start()
        sends.append(copy)
    own = family(me)
    loads = []
    for idx in order:
        load = pltpu.make_async_copy(part_hbm.at[rows_of(own[idx])], mine.at[idx], load_sem.at[idx])
        load.start()
        loads.append(load)
    targets = {1: (up, 1), 2: (down, 0), 3: (far, 2)}
    for pos, idx in enumerate(order[:3]):
        loads[pos].wait()
        remote(part_hbm.at[rows_of(own[idx])], chip_in.at[idx], idx, partner).wait_recv()
        cross_out[idx - 1] = (mine[idx] + chip_in[idx]).astype(cross_out.dtype)
        peer, dst_idx = targets[idx]
        copy = remote(cross_out.at[idx - 1], cross_in.at[dst_idx], 4 + dst_idx, peer)
        copy.start()
        sends.append(copy)
    loads[3].wait()
    remote(part_hbm.at[rows_of(own[0])], chip_in.at[0], 0, partner).wait_recv()
    total = mine[0] + chip_in[0]
    for idx, peer in ((0, up), (1, down), (2, far)):
        remote(cross_out.at[idx], cross_in.at[idx], 4 + idx, peer).wait_recv()
    for idx in range(3):
        total = total + cross_in[idx].astype(jnp.float32)
    out_ref[...] = total
    for copy in sends:
        copy.wait_send()


def scatter_over_tok(partial, tok_count, collective_id):
    assert tok_count == 8
    rows, cols = partial.shape
    share = rows // tok_count
    vmem = pltpu.MemorySpace.VMEM
    return pl.pallas_call(
        lambda *refs: scatter_tok_kernel(tok_count, *refs),
        out_shape=jax.ShapeDtypeStruct((share, cols), jnp.float32),
        in_specs=[pl.BlockSpec(memory_space=pl.ANY)],
        out_specs=pl.BlockSpec(memory_space=vmem),
        scratch_shapes=[
            pltpu.VMEM((4, share, cols), jnp.float32),
            pltpu.VMEM((4, share, cols), jnp.float32),
            pltpu.VMEM((3, share, cols), jnp.bfloat16),
            pltpu.VMEM((3, share, cols), jnp.bfloat16),
            pltpu.SemaphoreType.DMA((4,)),
            pltpu.SemaphoreType.DMA((7,)),
            pltpu.SemaphoreType.DMA((7,)),
        ],
        compiler_params=pltpu.CompilerParams(
            collective_id=collective_id, has_side_effects=True, vmem_limit_bytes=48 * 1024 * 1024
        ),
        cost_estimate=pl.CostEstimate(
            flops=8 * share * cols, transcendentals=0, bytes_accessed=rows * cols * 4 * 2
        ),
    )(partial)


def local(
    queries,
    suffix_kv,
    prefix_cache,
    q_gain,
    k_gain,
    lengths,
    group_of,
    owner_order,
    residual,
    w_out,
    attn_gain,
    ffn_in_gain,
    ffn_out_gain,
    w_gate,
    w_up,
    w_down,
):
    req_count = lax.axis_size("req")
    tok_count = lax.axis_size("tok")
    req_index = lax.axis_index("req")
    tok_index = lax.axis_index("tok")
    row_count = queries.shape[0]
    heads_here = queries.shape[1] // HD
    head_ratio = H // KVH
    kv_first = tok_index * heads_here // head_ratio
    kv_width = KVH * HD
    own_count = req_count // GROUPS

    with jax.named_scope("prefix_gather"):
        pref_keys = lax.dynamic_slice_in_dim(prefix_cache, kv_first * HD, HD, 1)
        pref_vals = lax.dynamic_slice_in_dim(prefix_cache, kv_width + kv_first * HD, HD, 1)
        pref_kv = jnp.concatenate([pref_keys, pref_vals], axis=1)
        half_rows = pref_kv.shape[0] // 2
        core = tok_index % 2
        my_half = lax.dynamic_slice_in_dim(pref_kv, core * half_rows, half_rows, 0)
        gathered = lax.all_gather(my_half, "req", axis=0, tiled=False)
        w_out_all = gather_over_tok(w_out, tok_count, 0)
        gathered, w_out_all = lax.optimization_barrier((gathered, w_out_all))
        own_group = group_of[req_index]
        owner_ids = lax.dynamic_slice_in_dim(owner_order, own_group * own_count, own_count)
        picked = jnp.take(gathered, owner_ids, axis=0).reshape(-1, 2 * HD)
        partner = [(t, t ^ 1) for t in range(tok_count)]
        swapped = lax.ppermute(picked, "tok", perm=partner)
        shared = jnp.concatenate([picked, swapped], axis=0)

    with jax.named_scope("attention"):
        query_normed = norm_heads(queries, q_gain, heads_here)
        suf_keys = norm_heads(
            lax.dynamic_slice_in_dim(suffix_kv, kv_first * HD, HD, 1), k_gain, 1
        )
        suf_vals = lax.dynamic_slice_in_dim(suffix_kv, kv_width + kv_first * HD, HD, 1)
        all_keys = jnp.concatenate([shared[:, :HD], suf_keys], axis=0)
        all_vals = jnp.concatenate([shared[:, HD:], suf_vals], axis=0)
        seg_ends = jnp.cumsum(lengths[0])
        positions = jnp.arange(row_count, dtype=jnp.int32)
        segment = jnp.sum((positions[:, None] >= seg_ends[None, :]).astype(jnp.int32), axis=1)
        causal = (segment[:, None] == segment[None, :]) & (positions[None, :] <= positions[:, None])
        visible = jnp.concatenate(
            [jnp.ones((row_count, shared.shape[0]), jnp.bool_), causal], axis=1
        )
        outputs = []
        for head_idx in range(heads_here):
            head_q = query_normed[:, head_idx * HD:(head_idx + 1) * HD]
            scores = jnp.dot(head_q, all_keys.T, preferred_element_type=jnp.float32) * HD ** (-0.5)
            scores = jnp.where(visible, scores, MASKED)
            row_max = jnp.max(scores, axis=-1, keepdims=True)
            weights = jnp.exp(scores - row_max)
            row_sum = jnp.sum(weights, axis=-1, keepdims=True)
            head_out = jnp.dot(
                weights.astype(jnp.bfloat16), all_vals, preferred_element_type=jnp.float32
            ) / row_sum
            outputs.append(head_out)
        attention = jnp.concatenate(outputs, axis=1).astype(jnp.bfloat16)

    share = row_count // tok_count
    first_row = tok_index * share
    with jax.named_scope("out_projection"):
        projected = project_over_tok(attention, w_out_all, tok_count, 1)
        mixed_rows = residual.astype(jnp.float32) + rms_scale(projected, attn_gain)
        normed = rms_scale(mixed_rows, ffn_in_gain).astype(jnp.bfloat16)
        mixed_share = lax.dynamic_slice_in_dim(mixed_rows, first_row, share, 0)
    with jax.named_scope("feed_forward"):
        gate = jnp.dot(normed, w_gate, preferred_element_type=jnp.float32)
        upward = jnp.dot(normed, w_up, preferred_element_type=jnp.float32)
        hidden = (jax.nn.gelu(gate, approximate=True) * upward).astype(jnp.bfloat16)
        down_share = scatter_over_tok(
            jnp.dot(hidden, w_down, preferred_element_type=jnp.float32), tok_count, 2
        )
    return (mixed_share + rms_scale(down_share.astype(jnp.float32), ffn_out_gain)).astype(
        jnp.bfloat16
    )


def solution(mesh):
    in_specs = (
        P("req", "tok"),
        P("req", None),
        P("req", None),
        P(),
        P(),
        P("req", None),
        P(),
        P(),
        P("req", None),
        P("tok", None),
        P(),
        P(),
        P(),
        P(None, "tok"),
        P(None, "tok"),
        P("tok", None),
    )
    out_specs = P(("req", "tok"), None)
    return jax.shard_map(local, mesh=mesh, in_specs=in_specs, out_specs=out_specs, check_vma=False)
```

```python
import jax
import jax.numpy as jnp
from jax import lax
from jax.sharding import PartitionSpec as P
from jax.experimental import pallas as pl
from jax.experimental.pallas import tpu as pltpu

H = 8
KVH = 4
HD = 256
GROUPS = 2


EPSILON = 1e-06
MASKED = -1e30


def rms_scale(values_in, gain_vec):
    return (
        values_in
        * lax.rsqrt(jnp.mean(values_in * values_in, axis=-1, keepdims=True) + EPSILON)
        * gain_vec
    )


def norm_heads(values_in, gain_vec, head_count):
    row_count = values_in.shape[0]
    shaped = values_in.astype(jnp.float32).reshape(row_count, head_count, HD)
    return rms_scale(shaped, gain_vec).astype(jnp.bfloat16).reshape(row_count, head_count * HD)


def gather_tok_kernel(tok_count, w_ref, out_ref, send_sem, recv_sem, local_sem):
    mesh_ids = pl.DeviceIdType.MESH
    me = lax.axis_index("tok")
    up = lax.rem(me + 2, tok_count)
    down = lax.rem(me + tok_count - 2, tok_count)
    far = lax.rem(me + 4, tok_count)
    partner = me + 1 - 2 * lax.rem(me, 2)
    half = w_ref.shape[0] // 2

    barrier = pltpu.get_barrier_semaphore()
    for peer in (up, down, partner):
        pl.semaphore_signal(barrier, inc=1, device_id={"tok": peer}, device_id_type=mesh_ids)
    pl.semaphore_wait(barrier, 3)

    def remote(src, dst, slot, peer):
        return pltpu.make_async_remote_copy(
            src_ref=src,
            dst_ref=dst,
            send_sem=send_sem.at[slot],
            recv_sem=recv_sem.at[slot],
            device_id={"tok": peer},
            device_id_type=mesh_ids,
        )

    local = pltpu.make_async_copy(w_ref, out_ref.at[me], local_sem.at[0])
    local.start()
    to_up = remote(w_ref, out_ref.at[me], 0, up)
    to_down = remote(w_ref, out_ref.at[me], 1, down)
    to_up.start()
    to_down.start()
    remote(w_ref, out_ref.at[down], 0, down).wait_recv()
    remote(w_ref, out_ref.at[up], 1, up).wait_recv()

    first = pl.ds(0, half)
    second = pl.ds(half, half)
    fwd_up = remote(out_ref.at[down, first], out_ref.at[down, first], 2, up)
    fwd_down = remote(out_ref.at[up, second], out_ref.at[up, second], 3, down)
    fwd_up.start()
    fwd_down.start()
    remote(out_ref.at[far, first], out_ref.at[far, first], 2, down).wait_recv()
    remote(out_ref.at[far, second], out_ref.at[far, second], 3, up).wait_recv()
    local.wait()

    mine = (me, up, down, far)
    theirs = (
        partner,
        lax.rem(partner + 2, tok_count),
        lax.rem(partner + tok_count - 2, tok_count),
        lax.rem(partner + 4, tok_count),
    )
    to_partner = []
    for idx, slot in enumerate(mine):
        copy = remote(out_ref.at[slot], out_ref.at[slot], 4 + idx, partner)
        copy.start()
        to_partner.append(copy)
    for idx, slot in enumerate(theirs):
        remote(out_ref.at[slot], out_ref.at[slot], 4 + idx, partner).wait_recv()
    for copy in [to_up, to_down, fwd_up, fwd_down] + to_partner:
        copy.wait_send()


def gather_over_tok(block, tok_count, collective_id):
    assert tok_count == 8
    rows, cols = block.shape
    return pl.pallas_call(
        lambda *refs: gather_tok_kernel(tok_count, *refs),
        out_shape=jax.ShapeDtypeStruct((tok_count, rows, cols), block.dtype),
        in_specs=[pl.BlockSpec(memory_space=pl.ANY)],
        out_specs=pl.BlockSpec(memory_space=pl.ANY),
        scratch_shapes=[
            pltpu.SemaphoreType.DMA((8,)),
            pltpu.SemaphoreType.DMA((8,)),
            pltpu.SemaphoreType.DMA((1,)),
        ],
        compiler_params=pltpu.CompilerParams(collective_id=collective_id, has_side_effects=True),
        cost_estimate=pl.CostEstimate(
            flops=0, transcendentals=0, bytes_accessed=2 * tok_count * rows * cols * 2
        ),
    )(block)


def project_tok_kernel(
    tok_count, att_ref, w_hbm, out_ref, att_all, w_buf, send_sem, recv_sem, load_sem
):
    mesh_ids = pl.DeviceIdType.MESH
    me = lax.axis_index("tok")
    up = lax.rem(me + 2, tok_count)
    down = lax.rem(me + tok_count - 2, tok_count)
    far = lax.rem(me + 4, tok_count)
    partner = me + 1 - 2 * lax.rem(me, 2)
    half = att_ref.shape[0] // 2
    cols = out_ref.shape[1]
    tile = 512
    tiles = cols // tile

    barrier = pltpu.get_barrier_semaphore()
    for peer in (up, down, partner):
        pl.semaphore_signal(barrier, inc=1, device_id={"tok": peer}, device_id_type=mesh_ids)
    pl.semaphore_wait(barrier, 3)

    def remote(src, dst, slot, peer):
        return pltpu.make_async_remote_copy(
            src_ref=src,
            dst_ref=dst,
            send_sem=send_sem.at[slot],
            recv_sem=recv_sem.at[slot],
            device_id={"tok": peer},
            device_id_type=mesh_ids,
        )

    theirs = (
        partner,
        lax.rem(partner + 2, tok_count),
        lax.rem(partner + tok_count - 2, tok_count),
        lax.rem(partner + 4, tok_count),
    )
    order = (me, down, up, far) + theirs

    def load(idx):
        return pltpu.make_async_copy(w_hbm.at[order[idx]], w_buf.at[idx % 2], load_sem.at[idx % 2])

    def accumulate(idx, source, first):
        load(idx).wait()
        if idx + 1 < len(order):
            load(idx + 1).start()
        weights = w_buf.at[idx % 2]

        def one_tile(col):
            span = pl.ds(pl.multiple_of(col * tile, tile), tile)
            term = jnp.dot(source[...], weights[:, span], preferred_element_type=jnp.float32)
            if first:
                out_ref[:, span] = term
            else:
                out_ref[:, span] = out_ref[:, span] + term

        pl.loop(0, tiles)(one_tile)

    load(0).start()
    sends = []
    to_up = remote(att_ref, att_all.at[me], 0, up)
    to_down = remote(att_ref, att_all.at[me], 1, down)
    to_up.start()
    to_down.start()
    sends += [to_up, to_down]
    accumulate(0, att_ref, True)
    remote(att_ref, att_all.at[down], 0, down).wait_recv()
    remote(att_ref, att_all.at[up], 1, up).wait_recv()
    first = pl.ds(0, half)
    second = pl.ds(half, half)
    fwd_up = remote(att_all.at[down, first], att_all.at[down, first], 2, up)
    fwd_down = remote(att_all.at[up, second], att_all.at[up, second], 3, down)
    fwd_up.start()
    fwd_down.start()
    sends += [fwd_up, fwd_down]
    accumulate(1, att_all.at[down], False)
    accumulate(2, att_all.at[up], False)
    remote(att_all.at[far, first], att_all.at[far, first], 2, down).wait_recv()
    remote(att_all.at[far, second], att_all.at[far, second], 3, up).wait_recv()
    for idx, (src, slot) in enumerate(
        ((att_ref, me), (att_all.at[up], up), (att_all.at[down], down), (att_all.at[far], far))
    ):
        copy = remote(src, att_all.at[slot], 4 + idx, partner)
        copy.start()
        sends.append(copy)
    accumulate(3, att_all.at[far], False)
    for idx, slot in enumerate(theirs):
        remote(att_all.at[slot], att_all.at[slot], 4 + idx, partner).wait_recv()
        accumulate(4 + idx, att_all.at[slot], False)
    for copy in sends:
        copy.wait_send()


def project_over_tok(attention, w_all, tok_count, collective_id):
    assert tok_count == 8
    rows, width = attention.shape
    cols = w_all.shape[2]
    vmem = pltpu.MemorySpace.VMEM
    return pl.pallas_call(
        lambda *refs: project_tok_kernel(tok_count, *refs),
        out_shape=jax.ShapeDtypeStruct((rows, cols), jnp.float32),
        in_specs=[pl.BlockSpec(memory_space=vmem), pl.BlockSpec(memory_space=pl.ANY)],
        out_specs=pl.BlockSpec(memory_space=vmem),
        scratch_shapes=[
            pltpu.VMEM((tok_count, rows, width), attention.dtype),
            pltpu.VMEM((2, width, cols), w_all.dtype),
            pltpu.SemaphoreType.DMA((8,)),
            pltpu.SemaphoreType.DMA((8,)),
            pltpu.SemaphoreType.DMA((2,)),
        ],
        compiler_params=pltpu.CompilerParams(
            collective_id=collective_id, has_side_effects=True, vmem_limit_bytes=48 * 1024 * 1024
        ),
        cost_estimate=pl.CostEstimate(
            flops=2 * rows * width * tok_count * cols,
            transcendentals=0,
            bytes_accessed=tok_count * width * cols * 2 + rows * cols * 4,
        ),
    )(attention, w_all)


def scatter_tok_kernel(
    tok_count, part_hbm, out_ref, mine, chip_in, cross_out, cross_in, load_sem, send_sem, recv_sem
):
    mesh_ids = pl.DeviceIdType.MESH
    me = lax.axis_index("tok")
    up = lax.rem(me + 2, tok_count)
    down = lax.rem(me + tok_count - 2, tok_count)
    far = lax.rem(me + 4, tok_count)
    partner = me + 1 - 2 * lax.rem(me, 2)
    share = out_ref.shape[0]

    barrier = pltpu.get_barrier_semaphore()
    for peer in (up, down, far, partner):
        pl.semaphore_signal(barrier, inc=1, device_id={"tok": peer}, device_id_type=mesh_ids)
    pl.semaphore_wait(barrier, 4)

    def remote(src, dst, slot, peer):
        return pltpu.make_async_remote_copy(
            src_ref=src,
            dst_ref=dst,
            send_sem=send_sem.at[slot],
            recv_sem=recv_sem.at[slot],
            device_id={"tok": peer},
            device_id_type=mesh_ids,
        )

    def family(base):
        return (
            base,
            lax.rem(base + 2, tok_count),
            lax.rem(base + tok_count - 2, tok_count),
            lax.rem(base + 4, tok_count),
        )

    def rows_of(block):
        return pl.ds(pl.multiple_of(block * share, share), share)

    order = (3, 1, 2, 0)
    sends = []
    theirs = family(partner)
    for idx in order:
        copy = remote(part_hbm.at[rows_of(theirs[idx])], chip_in.at[idx], idx, partner)
        copy.start()
        sends.append(copy)
    own = family(me)
    loads = []
    for idx in order:
        load = pltpu.make_async_copy(part_hbm.at[rows_of(own[idx])], mine.at[idx], load_sem.at[idx])
        load.start()
        loads.append(load)
    targets = {1: (up, 1), 2: (down, 0), 3: (far, 2)}
    for pos, idx in enumerate(order[:3]):
        loads[pos].wait()
        remote(part_hbm.at[rows_of(own[idx])], chip_in.at[idx], idx, partner).wait_recv()
        cross_out[idx - 1] = (mine[idx] + chip_in[idx]).astype(cross_out.dtype)
        peer, dst_idx = targets[idx]
        copy = remote(cross_out.at[idx - 1], cross_in.at[dst_idx], 4 + dst_idx, peer)
        copy.start()
        sends.append(copy)
    loads[3].wait()
    remote(part_hbm.at[rows_of(own[0])], chip_in.at[0], 0, partner).wait_recv()
    total = mine[0] + chip_in[0]
    for idx, peer in ((0, up), (1, down), (2, far)):
        remote(cross_out.at[idx], cross_in.at[idx], 4 + idx, peer).wait_recv()
    for idx in range(3):
        total = total + cross_in[idx].astype(jnp.float32)
    out_ref[...] = total
    for copy in sends:
        copy.wait_send()


def scatter_over_tok(partial, tok_count, collective_id):
    assert tok_count == 8
    rows, cols = partial.shape
    share = rows // tok_count
    vmem = pltpu.MemorySpace.VMEM
    return pl.pallas_call(
        lambda *refs: scatter_tok_kernel(tok_count, *refs),
        out_shape=jax.ShapeDtypeStruct((share, cols), jnp.float32),
        in_specs=[pl.BlockSpec(memory_space=pltpu.MemorySpace.HBM)],
        out_specs=pl.BlockSpec(memory_space=vmem),
        scratch_shapes=[
            pltpu.VMEM((4, share, cols), jnp.float32),
            pltpu.VMEM((4, share, cols), jnp.float32),
            pltpu.VMEM((3, share, cols), jnp.bfloat16),
            pltpu.VMEM((3, share, cols), jnp.bfloat16),
            pltpu.SemaphoreType.DMA((4,)),
            pltpu.SemaphoreType.DMA((7,)),
            pltpu.SemaphoreType.DMA((7,)),
        ],
        compiler_params=pltpu.CompilerParams(
            collective_id=collective_id, has_side_effects=True, vmem_limit_bytes=48 * 1024 * 1024
        ),
        cost_estimate=pl.CostEstimate(
            flops=8 * share * cols, transcendentals=0, bytes_accessed=rows * cols * 4 * 2
        ),
    )(partial)


def local(
    queries,
    suffix_kv,
    prefix_cache,
    q_gain,
    k_gain,
    lengths,
    group_of,
    owner_order,
    residual,
    w_out,
    attn_gain,
    ffn_in_gain,
    ffn_out_gain,
    w_gate,
    w_up,
    w_down,
):
    req_count = lax.axis_size("req")
    tok_count = lax.axis_size("tok")
    req_index = lax.axis_index("req")
    tok_index = lax.axis_index("tok")
    row_count = queries.shape[0]
    heads_here = queries.shape[1] // HD
    head_ratio = H // KVH
    kv_first = tok_index * heads_here // head_ratio
    kv_width = KVH * HD
    own_count = req_count // GROUPS

    with jax.named_scope("prefix_gather"):
        pref_keys = lax.dynamic_slice_in_dim(prefix_cache, kv_first * HD, HD, 1)
        pref_vals = lax.dynamic_slice_in_dim(prefix_cache, kv_width + kv_first * HD, HD, 1)
        pref_kv = jnp.concatenate([pref_keys, pref_vals], axis=1)
        half_rows = pref_kv.shape[0] // 2
        core = tok_index % 2
        my_half = lax.dynamic_slice_in_dim(pref_kv, core * half_rows, half_rows, 0)
        gathered = lax.all_gather(my_half, "req", axis=0, tiled=False)
        w_out_all = gather_over_tok(w_out, tok_count, 0)
        gathered, w_out_all = lax.optimization_barrier((gathered, w_out_all))
        own_group = group_of[req_index]
        owner_ids = lax.dynamic_slice_in_dim(owner_order, own_group * own_count, own_count)
        picked = jnp.take(gathered, owner_ids, axis=0).reshape(-1, 2 * HD)
        partner = [(t, t ^ 1) for t in range(tok_count)]
        swapped = lax.ppermute(picked, "tok", perm=partner)
        shared = jnp.concatenate([picked, swapped], axis=0)

    with jax.named_scope("attention"):
        query_normed = norm_heads(queries, q_gain, heads_here)
        suf_keys = norm_heads(
            lax.dynamic_slice_in_dim(suffix_kv, kv_first * HD, HD, 1), k_gain, 1
        )
        suf_vals = lax.dynamic_slice_in_dim(suffix_kv, kv_width + kv_first * HD, HD, 1)
        all_keys = jnp.concatenate([shared[:, :HD], suf_keys], axis=0)
        all_vals = jnp.concatenate([shared[:, HD:], suf_vals], axis=0)
        seg_ends = jnp.cumsum(lengths[0])
        positions = jnp.arange(row_count, dtype=jnp.int32)
        segment = jnp.sum((positions[:, None] >= seg_ends[None, :]).astype(jnp.int32), axis=1)
        causal = (segment[:, None] == segment[None, :]) & (positions[None, :] <= positions[:, None])
        visible = jnp.concatenate(
            [jnp.ones((row_count, shared.shape[0]), jnp.bool_), causal], axis=1
        )
        outputs = []
        for head_idx in range(heads_here):
            head_q = query_normed[:, head_idx * HD:(head_idx + 1) * HD]
            scores = jnp.dot(head_q, all_keys.T, preferred_element_type=jnp.float32) * HD ** (-0.5)
            scores = jnp.where(visible, scores, MASKED)
            row_max = jnp.max(scores, axis=-1, keepdims=True)
            weights = jnp.exp(scores - row_max)
            row_sum = jnp.sum(weights, axis=-1, keepdims=True)
            head_out = jnp.dot(
                weights.astype(jnp.bfloat16), all_vals, preferred_element_type=jnp.float32
            ) / row_sum
            outputs.append(head_out)
        attention = jnp.concatenate(outputs, axis=1).astype(jnp.bfloat16)

    share = row_count // tok_count
    first_row = tok_index * share
    with jax.named_scope("out_projection"):
        projected = project_over_tok(attention, w_out_all, tok_count, 1)
        mixed_rows = residual.astype(jnp.float32) + rms_scale(projected, attn_gain)
        normed = rms_scale(mixed_rows, ffn_in_gain).astype(jnp.bfloat16)
        mixed_share = lax.dynamic_slice_in_dim(mixed_rows, first_row, share, 0)
    with jax.named_scope("feed_forward"):
        normed = lax.optimization_barrier(normed)
        gate = jnp.dot(normed, w_gate, preferred_element_type=jnp.float32)
        upward = jnp.dot(normed, w_up, preferred_element_type=jnp.float32)
        hidden = (jax.nn.gelu(gate, approximate=True) * upward).astype(jnp.bfloat16)
        hidden = lax.optimization_barrier(hidden)
        down_share = scatter_over_tok(
            jnp.dot(hidden, w_down, preferred_element_type=jnp.float32), tok_count, 2
        )
    return (mixed_share + rms_scale(down_share.astype(jnp.float32), ffn_out_gain)).astype(
        jnp.bfloat16
    )


def solution(mesh):
    in_specs = (
        P("req", "tok"),
        P("req", None),
        P("req", None),
        P(),
        P(),
        P("req", None),
        P(),
        P(),
        P("req", None),
        P("tok", None),
        P(),
        P(),
        P(),
        P(None, "tok"),
        P(None, "tok"),
        P("tok", None),
    )
    out_specs = P(("req", "tok"), None)
    return jax.shard_map(local, mesh=mesh, in_specs=in_specs, out_specs=out_specs, check_vma=False)
```

```python
import jax
import jax.numpy as jnp
from jax import lax
from jax.sharding import PartitionSpec as P
from jax.experimental import pallas as pl
from jax.experimental.pallas import tpu as pltpu

H = 8
KVH = 4
HD = 256
GROUPS = 2


EPSILON = 1e-06
MASKED = -1e30


def rms_scale(values_in, gain_vec):
    return (
        values_in
        * lax.rsqrt(jnp.mean(values_in * values_in, axis=-1, keepdims=True) + EPSILON)
        * gain_vec
    )


def norm_heads(values_in, gain_vec, head_count):
    row_count = values_in.shape[0]
    shaped = values_in.astype(jnp.float32).reshape(row_count, head_count, HD)
    return rms_scale(shaped, gain_vec).astype(jnp.bfloat16).reshape(row_count, head_count * HD)


def gather_tok_kernel(tok_count, w_ref, out_ref, send_sem, recv_sem, local_sem):
    mesh_ids = pl.DeviceIdType.MESH
    me = lax.axis_index("tok")
    up = lax.rem(me + 2, tok_count)
    down = lax.rem(me + tok_count - 2, tok_count)
    far = lax.rem(me + 4, tok_count)
    partner = me + 1 - 2 * lax.rem(me, 2)
    half = w_ref.shape[0] // 2

    barrier = pltpu.get_barrier_semaphore()
    for peer in (up, down, partner):
        pl.semaphore_signal(barrier, inc=1, device_id={"tok": peer}, device_id_type=mesh_ids)
    pl.semaphore_wait(barrier, 3)

    def remote(src, dst, slot, peer):
        return pltpu.make_async_remote_copy(
            src_ref=src,
            dst_ref=dst,
            send_sem=send_sem.at[slot],
            recv_sem=recv_sem.at[slot],
            device_id={"tok": peer},
            device_id_type=mesh_ids,
        )

    local = pltpu.make_async_copy(w_ref, out_ref.at[me], local_sem.at[0])
    local.start()
    to_up = remote(w_ref, out_ref.at[me], 0, up)
    to_down = remote(w_ref, out_ref.at[me], 1, down)
    to_up.start()
    to_down.start()
    remote(w_ref, out_ref.at[down], 0, down).wait_recv()
    remote(w_ref, out_ref.at[up], 1, up).wait_recv()

    first = pl.ds(0, half)
    second = pl.ds(half, half)
    fwd_up = remote(out_ref.at[down, first], out_ref.at[down, first], 2, up)
    fwd_down = remote(out_ref.at[up, second], out_ref.at[up, second], 3, down)
    fwd_up.start()
    fwd_down.start()
    remote(out_ref.at[far, first], out_ref.at[far, first], 2, down).wait_recv()
    remote(out_ref.at[far, second], out_ref.at[far, second], 3, up).wait_recv()
    local.wait()

    mine = (me, up, down, far)
    theirs = (
        partner,
        lax.rem(partner + 2, tok_count),
        lax.rem(partner + tok_count - 2, tok_count),
        lax.rem(partner + 4, tok_count),
    )
    to_partner = []
    for idx, slot in enumerate(mine):
        copy = remote(out_ref.at[slot], out_ref.at[slot], 4 + idx, partner)
        copy.start()
        to_partner.append(copy)
    for idx, slot in enumerate(theirs):
        remote(out_ref.at[slot], out_ref.at[slot], 4 + idx, partner).wait_recv()
    for copy in [to_up, to_down, fwd_up, fwd_down] + to_partner:
        copy.wait_send()


def gather_over_tok(block, tok_count, collective_id):
    assert tok_count == 8
    rows, cols = block.shape
    return pl.pallas_call(
        lambda *refs: gather_tok_kernel(tok_count, *refs),
        out_shape=jax.ShapeDtypeStruct((tok_count, rows, cols), block.dtype),
        in_specs=[pl.BlockSpec(memory_space=pl.ANY)],
        out_specs=pl.BlockSpec(memory_space=pl.ANY),
        scratch_shapes=[
            pltpu.SemaphoreType.DMA((8,)),
            pltpu.SemaphoreType.DMA((8,)),
            pltpu.SemaphoreType.DMA((1,)),
        ],
        compiler_params=pltpu.CompilerParams(collective_id=collective_id, has_side_effects=True),
        cost_estimate=pl.CostEstimate(
            flops=0, transcendentals=0, bytes_accessed=2 * tok_count * rows * cols * 2
        ),
    )(block)


def project_tok_kernel(
    tok_count, att_ref, w_hbm, out_ref, att_all, w_buf, send_sem, recv_sem, load_sem
):
    mesh_ids = pl.DeviceIdType.MESH
    me = lax.axis_index("tok")
    up = lax.rem(me + 2, tok_count)
    down = lax.rem(me + tok_count - 2, tok_count)
    far = lax.rem(me + 4, tok_count)
    partner = me + 1 - 2 * lax.rem(me, 2)
    half = att_ref.shape[0] // 2
    cols = out_ref.shape[1]
    tile = 512
    tiles = cols // tile

    barrier = pltpu.get_barrier_semaphore()
    for peer in (up, down, partner):
        pl.semaphore_signal(barrier, inc=1, device_id={"tok": peer}, device_id_type=mesh_ids)
    pl.semaphore_wait(barrier, 3)

    def remote(src, dst, slot, peer):
        return pltpu.make_async_remote_copy(
            src_ref=src,
            dst_ref=dst,
            send_sem=send_sem.at[slot],
            recv_sem=recv_sem.at[slot],
            device_id={"tok": peer},
            device_id_type=mesh_ids,
        )

    theirs = (
        partner,
        lax.rem(partner + 2, tok_count),
        lax.rem(partner + tok_count - 2, tok_count),
        lax.rem(partner + 4, tok_count),
    )
    order = (me, down, up, far) + theirs

    def load(idx):
        return pltpu.make_async_copy(w_hbm.at[order[idx]], w_buf.at[idx % 2], load_sem.at[idx % 2])

    def accumulate(idx, source, first):
        load(idx).wait()
        if idx + 1 < len(order):
            load(idx + 1).start()
        weights = w_buf.at[idx % 2]

        def one_tile(col):
            span = pl.ds(pl.multiple_of(col * tile, tile), tile)
            term = jnp.dot(source[...], weights[:, span], preferred_element_type=jnp.float32)
            if first:
                out_ref[:, span] = term
            else:
                out_ref[:, span] = out_ref[:, span] + term

        pl.loop(0, tiles)(one_tile)

    load(0).start()
    sends = []
    to_up = remote(att_ref, att_all.at[me], 0, up)
    to_down = remote(att_ref, att_all.at[me], 1, down)
    to_up.start()
    to_down.start()
    sends += [to_up, to_down]
    accumulate(0, att_ref, True)
    remote(att_ref, att_all.at[down], 0, down).wait_recv()
    remote(att_ref, att_all.at[up], 1, up).wait_recv()
    first = pl.ds(0, half)
    second = pl.ds(half, half)
    fwd_up = remote(att_all.at[down, first], att_all.at[down, first], 2, up)
    fwd_down = remote(att_all.at[up, second], att_all.at[up, second], 3, down)
    fwd_up.start()
    fwd_down.start()
    sends += [fwd_up, fwd_down]
    accumulate(1, att_all.at[down], False)
    accumulate(2, att_all.at[up], False)
    remote(att_all.at[far, first], att_all.at[far, first], 2, down).wait_recv()
    remote(att_all.at[far, second], att_all.at[far, second], 3, up).wait_recv()
    for idx, (src, slot) in enumerate(
        ((att_ref, me), (att_all.at[up], up), (att_all.at[down], down), (att_all.at[far], far))
    ):
        copy = remote(src, att_all.at[slot], 4 + idx, partner)
        copy.start()
        sends.append(copy)
    accumulate(3, att_all.at[far], False)
    for idx, slot in enumerate(theirs):
        remote(att_all.at[slot], att_all.at[slot], 4 + idx, partner).wait_recv()
        accumulate(4 + idx, att_all.at[slot], False)
    for copy in sends:
        copy.wait_send()


def project_over_tok(attention, w_all, tok_count, collective_id):
    assert tok_count == 8
    rows, width = attention.shape
    cols = w_all.shape[2]
    vmem = pltpu.MemorySpace.VMEM
    return pl.pallas_call(
        lambda *refs: project_tok_kernel(tok_count, *refs),
        out_shape=jax.ShapeDtypeStruct((rows, cols), jnp.float32),
        in_specs=[pl.BlockSpec(memory_space=vmem), pl.BlockSpec(memory_space=pl.ANY)],
        out_specs=pl.BlockSpec(memory_space=vmem),
        scratch_shapes=[
            pltpu.VMEM((tok_count, rows, width), attention.dtype),
            pltpu.VMEM((2, width, cols), w_all.dtype),
            pltpu.SemaphoreType.DMA((8,)),
            pltpu.SemaphoreType.DMA((8,)),
            pltpu.SemaphoreType.DMA((2,)),
        ],
        compiler_params=pltpu.CompilerParams(
            collective_id=collective_id, has_side_effects=True, vmem_limit_bytes=48 * 1024 * 1024
        ),
        cost_estimate=pl.CostEstimate(
            flops=2 * rows * width * tok_count * cols,
            transcendentals=0,
            bytes_accessed=tok_count * width * cols * 2 + rows * cols * 4,
        ),
    )(attention, w_all)


def scatter_tok_kernel(
    tok_count, part_hbm, out_ref, mine, chip_in, cross_out, cross_in, load_sem, send_sem, recv_sem
):
    mesh_ids = pl.DeviceIdType.MESH
    me = lax.axis_index("tok")
    up = lax.rem(me + 2, tok_count)
    down = lax.rem(me + tok_count - 2, tok_count)
    far = lax.rem(me + 4, tok_count)
    partner = me + 1 - 2 * lax.rem(me, 2)
    share = out_ref.shape[0]

    barrier = pltpu.get_barrier_semaphore()
    for peer in (up, down, far, partner):
        pl.semaphore_signal(barrier, inc=1, device_id={"tok": peer}, device_id_type=mesh_ids)
    pl.semaphore_wait(barrier, 4)

    def remote(src, dst, slot, peer):
        return pltpu.make_async_remote_copy(
            src_ref=src,
            dst_ref=dst,
            send_sem=send_sem.at[slot],
            recv_sem=recv_sem.at[slot],
            device_id={"tok": peer},
            device_id_type=mesh_ids,
        )

    def family(base):
        return (
            base,
            lax.rem(base + 2, tok_count),
            lax.rem(base + tok_count - 2, tok_count),
            lax.rem(base + 4, tok_count),
        )

    def rows_of(block):
        return pl.ds(pl.multiple_of(block * share, share), share)

    order = (3, 1, 2, 0)
    sends = []
    theirs = family(partner)
    for idx in order:
        copy = remote(part_hbm.at[rows_of(theirs[idx])], chip_in.at[idx], idx, partner)
        copy.start()
        sends.append(copy)
    own = family(me)
    loads = []
    for idx in order:
        load = pltpu.make_async_copy(part_hbm.at[rows_of(own[idx])], mine.at[idx], load_sem.at[idx])
        load.start()
        loads.append(load)
    targets = {1: (up, 1), 2: (down, 0), 3: (far, 2)}
    for pos, idx in enumerate(order[:3]):
        loads[pos].wait()
        remote(part_hbm.at[rows_of(own[idx])], chip_in.at[idx], idx, partner).wait_recv()
        cross_out[idx - 1] = (mine[idx] + chip_in[idx]).astype(cross_out.dtype)
        peer, dst_idx = targets[idx]
        copy = remote(cross_out.at[idx - 1], cross_in.at[dst_idx], 4 + dst_idx, peer)
        copy.start()
        sends.append(copy)
    loads[3].wait()
    remote(part_hbm.at[rows_of(own[0])], chip_in.at[0], 0, partner).wait_recv()
    total = mine[0] + chip_in[0]
    for idx, peer in ((0, up), (1, down), (2, far)):
        remote(cross_out.at[idx], cross_in.at[idx], 4 + idx, peer).wait_recv()
    for idx in range(3):
        total = total + cross_in[idx].astype(jnp.float32)
    out_ref[...] = total
    for copy in sends:
        copy.wait_send()


def scatter_over_tok(partial, tok_count, collective_id):
    assert tok_count == 8
    rows, cols = partial.shape
    share = rows // tok_count
    vmem = pltpu.MemorySpace.VMEM
    return pl.pallas_call(
        lambda *refs: scatter_tok_kernel(tok_count, *refs),
        out_shape=jax.ShapeDtypeStruct((share, cols), jnp.float32),
        in_specs=[pl.BlockSpec(memory_space=pltpu.MemorySpace.HBM)],
        out_specs=pl.BlockSpec(memory_space=vmem),
        scratch_shapes=[
            pltpu.VMEM((4, share, cols), jnp.float32),
            pltpu.VMEM((4, share, cols), jnp.float32),
            pltpu.VMEM((3, share, cols), jnp.bfloat16),
            pltpu.VMEM((3, share, cols), jnp.bfloat16),
            pltpu.SemaphoreType.DMA((4,)),
            pltpu.SemaphoreType.DMA((7,)),
            pltpu.SemaphoreType.DMA((7,)),
        ],
        compiler_params=pltpu.CompilerParams(
            collective_id=collective_id, has_side_effects=True, vmem_limit_bytes=48 * 1024 * 1024
        ),
        cost_estimate=pl.CostEstimate(
            flops=8 * share * cols, transcendentals=0, bytes_accessed=rows * cols * 4 * 2
        ),
    )(partial)


def local(
    queries,
    suffix_kv,
    prefix_cache,
    q_gain,
    k_gain,
    lengths,
    group_of,
    owner_order,
    residual,
    w_out,
    attn_gain,
    ffn_in_gain,
    ffn_out_gain,
    w_gate,
    w_up,
    w_down,
):
    req_count = lax.axis_size("req")
    tok_count = lax.axis_size("tok")
    req_index = lax.axis_index("req")
    tok_index = lax.axis_index("tok")
    row_count = queries.shape[0]
    heads_here = queries.shape[1] // HD
    head_ratio = H // KVH
    kv_first = tok_index * heads_here // head_ratio
    kv_width = KVH * HD
    own_count = req_count // GROUPS

    with jax.named_scope("prefix_gather"):
        pref_keys = lax.dynamic_slice_in_dim(prefix_cache, kv_first * HD, HD, 1)
        pref_vals = lax.dynamic_slice_in_dim(prefix_cache, kv_width + kv_first * HD, HD, 1)
        pref_kv = jnp.concatenate([pref_keys, pref_vals], axis=1)
        half_rows = pref_kv.shape[0] // 2
        core = tok_index % 2
        my_half = lax.dynamic_slice_in_dim(pref_kv, core * half_rows, half_rows, 0)
        gathered = lax.all_gather(my_half, "req", axis=0, tiled=False)
        w_out_all = gather_over_tok(w_out, tok_count, 0)
        gathered, w_out_all = lax.optimization_barrier((gathered, w_out_all))
        own_group = group_of[req_index]
        owner_ids = lax.dynamic_slice_in_dim(owner_order, own_group * own_count, own_count)
        picked = jnp.concatenate(
            [lax.dynamic_index_in_dim(gathered, owner_ids[j], 0, keepdims=False) for j in range(own_count)],
            axis=0,
        )
        partner = [(t, t ^ 1) for t in range(tok_count)]
        swapped = lax.ppermute(picked, "tok", perm=partner)

    with jax.named_scope("attention"):
        query_normed = norm_heads(queries, q_gain, heads_here)
        suf_keys = norm_heads(
            lax.dynamic_slice_in_dim(suffix_kv, kv_first * HD, HD, 1), k_gain, 1
        )
        suf_vals = lax.dynamic_slice_in_dim(suffix_kv, kv_width + kv_first * HD, HD, 1)
        seg_ends = jnp.cumsum(lengths[0])
        positions = jnp.arange(row_count, dtype=jnp.int32)
        segment = jnp.sum((positions[:, None] >= seg_ends[None, :]).astype(jnp.int32), axis=1)
        causal = (segment[:, None] == segment[None, :]) & (positions[None, :] <= positions[:, None])
        key_sets = (
            (picked[:, :HD], picked[:, HD:], None),
            (swapped[:, :HD], swapped[:, HD:], None),
            (suf_keys, suf_vals, causal),
        )
        outputs = []
        for head_idx in range(heads_here):
            head_q = query_normed[:, head_idx * HD:(head_idx + 1) * HD]
            parts = []
            for keys, vals, mask in key_sets:
                scores = jnp.dot(head_q, keys.T, preferred_element_type=jnp.float32) * HD ** (-0.5)
                if mask is not None:
                    scores = jnp.where(mask, scores, MASKED)
                parts.append(scores)
            row_max = parts[0].max(axis=-1, keepdims=True)
            for scores in parts[1:]:
                row_max = jnp.maximum(row_max, scores.max(axis=-1, keepdims=True))
            row_sum = 0.0
            head_out = 0.0
            for scores, (keys, vals, mask) in zip(parts, key_sets):
                weights = jnp.exp(scores - row_max)
                row_sum = row_sum + jnp.sum(weights, axis=-1, keepdims=True)
                head_out = head_out + jnp.dot(
                    weights.astype(jnp.bfloat16), vals, preferred_element_type=jnp.float32
                )
            outputs.append(head_out / row_sum)
        attention = jnp.concatenate(outputs, axis=1).astype(jnp.bfloat16)

    share = row_count // tok_count
    first_row = tok_index * share
    with jax.named_scope("out_projection"):
        projected = project_over_tok(attention, w_out_all, tok_count, 1)
        mixed_rows = residual.astype(jnp.float32) + rms_scale(projected, attn_gain)
        normed = rms_scale(mixed_rows, ffn_in_gain).astype(jnp.bfloat16)
        mixed_share = lax.dynamic_slice_in_dim(mixed_rows, first_row, share, 0)
    with jax.named_scope("feed_forward"):
        normed = lax.optimization_barrier(normed)
        gate = jnp.dot(normed, w_gate, preferred_element_type=jnp.float32)
        upward = jnp.dot(normed, w_up, preferred_element_type=jnp.float32)
        hidden = (jax.nn.gelu(gate, approximate=True) * upward).astype(jnp.bfloat16)
        hidden = lax.optimization_barrier(hidden)
        down_share = scatter_over_tok(
            jnp.dot(hidden, w_down, preferred_element_type=jnp.float32), tok_count, 2
        )
    return (mixed_share + rms_scale(down_share.astype(jnp.float32), ffn_out_gain)).astype(
        jnp.bfloat16
    )


def solution(mesh):
    in_specs = (
        P("req", "tok"),
        P("req", None),
        P("req", None),
        P(),
        P(),
        P("req", None),
        P(),
        P(),
        P("req", None),
        P("tok", None),
        P(),
        P(),
        P(),
        P(None, "tok"),
        P(None, "tok"),
        P("tok", None),
    )
    out_specs = P(("req", "tok"), None)
    return jax.shard_map(local, mesh=mesh, in_specs=in_specs, out_specs=out_specs, check_vma=False)
```

```python
import jax
import jax.numpy as jnp
from jax import lax
from jax.sharding import PartitionSpec as P
from jax.experimental import pallas as pl
from jax.experimental.pallas import tpu as pltpu

H = 8
KVH = 4
HD = 256
GROUPS = 2


EPSILON = 1e-06
MASKED = -1e30


def rms_scale(values_in, gain_vec):
    return (
        values_in
        * lax.rsqrt(jnp.mean(values_in * values_in, axis=-1, keepdims=True) + EPSILON)
        * gain_vec
    )


def norm_heads(values_in, gain_vec, head_count):
    row_count = values_in.shape[0]
    shaped = values_in.astype(jnp.float32).reshape(row_count, head_count, HD)
    return rms_scale(shaped, gain_vec).astype(jnp.bfloat16).reshape(row_count, head_count * HD)


def gather_tok_kernel(tok_count, w_ref, out_ref, send_sem, recv_sem, local_sem):
    mesh_ids = pl.DeviceIdType.MESH
    me = lax.axis_index("tok")
    up = lax.rem(me + 2, tok_count)
    down = lax.rem(me + tok_count - 2, tok_count)
    far = lax.rem(me + 4, tok_count)
    partner = me + 1 - 2 * lax.rem(me, 2)
    half = w_ref.shape[0] // 2

    barrier = pltpu.get_barrier_semaphore()
    for peer in (up, down, partner):
        pl.semaphore_signal(barrier, inc=1, device_id={"tok": peer}, device_id_type=mesh_ids)
    pl.semaphore_wait(barrier, 3)

    def remote(src, dst, slot, peer):
        return pltpu.make_async_remote_copy(
            src_ref=src,
            dst_ref=dst,
            send_sem=send_sem.at[slot],
            recv_sem=recv_sem.at[slot],
            device_id={"tok": peer},
            device_id_type=mesh_ids,
        )

    local = pltpu.make_async_copy(w_ref, out_ref.at[me], local_sem.at[0])
    local.start()
    to_up = remote(w_ref, out_ref.at[me], 0, up)
    to_down = remote(w_ref, out_ref.at[me], 1, down)
    to_up.start()
    to_down.start()
    remote(w_ref, out_ref.at[down], 0, down).wait_recv()
    remote(w_ref, out_ref.at[up], 1, up).wait_recv()

    first = pl.ds(0, half)
    second = pl.ds(half, half)
    fwd_up = remote(out_ref.at[down, first], out_ref.at[down, first], 2, up)
    fwd_down = remote(out_ref.at[up, second], out_ref.at[up, second], 3, down)
    fwd_up.start()
    fwd_down.start()
    remote(out_ref.at[far, first], out_ref.at[far, first], 2, down).wait_recv()
    remote(out_ref.at[far, second], out_ref.at[far, second], 3, up).wait_recv()
    local.wait()

    mine = (me, up, down, far)
    theirs = (
        partner,
        lax.rem(partner + 2, tok_count),
        lax.rem(partner + tok_count - 2, tok_count),
        lax.rem(partner + 4, tok_count),
    )
    to_partner = []
    for idx, slot in enumerate(mine):
        copy = remote(out_ref.at[slot], out_ref.at[slot], 4 + idx, partner)
        copy.start()
        to_partner.append(copy)
    for idx, slot in enumerate(theirs):
        remote(out_ref.at[slot], out_ref.at[slot], 4 + idx, partner).wait_recv()
    for copy in [to_up, to_down, fwd_up, fwd_down] + to_partner:
        copy.wait_send()


def gather_over_tok(block, tok_count, collective_id):
    assert tok_count == 8
    rows, cols = block.shape
    return pl.pallas_call(
        lambda *refs: gather_tok_kernel(tok_count, *refs),
        out_shape=jax.ShapeDtypeStruct((tok_count, rows, cols), block.dtype),
        in_specs=[pl.BlockSpec(memory_space=pl.ANY)],
        out_specs=pl.BlockSpec(memory_space=pl.ANY),
        scratch_shapes=[
            pltpu.SemaphoreType.DMA((8,)),
            pltpu.SemaphoreType.DMA((8,)),
            pltpu.SemaphoreType.DMA((1,)),
        ],
        compiler_params=pltpu.CompilerParams(collective_id=collective_id, has_side_effects=True),
        cost_estimate=pl.CostEstimate(
            flops=0, transcendentals=0, bytes_accessed=2 * tok_count * rows * cols * 2
        ),
    )(block)


def project_tok_kernel(
    tok_count, att_ref, w_hbm, out_ref, att_all, w_buf, send_sem, recv_sem, load_sem
):
    mesh_ids = pl.DeviceIdType.MESH
    me = lax.axis_index("tok")
    up = lax.rem(me + 2, tok_count)
    down = lax.rem(me + tok_count - 2, tok_count)
    far = lax.rem(me + 4, tok_count)
    partner = me + 1 - 2 * lax.rem(me, 2)
    half = att_ref.shape[0] // 2
    cols = out_ref.shape[1]
    tile = 512
    tiles = cols // tile

    barrier = pltpu.get_barrier_semaphore()
    for peer in (up, down, partner):
        pl.semaphore_signal(barrier, inc=1, device_id={"tok": peer}, device_id_type=mesh_ids)
    pl.semaphore_wait(barrier, 3)

    def remote(src, dst, slot, peer):
        return pltpu.make_async_remote_copy(
            src_ref=src,
            dst_ref=dst,
            send_sem=send_sem.at[slot],
            recv_sem=recv_sem.at[slot],
            device_id={"tok": peer},
            device_id_type=mesh_ids,
        )

    theirs = (
        partner,
        lax.rem(partner + 2, tok_count),
        lax.rem(partner + tok_count - 2, tok_count),
        lax.rem(partner + 4, tok_count),
    )
    order = (me, down, up, theirs[0], far) + theirs[1:]

    def load(idx):
        return pltpu.make_async_copy(w_hbm.at[order[idx]], w_buf.at[idx % 2], load_sem.at[idx % 2])

    def accumulate(idx, source, first):
        load(idx).wait()
        if idx + 1 < len(order):
            load(idx + 1).start()
        weights = w_buf.at[idx % 2]

        def one_tile(col):
            span = pl.ds(pl.multiple_of(col * tile, tile), tile)
            term = jnp.dot(source[...], weights[:, span], preferred_element_type=jnp.float32)
            if first:
                out_ref[:, span] = term
            else:
                out_ref[:, span] = out_ref[:, span] + term

        pl.loop(0, tiles)(one_tile)

    load(0).start()
    sends = []

    def send(src, slot, index, peer):
        copy = remote(src, att_all.at[slot], index, peer)
        copy.start()
        sends.append(copy)

    def arrived(slot, index, peer, rows=None):
        dst = att_all.at[slot] if rows is None else att_all.at[slot, rows]
        remote(dst, dst, index, peer).wait_recv()

    first = pl.ds(0, half)
    second = pl.ds(half, half)
    send(att_ref, me, 0, up)
    send(att_ref, me, 1, down)
    send(att_ref, me, 4, partner)
    accumulate(0, att_ref, True)
    arrived(down, 0, down)
    arrived(up, 1, up)
    for src, index, peer in ((att_all.at[down, first], 2, up), (att_all.at[up, second], 3, down)):
        copy = remote(src, src, index, peer)
        copy.start()
        sends.append(copy)
    send(att_all.at[up], up, 5, partner)
    send(att_all.at[down], down, 6, partner)
    accumulate(1, att_all.at[down], False)
    accumulate(2, att_all.at[up], False)
    arrived(theirs[0], 4, partner)
    accumulate(3, att_all.at[theirs[0]], False)
    arrived(far, 2, down, first)
    arrived(far, 3, up, second)
    send(att_all.at[far], far, 7, partner)
    accumulate(4, att_all.at[far], False)
    for idx in range(1, 4):
        arrived(theirs[idx], 4 + idx, partner)
        accumulate(4 + idx, att_all.at[theirs[idx]], False)
    for copy in sends:
        copy.wait_send()


def project_over_tok(attention, w_all, tok_count, collective_id):
    assert tok_count == 8
    rows, width = attention.shape
    cols = w_all.shape[2]
    vmem = pltpu.MemorySpace.VMEM
    return pl.pallas_call(
        lambda *refs: project_tok_kernel(tok_count, *refs),
        out_shape=jax.ShapeDtypeStruct((rows, cols), jnp.float32),
        in_specs=[pl.BlockSpec(memory_space=vmem), pl.BlockSpec(memory_space=pl.ANY)],
        out_specs=pl.BlockSpec(memory_space=vmem),
        scratch_shapes=[
            pltpu.VMEM((tok_count, rows, width), attention.dtype),
            pltpu.VMEM((2, width, cols), w_all.dtype),
            pltpu.SemaphoreType.DMA((8,)),
            pltpu.SemaphoreType.DMA((8,)),
            pltpu.SemaphoreType.DMA((2,)),
        ],
        compiler_params=pltpu.CompilerParams(
            collective_id=collective_id, has_side_effects=True, vmem_limit_bytes=48 * 1024 * 1024
        ),
        cost_estimate=pl.CostEstimate(
            flops=2 * rows * width * tok_count * cols,
            transcendentals=0,
            bytes_accessed=tok_count * width * cols * 2 + rows * cols * 4,
        ),
    )(attention, w_all)


def scatter_tok_kernel(
    tok_count, part_hbm, out_ref, mine, chip_in, cross_out, cross_in, load_sem, send_sem, recv_sem
):
    mesh_ids = pl.DeviceIdType.MESH
    me = lax.axis_index("tok")
    up = lax.rem(me + 2, tok_count)
    down = lax.rem(me + tok_count - 2, tok_count)
    far = lax.rem(me + 4, tok_count)
    partner = me + 1 - 2 * lax.rem(me, 2)
    share = out_ref.shape[0]

    barrier = pltpu.get_barrier_semaphore()
    for peer in (up, down, far, partner):
        pl.semaphore_signal(barrier, inc=1, device_id={"tok": peer}, device_id_type=mesh_ids)
    pl.semaphore_wait(barrier, 4)

    def remote(src, dst, slot, peer):
        return pltpu.make_async_remote_copy(
            src_ref=src,
            dst_ref=dst,
            send_sem=send_sem.at[slot],
            recv_sem=recv_sem.at[slot],
            device_id={"tok": peer},
            device_id_type=mesh_ids,
        )

    def family(base):
        return (
            base,
            lax.rem(base + 2, tok_count),
            lax.rem(base + tok_count - 2, tok_count),
            lax.rem(base + 4, tok_count),
        )

    def rows_of(block):
        return pl.ds(pl.multiple_of(block * share, share), share)

    order = (3, 1, 2, 0)
    sends = []
    theirs = family(partner)
    for idx in order:
        copy = remote(part_hbm.at[rows_of(theirs[idx])], chip_in.at[idx], idx, partner)
        copy.start()
        sends.append(copy)
    own = family(me)
    loads = []
    for idx in order:
        load = pltpu.make_async_copy(part_hbm.at[rows_of(own[idx])], mine.at[idx], load_sem.at[idx])
        load.start()
        loads.append(load)
    targets = {1: (up, 1), 2: (down, 0), 3: (far, 2)}
    for pos, idx in enumerate(order[:3]):
        loads[pos].wait()
        remote(part_hbm.at[rows_of(own[idx])], chip_in.at[idx], idx, partner).wait_recv()
        cross_out[idx - 1] = (mine[idx] + chip_in[idx]).astype(cross_out.dtype)
        peer, dst_idx = targets[idx]
        copy = remote(cross_out.at[idx - 1], cross_in.at[dst_idx], 4 + dst_idx, peer)
        copy.start()
        sends.append(copy)
    loads[3].wait()
    remote(part_hbm.at[rows_of(own[0])], chip_in.at[0], 0, partner).wait_recv()
    total = mine[0] + chip_in[0]
    for idx, peer in ((0, up), (1, down), (2, far)):
        remote(cross_out.at[idx], cross_in.at[idx], 4 + idx, peer).wait_recv()
    for idx in range(3):
        total = total + cross_in[idx].astype(jnp.float32)
    out_ref[...] = total
    for copy in sends:
        copy.wait_send()


def scatter_over_tok(partial, tok_count, collective_id):
    assert tok_count == 8
    rows, cols = partial.shape
    share = rows // tok_count
    vmem = pltpu.MemorySpace.VMEM
    return pl.pallas_call(
        lambda *refs: scatter_tok_kernel(tok_count, *refs),
        out_shape=jax.ShapeDtypeStruct((share, cols), jnp.float32),
        in_specs=[pl.BlockSpec(memory_space=pltpu.MemorySpace.HBM)],
        out_specs=pl.BlockSpec(memory_space=vmem),
        scratch_shapes=[
            pltpu.VMEM((4, share, cols), jnp.float32),
            pltpu.VMEM((4, share, cols), jnp.float32),
            pltpu.VMEM((3, share, cols), jnp.bfloat16),
            pltpu.VMEM((3, share, cols), jnp.bfloat16),
            pltpu.SemaphoreType.DMA((4,)),
            pltpu.SemaphoreType.DMA((7,)),
            pltpu.SemaphoreType.DMA((7,)),
        ],
        compiler_params=pltpu.CompilerParams(
            collective_id=collective_id, has_side_effects=True, vmem_limit_bytes=48 * 1024 * 1024
        ),
        cost_estimate=pl.CostEstimate(
            flops=8 * share * cols, transcendentals=0, bytes_accessed=rows * cols * 4 * 2
        ),
    )(partial)


def local(
    queries,
    suffix_kv,
    prefix_cache,
    q_gain,
    k_gain,
    lengths,
    group_of,
    owner_order,
    residual,
    w_out,
    attn_gain,
    ffn_in_gain,
    ffn_out_gain,
    w_gate,
    w_up,
    w_down,
):
    req_count = lax.axis_size("req")
    tok_count = lax.axis_size("tok")
    req_index = lax.axis_index("req")
    tok_index = lax.axis_index("tok")
    row_count = queries.shape[0]
    heads_here = queries.shape[1] // HD
    head_ratio = H // KVH
    kv_first = tok_index * heads_here // head_ratio
    kv_width = KVH * HD
    own_count = req_count // GROUPS

    with jax.named_scope("prefix_gather"):
        pref_keys = lax.dynamic_slice_in_dim(prefix_cache, kv_first * HD, HD, 1)
        pref_vals = lax.dynamic_slice_in_dim(prefix_cache, kv_width + kv_first * HD, HD, 1)
        pref_kv = jnp.concatenate([pref_keys, pref_vals], axis=1)
        half_rows = pref_kv.shape[0] // 2
        core = tok_index % 2
        my_half = lax.dynamic_slice_in_dim(pref_kv, core * half_rows, half_rows, 0)
        gathered = lax.all_gather(my_half, "req", axis=0, tiled=False)
        w_out_all = gather_over_tok(w_out, tok_count, 0)
        gathered, w_out_all = lax.optimization_barrier((gathered, w_out_all))
        own_group = group_of[req_index]
        owner_ids = lax.dynamic_slice_in_dim(owner_order, own_group * own_count, own_count)
        picked = jnp.take(gathered, owner_ids, axis=0, mode="clip").reshape(-1, 2 * HD)
        partner = [(t, t ^ 1) for t in range(tok_count)]
        swapped = lax.ppermute(picked, "tok", perm=partner)
        shared = jnp.concatenate([picked, swapped], axis=0)

    with jax.named_scope("attention"):
        query_normed = norm_heads(queries, q_gain, heads_here)
        suf_keys = norm_heads(
            lax.dynamic_slice_in_dim(suffix_kv, kv_first * HD, HD, 1), k_gain, 1
        )
        suf_vals = lax.dynamic_slice_in_dim(suffix_kv, kv_width + kv_first * HD, HD, 1)
        all_keys = jnp.concatenate([shared[:, :HD], suf_keys], axis=0)
        all_vals = jnp.concatenate([shared[:, HD:], suf_vals], axis=0)
        seg_ends = jnp.cumsum(lengths[0])
        positions = jnp.arange(row_count, dtype=jnp.int32)
        segment = jnp.sum((positions[:, None] >= seg_ends[None, :]).astype(jnp.int32), axis=1)
        causal = (segment[:, None] == segment[None, :]) & (positions[None, :] <= positions[:, None])
        visible = jnp.concatenate(
            [jnp.ones((row_count, shared.shape[0]), jnp.bool_), causal], axis=1
        )
        outputs = []
        for head_idx in range(heads_here):
            head_q = query_normed[:, head_idx * HD:(head_idx + 1) * HD]
            scores = jnp.dot(head_q, all_keys.T, preferred_element_type=jnp.float32) * HD ** (-0.5)
            scores = jnp.where(visible, scores, MASKED)
            row_max = jnp.max(scores, axis=-1, keepdims=True)
            weights = jnp.exp(scores - row_max)
            row_sum = jnp.sum(weights, axis=-1, keepdims=True)
            head_out = jnp.dot(
                weights.astype(jnp.bfloat16), all_vals, preferred_element_type=jnp.float32
            ) / row_sum
            outputs.append(head_out)
        attention = jnp.concatenate(outputs, axis=1).astype(jnp.bfloat16)

    share = row_count // tok_count
    first_row = tok_index * share
    with jax.named_scope("out_projection"):
        projected = project_over_tok(attention, w_out_all, tok_count, 1)
        mixed_rows = residual.astype(jnp.float32) + rms_scale(projected, attn_gain)
        normed = rms_scale(mixed_rows, ffn_in_gain).astype(jnp.bfloat16)
        mixed_share = lax.dynamic_slice_in_dim(mixed_rows, first_row, share, 0)
    with jax.named_scope("feed_forward"):
        normed = lax.optimization_barrier(normed)
        gate = jnp.dot(normed, w_gate, preferred_element_type=jnp.float32)
        upward = jnp.dot(normed, w_up, preferred_element_type=jnp.float32)
        hidden = (jax.nn.gelu(gate, approximate=True) * upward).astype(jnp.bfloat16)
        hidden = lax.optimization_barrier(hidden)
        down_share = scatter_over_tok(
            jnp.dot(hidden, w_down, preferred_element_type=jnp.float32), tok_count, 2
        )
    return (mixed_share + rms_scale(down_share.astype(jnp.float32), ffn_out_gain)).astype(
        jnp.bfloat16
    )


def solution(mesh):
    in_specs = (
        P("req", "tok"),
        P("req", None),
        P("req", None),
        P(),
        P(),
        P("req", None),
        P(),
        P(),
        P("req", None),
        P("tok", None),
        P(),
        P(),
        P(),
        P(None, "tok"),
        P(None, "tok"),
        P("tok", None),
    )
    out_specs = P(("req", "tok"), None)
    return jax.shard_map(local, mesh=mesh, in_specs=in_specs, out_specs=out_specs, check_vma=False)
```

```python
import jax
import jax.numpy as jnp
from jax import lax
from jax.sharding import PartitionSpec as P
from jax.experimental import pallas as pl
from jax.experimental.pallas import tpu as pltpu

H = 8
KVH = 4
HD = 256
GROUPS = 2


EPSILON = 1e-06
MASKED = -1e30


def rms_scale(values_in, gain_vec):
    return (
        values_in
        * lax.rsqrt(jnp.mean(values_in * values_in, axis=-1, keepdims=True) + EPSILON)
        * gain_vec
    )


def norm_heads(values_in, gain_vec, head_count):
    row_count = values_in.shape[0]
    shaped = values_in.astype(jnp.float32).reshape(row_count, head_count, HD)
    return rms_scale(shaped, gain_vec).astype(jnp.bfloat16).reshape(row_count, head_count * HD)


def gather_tok_kernel(tok_count, w_ref, out_ref, send_sem, recv_sem, local_sem):
    mesh_ids = pl.DeviceIdType.MESH
    me = lax.axis_index("tok")
    up = lax.rem(me + 2, tok_count)
    down = lax.rem(me + tok_count - 2, tok_count)
    far = lax.rem(me + 4, tok_count)
    partner = me + 1 - 2 * lax.rem(me, 2)
    half = w_ref.shape[0] // 2

    barrier = pltpu.get_barrier_semaphore()
    for peer in (up, down, partner):
        pl.semaphore_signal(barrier, inc=1, device_id={"tok": peer}, device_id_type=mesh_ids)
    pl.semaphore_wait(barrier, 3)

    def remote(src, dst, slot, peer):
        return pltpu.make_async_remote_copy(
            src_ref=src,
            dst_ref=dst,
            send_sem=send_sem.at[slot],
            recv_sem=recv_sem.at[slot],
            device_id={"tok": peer},
            device_id_type=mesh_ids,
        )

    local = pltpu.make_async_copy(w_ref, out_ref.at[me], local_sem.at[0])
    local.start()
    sends = []

    def send(src, dst, slot, peer):
        copy = remote(src, dst, slot, peer)
        copy.start()
        sends.append(copy)

    send(w_ref, out_ref.at[me], 0, up)
    send(w_ref, out_ref.at[me], 1, down)
    send(w_ref, out_ref.at[me], 4, partner)
    remote(w_ref, out_ref.at[down], 0, down).wait_recv()
    remote(w_ref, out_ref.at[up], 1, up).wait_recv()

    first = pl.ds(0, half)
    second = pl.ds(half, half)
    send(out_ref.at[down, first], out_ref.at[down, first], 2, up)
    send(out_ref.at[up, second], out_ref.at[up, second], 3, down)
    send(out_ref.at[up], out_ref.at[up], 5, partner)
    send(out_ref.at[down], out_ref.at[down], 6, partner)
    remote(out_ref.at[far, first], out_ref.at[far, first], 2, down).wait_recv()
    remote(out_ref.at[far, second], out_ref.at[far, second], 3, up).wait_recv()
    send(out_ref.at[far], out_ref.at[far], 7, partner)
    local.wait()

    theirs = (
        partner,
        lax.rem(partner + 2, tok_count),
        lax.rem(partner + tok_count - 2, tok_count),
        lax.rem(partner + 4, tok_count),
    )
    for idx, slot in enumerate(theirs):
        remote(out_ref.at[slot], out_ref.at[slot], 4 + idx, partner).wait_recv()
    for copy in sends:
        copy.wait_send()


def gather_over_tok(block, tok_count, collective_id):
    assert tok_count == 8
    rows, cols = block.shape
    return pl.pallas_call(
        lambda *refs: gather_tok_kernel(tok_count, *refs),
        out_shape=jax.ShapeDtypeStruct((tok_count, rows, cols), block.dtype),
        in_specs=[pl.BlockSpec(memory_space=pl.ANY)],
        out_specs=pl.BlockSpec(memory_space=pl.ANY),
        scratch_shapes=[
            pltpu.SemaphoreType.DMA((8,)),
            pltpu.SemaphoreType.DMA((8,)),
            pltpu.SemaphoreType.DMA((1,)),
        ],
        compiler_params=pltpu.CompilerParams(collective_id=collective_id, has_side_effects=True),
        cost_estimate=pl.CostEstimate(
            flops=0, transcendentals=0, bytes_accessed=2 * tok_count * rows * cols * 2
        ),
    )(block)


def project_tok_kernel(
    tok_count, att_ref, w_hbm, out_ref, att_all, w_buf, send_sem, recv_sem, load_sem
):
    mesh_ids = pl.DeviceIdType.MESH
    me = lax.axis_index("tok")
    up = lax.rem(me + 2, tok_count)
    down = lax.rem(me + tok_count - 2, tok_count)
    far = lax.rem(me + 4, tok_count)
    partner = me + 1 - 2 * lax.rem(me, 2)
    half = att_ref.shape[0] // 2
    cols = out_ref.shape[1]
    tile = 512
    tiles = cols // tile

    barrier = pltpu.get_barrier_semaphore()
    for peer in (up, down, partner):
        pl.semaphore_signal(barrier, inc=1, device_id={"tok": peer}, device_id_type=mesh_ids)
    pl.semaphore_wait(barrier, 3)

    def remote(src, dst, slot, peer):
        return pltpu.make_async_remote_copy(
            src_ref=src,
            dst_ref=dst,
            send_sem=send_sem.at[slot],
            recv_sem=recv_sem.at[slot],
            device_id={"tok": peer},
            device_id_type=mesh_ids,
        )

    theirs = (
        partner,
        lax.rem(partner + 2, tok_count),
        lax.rem(partner + tok_count - 2, tok_count),
        lax.rem(partner + 4, tok_count),
    )
    order = (me, down, up, theirs[0], far) + theirs[1:]

    def load(idx):
        return pltpu.make_async_copy(w_hbm.at[order[idx]], w_buf.at[idx % 2], load_sem.at[idx % 2])

    def accumulate(idx, source, first):
        load(idx).wait()
        if idx + 1 < len(order):
            load(idx + 1).start()
        weights = w_buf.at[idx % 2]

        def one_tile(col):
            span = pl.ds(pl.multiple_of(col * tile, tile), tile)
            term = jnp.dot(source[...], weights[:, span], preferred_element_type=jnp.float32)
            if first:
                out_ref[:, span] = term
            else:
                out_ref[:, span] = out_ref[:, span] + term

        pl.loop(0, tiles)(one_tile)

    load(0).start()
    sends = []

    def send(src, slot, index, peer):
        copy = remote(src, att_all.at[slot], index, peer)
        copy.start()
        sends.append(copy)

    def arrived(slot, index, peer, rows=None):
        dst = att_all.at[slot] if rows is None else att_all.at[slot, rows]
        remote(dst, dst, index, peer).wait_recv()

    first = pl.ds(0, half)
    second = pl.ds(half, half)
    send(att_ref, me, 0, up)
    send(att_ref, me, 1, down)
    send(att_ref, me, 4, partner)
    accumulate(0, att_ref, True)
    arrived(down, 0, down)
    arrived(up, 1, up)
    for src, index, peer in ((att_all.at[down, first], 2, up), (att_all.at[up, second], 3, down)):
        copy = remote(src, src, index, peer)
        copy.start()
        sends.append(copy)
    send(att_all.at[up], up, 5, partner)
    send(att_all.at[down], down, 6, partner)
    accumulate(1, att_all.at[down], False)
    accumulate(2, att_all.at[up], False)
    arrived(theirs[0], 4, partner)
    accumulate(3, att_all.at[theirs[0]], False)
    arrived(far, 2, down, first)
    arrived(far, 3, up, second)
    send(att_all.at[far], far, 7, partner)
    accumulate(4, att_all.at[far], False)
    for idx in range(1, 4):
        arrived(theirs[idx], 4 + idx, partner)
        accumulate(4 + idx, att_all.at[theirs[idx]], False)
    for copy in sends:
        copy.wait_send()


def project_over_tok(attention, w_all, tok_count, collective_id):
    assert tok_count == 8
    rows, width = attention.shape
    cols = w_all.shape[2]
    vmem = pltpu.MemorySpace.VMEM
    return pl.pallas_call(
        lambda *refs: project_tok_kernel(tok_count, *refs),
        out_shape=jax.ShapeDtypeStruct((rows, cols), jnp.float32),
        in_specs=[pl.BlockSpec(memory_space=vmem), pl.BlockSpec(memory_space=pl.ANY)],
        out_specs=pl.BlockSpec(memory_space=vmem),
        scratch_shapes=[
            pltpu.VMEM((tok_count, rows, width), attention.dtype),
            pltpu.VMEM((2, width, cols), w_all.dtype),
            pltpu.SemaphoreType.DMA((8,)),
            pltpu.SemaphoreType.DMA((8,)),
            pltpu.SemaphoreType.DMA((2,)),
        ],
        compiler_params=pltpu.CompilerParams(
            collective_id=collective_id, has_side_effects=True, vmem_limit_bytes=48 * 1024 * 1024
        ),
        cost_estimate=pl.CostEstimate(
            flops=2 * rows * width * tok_count * cols,
            transcendentals=0,
            bytes_accessed=tok_count * width * cols * 2 + rows * cols * 4,
        ),
    )(attention, w_all)


def scatter_tok_kernel(
    tok_count, part_hbm, out_ref, mine, chip_in, cross_out, cross_in, load_sem, send_sem, recv_sem
):
    mesh_ids = pl.DeviceIdType.MESH
    me = lax.axis_index("tok")
    up = lax.rem(me + 2, tok_count)
    down = lax.rem(me + tok_count - 2, tok_count)
    far = lax.rem(me + 4, tok_count)
    partner = me + 1 - 2 * lax.rem(me, 2)
    share = out_ref.shape[0]

    barrier = pltpu.get_barrier_semaphore()
    for peer in (up, down, far, partner):
        pl.semaphore_signal(barrier, inc=1, device_id={"tok": peer}, device_id_type=mesh_ids)
    pl.semaphore_wait(barrier, 4)

    def remote(src, dst, slot, peer):
        return pltpu.make_async_remote_copy(
            src_ref=src,
            dst_ref=dst,
            send_sem=send_sem.at[slot],
            recv_sem=recv_sem.at[slot],
            device_id={"tok": peer},
            device_id_type=mesh_ids,
        )

    def family(base):
        return (
            base,
            lax.rem(base + 2, tok_count),
            lax.rem(base + tok_count - 2, tok_count),
            lax.rem(base + 4, tok_count),
        )

    def rows_of(block):
        return pl.ds(pl.multiple_of(block * share, share), share)

    order = (3, 1, 2, 0)
    sends = []
    theirs = family(partner)
    for idx in order:
        copy = remote(part_hbm.at[rows_of(theirs[idx])], chip_in.at[idx], idx, partner)
        copy.start()
        sends.append(copy)
    own = family(me)
    loads = []
    for idx in order:
        load = pltpu.make_async_copy(part_hbm.at[rows_of(own[idx])], mine.at[idx], load_sem.at[idx])
        load.start()
        loads.append(load)
    targets = {1: (up, 1), 2: (down, 0), 3: (far, 2)}
    for pos, idx in enumerate(order[:3]):
        loads[pos].wait()
        remote(part_hbm.at[rows_of(own[idx])], chip_in.at[idx], idx, partner).wait_recv()
        cross_out[idx - 1] = (mine[idx] + chip_in[idx]).astype(cross_out.dtype)
        peer, dst_idx = targets[idx]
        copy = remote(cross_out.at[idx - 1], cross_in.at[dst_idx], 4 + dst_idx, peer)
        copy.start()
        sends.append(copy)
    loads[3].wait()
    remote(part_hbm.at[rows_of(own[0])], chip_in.at[0], 0, partner).wait_recv()
    total = mine[0] + chip_in[0]
    for idx, peer in ((0, up), (1, down), (2, far)):
        remote(cross_out.at[idx], cross_in.at[idx], 4 + idx, peer).wait_recv()
    for idx in range(3):
        total = total + cross_in[idx].astype(jnp.float32)
    out_ref[...] = total
    for copy in sends:
        copy.wait_send()


def scatter_over_tok(partial, tok_count, collective_id):
    assert tok_count == 8
    rows, cols = partial.shape
    share = rows // tok_count
    vmem = pltpu.MemorySpace.VMEM
    return pl.pallas_call(
        lambda *refs: scatter_tok_kernel(tok_count, *refs),
        out_shape=jax.ShapeDtypeStruct((share, cols), jnp.float32),
        in_specs=[pl.BlockSpec(memory_space=pltpu.MemorySpace.HBM)],
        out_specs=pl.BlockSpec(memory_space=vmem),
        scratch_shapes=[
            pltpu.VMEM((4, share, cols), jnp.float32),
            pltpu.VMEM((4, share, cols), jnp.float32),
            pltpu.VMEM((3, share, cols), jnp.bfloat16),
            pltpu.VMEM((3, share, cols), jnp.bfloat16),
            pltpu.SemaphoreType.DMA((4,)),
            pltpu.SemaphoreType.DMA((7,)),
            pltpu.SemaphoreType.DMA((7,)),
        ],
        compiler_params=pltpu.CompilerParams(
            collective_id=collective_id, has_side_effects=True, vmem_limit_bytes=48 * 1024 * 1024
        ),
        cost_estimate=pl.CostEstimate(
            flops=8 * share * cols, transcendentals=0, bytes_accessed=rows * cols * 4 * 2
        ),
    )(partial)


def local(
    queries,
    suffix_kv,
    prefix_cache,
    q_gain,
    k_gain,
    lengths,
    group_of,
    owner_order,
    residual,
    w_out,
    attn_gain,
    ffn_in_gain,
    ffn_out_gain,
    w_gate,
    w_up,
    w_down,
):
    req_count = lax.axis_size("req")
    tok_count = lax.axis_size("tok")
    req_index = lax.axis_index("req")
    tok_index = lax.axis_index("tok")
    row_count = queries.shape[0]
    heads_here = queries.shape[1] // HD
    head_ratio = H // KVH
    kv_first = tok_index * heads_here // head_ratio
    kv_width = KVH * HD
    own_count = req_count // GROUPS

    with jax.named_scope("prefix_gather"):
        pref_keys = lax.dynamic_slice_in_dim(prefix_cache, kv_first * HD, HD, 1)
        pref_vals = lax.dynamic_slice_in_dim(prefix_cache, kv_width + kv_first * HD, HD, 1)
        pref_kv = jnp.concatenate([pref_keys, pref_vals], axis=1)
        half_rows = pref_kv.shape[0] // 2
        core = tok_index % 2
        my_half = lax.dynamic_slice_in_dim(pref_kv, core * half_rows, half_rows, 0)
        gathered = lax.all_gather(my_half, "req", axis=0, tiled=False)
        w_out_all = gather_over_tok(w_out, tok_count, 0)
        gathered, w_out_all = lax.optimization_barrier((gathered, w_out_all))
        own_group = group_of[req_index]
        owner_ids = lax.dynamic_slice_in_dim(owner_order, own_group * own_count, own_count)
        picked = jnp.take(gathered, owner_ids, axis=0, mode="clip").reshape(-1, 2 * HD)
        partner = [(t, t ^ 1) for t in range(tok_count)]
        swapped = lax.ppermute(picked, "tok", perm=partner)
        shared = jnp.concatenate([picked, swapped], axis=0)

    with jax.named_scope("attention"):
        query_normed = norm_heads(queries, q_gain, heads_here)
        suf_keys = norm_heads(
            lax.dynamic_slice_in_dim(suffix_kv, kv_first * HD, HD, 1), k_gain, 1
        )
        suf_vals = lax.dynamic_slice_in_dim(suffix_kv, kv_width + kv_first * HD, HD, 1)
        all_keys = jnp.concatenate([shared[:, :HD], suf_keys], axis=0)
        all_vals = jnp.concatenate([shared[:, HD:], suf_vals], axis=0)
        seg_ends = jnp.cumsum(lengths[0])
        positions = jnp.arange(row_count, dtype=jnp.int32)
        segment = jnp.sum((positions[:, None] >= seg_ends[None, :]).astype(jnp.int32), axis=1)
        causal = (segment[:, None] == segment[None, :]) & (positions[None, :] <= positions[:, None])
        visible = jnp.concatenate(
            [jnp.ones((row_count, shared.shape[0]), jnp.bool_), causal], axis=1
        )
        outputs = []
        for head_idx in range(heads_here):
            head_q = query_normed[:, head_idx * HD:(head_idx + 1) * HD]
            scores = jnp.dot(head_q, all_keys.T, preferred_element_type=jnp.float32) * HD ** (-0.5)
            scores = jnp.where(visible, scores, MASKED)
            row_max = jnp.max(scores, axis=-1, keepdims=True)
            weights = jnp.exp(scores - row_max)
            row_sum = jnp.sum(weights, axis=-1, keepdims=True)
            head_out = jnp.dot(
                weights.astype(jnp.bfloat16), all_vals, preferred_element_type=jnp.float32
            ) / row_sum
            outputs.append(head_out)
        attention = jnp.concatenate(outputs, axis=1).astype(jnp.bfloat16)

    share = row_count // tok_count
    first_row = tok_index * share
    with jax.named_scope("out_projection"):
        projected = project_over_tok(attention, w_out_all, tok_count, 1)
        mixed_rows = residual.astype(jnp.float32) + rms_scale(projected, attn_gain)
        normed = rms_scale(mixed_rows, ffn_in_gain).astype(jnp.bfloat16)
        mixed_share = lax.dynamic_slice_in_dim(mixed_rows, first_row, share, 0)
    with jax.named_scope("feed_forward"):
        normed = lax.optimization_barrier(normed)
        gate = jnp.dot(normed, w_gate, preferred_element_type=jnp.float32)
        upward = jnp.dot(normed, w_up, preferred_element_type=jnp.float32)
        hidden = (jax.nn.gelu(gate, approximate=True) * upward).astype(jnp.bfloat16)
        hidden = lax.optimization_barrier(hidden)
        down_share = scatter_over_tok(
            jnp.dot(hidden, w_down, preferred_element_type=jnp.float32), tok_count, 2
        )
    return (mixed_share + rms_scale(down_share.astype(jnp.float32), ffn_out_gain)).astype(
        jnp.bfloat16
    )


def solution(mesh):
    in_specs = (
        P("req", "tok"),
        P("req", None),
        P("req", None),
        P(),
        P(),
        P("req", None),
        P(),
        P(),
        P("req", None),
        P("tok", None),
        P(),
        P(),
        P(),
        P(None, "tok"),
        P(None, "tok"),
        P("tok", None),
    )
    out_specs = P(("req", "tok"), None)
    return jax.shard_map(local, mesh=mesh, in_specs=in_specs, out_specs=out_specs, check_vma=False)
```

```python
import jax
import jax.numpy as jnp
from jax import lax
from jax.sharding import PartitionSpec as P
from jax.experimental import pallas as pl
from jax.experimental.pallas import tpu as pltpu

H = 8
KVH = 4
HD = 256
GROUPS = 2


EPSILON = 1e-06
MASKED = -1e30


def rms_scale(values_in, gain_vec):
    return (
        values_in
        * lax.rsqrt(jnp.mean(values_in * values_in, axis=-1, keepdims=True) + EPSILON)
        * gain_vec
    )


def norm_heads(values_in, gain_vec, head_count):
    row_count = values_in.shape[0]
    shaped = values_in.astype(jnp.float32).reshape(row_count, head_count, HD)
    return rms_scale(shaped, gain_vec).astype(jnp.bfloat16).reshape(row_count, head_count * HD)


def gather_tok_kernel(tok_count, w_ref, out_ref, send_sem, recv_sem, local_sem):
    mesh_ids = pl.DeviceIdType.MESH
    me = lax.axis_index("tok")
    up = lax.rem(me + 2, tok_count)
    down = lax.rem(me + tok_count - 2, tok_count)
    far = lax.rem(me + 4, tok_count)
    partner = me + 1 - 2 * lax.rem(me, 2)
    half = w_ref.shape[0] // 2

    barrier = pltpu.get_barrier_semaphore()
    for peer in (up, down, partner):
        pl.semaphore_signal(barrier, inc=1, device_id={"tok": peer}, device_id_type=mesh_ids)
    pl.semaphore_wait(barrier, 3)

    def remote(src, dst, slot, peer):
        return pltpu.make_async_remote_copy(
            src_ref=src,
            dst_ref=dst,
            send_sem=send_sem.at[slot],
            recv_sem=recv_sem.at[slot],
            device_id={"tok": peer},
            device_id_type=mesh_ids,
        )

    local = pltpu.make_async_copy(w_ref, out_ref.at[me], local_sem.at[0])
    local.start()
    sends = []

    def send(src, dst, slot, peer):
        copy = remote(src, dst, slot, peer)
        copy.start()
        sends.append(copy)

    send(w_ref, out_ref.at[me], 0, up)
    send(w_ref, out_ref.at[me], 1, down)
    send(w_ref, out_ref.at[me], 4, partner)
    remote(w_ref, out_ref.at[down], 0, down).wait_recv()
    remote(w_ref, out_ref.at[up], 1, up).wait_recv()

    first = pl.ds(0, half)
    second = pl.ds(half, half)
    send(out_ref.at[down, first], out_ref.at[down, first], 2, up)
    send(out_ref.at[up, second], out_ref.at[up, second], 3, down)
    send(out_ref.at[up], out_ref.at[up], 5, partner)
    send(out_ref.at[down], out_ref.at[down], 6, partner)
    remote(out_ref.at[far, first], out_ref.at[far, first], 2, down).wait_recv()
    remote(out_ref.at[far, second], out_ref.at[far, second], 3, up).wait_recv()
    send(out_ref.at[far], out_ref.at[far], 7, partner)
    local.wait()

    theirs = (
        partner,
        lax.rem(partner + 2, tok_count),
        lax.rem(partner + tok_count - 2, tok_count),
        lax.rem(partner + 4, tok_count),
    )
    for idx, slot in enumerate(theirs):
        remote(out_ref.at[slot], out_ref.at[slot], 4 + idx, partner).wait_recv()
    for copy in sends:
        copy.wait_send()


def gather_over_tok(block, tok_count, collective_id):
    assert tok_count == 8
    rows, cols = block.shape
    return pl.pallas_call(
        lambda *refs: gather_tok_kernel(tok_count, *refs),
        out_shape=jax.ShapeDtypeStruct((tok_count, rows, cols), block.dtype),
        in_specs=[pl.BlockSpec(memory_space=pl.ANY)],
        out_specs=pl.BlockSpec(memory_space=pl.ANY),
        scratch_shapes=[
            pltpu.SemaphoreType.DMA((8,)),
            pltpu.SemaphoreType.DMA((8,)),
            pltpu.SemaphoreType.DMA((1,)),
        ],
        compiler_params=pltpu.CompilerParams(collective_id=collective_id, has_side_effects=True),
        cost_estimate=pl.CostEstimate(
            flops=0, transcendentals=0, bytes_accessed=2 * tok_count * rows * cols * 2
        ),
    )(block)


def project_tok_kernel(
    tok_count, att_ref, w_hbm, out_ref, att_all, w_buf, send_sem, recv_sem, load_sem
):
    mesh_ids = pl.DeviceIdType.MESH
    me = lax.axis_index("tok")
    up = lax.rem(me + 2, tok_count)
    down = lax.rem(me + tok_count - 2, tok_count)
    far = lax.rem(me + 4, tok_count)
    partner = me + 1 - 2 * lax.rem(me, 2)
    half = att_ref.shape[0] // 2
    cols = out_ref.shape[1]
    tile = 512
    tiles = cols // tile

    barrier = pltpu.get_barrier_semaphore()
    for peer in (up, down, partner):
        pl.semaphore_signal(barrier, inc=1, device_id={"tok": peer}, device_id_type=mesh_ids)
    pl.semaphore_wait(barrier, 3)

    def remote(src, dst, slot, peer):
        return pltpu.make_async_remote_copy(
            src_ref=src,
            dst_ref=dst,
            send_sem=send_sem.at[slot],
            recv_sem=recv_sem.at[slot],
            device_id={"tok": peer},
            device_id_type=mesh_ids,
        )

    theirs = (
        partner,
        lax.rem(partner + 2, tok_count),
        lax.rem(partner + tok_count - 2, tok_count),
        lax.rem(partner + 4, tok_count),
    )
    order = (me, down, up, theirs[0], far) + theirs[1:]

    def load(idx):
        return pltpu.make_async_copy(w_hbm.at[order[idx]], w_buf.at[idx % 2], load_sem.at[idx % 2])

    def accumulate(idx, source, first):
        load(idx).wait()
        if idx + 1 < len(order):
            load(idx + 1).start()
        weights = w_buf.at[idx % 2]

        def one_tile(col):
            span = pl.ds(pl.multiple_of(col * tile, tile), tile)
            term = jnp.dot(source[...], weights[:, span], preferred_element_type=jnp.float32)
            if first:
                out_ref[:, span] = term
            else:
                out_ref[:, span] = out_ref[:, span] + term

        pl.loop(0, tiles)(one_tile)

    load(0).start()
    sends = []

    def send(src, slot, index, peer):
        copy = remote(src, att_all.at[slot], index, peer)
        copy.start()
        sends.append(copy)

    def arrived(slot, index, peer, rows=None):
        dst = att_all.at[slot] if rows is None else att_all.at[slot, rows]
        remote(dst, dst, index, peer).wait_recv()

    first = pl.ds(0, half)
    second = pl.ds(half, half)
    send(att_ref, me, 0, up)
    send(att_ref, me, 1, down)
    send(att_ref, me, 4, partner)
    accumulate(0, att_ref, True)
    arrived(down, 0, down)
    arrived(up, 1, up)
    for src, index, peer in ((att_all.at[down, first], 2, up), (att_all.at[up, second], 3, down)):
        copy = remote(src, src, index, peer)
        copy.start()
        sends.append(copy)
    send(att_all.at[up], up, 5, partner)
    send(att_all.at[down], down, 6, partner)
    accumulate(1, att_all.at[down], False)
    accumulate(2, att_all.at[up], False)
    arrived(theirs[0], 4, partner)
    accumulate(3, att_all.at[theirs[0]], False)
    arrived(far, 2, down, first)
    arrived(far, 3, up, second)
    send(att_all.at[far], far, 7, partner)
    accumulate(4, att_all.at[far], False)
    for idx in range(1, 4):
        arrived(theirs[idx], 4 + idx, partner)
        accumulate(4 + idx, att_all.at[theirs[idx]], False)
    for copy in sends:
        copy.wait_send()


def project_over_tok(attention, w_all, tok_count, collective_id):
    assert tok_count == 8
    rows, width = attention.shape
    cols = w_all.shape[2]
    vmem = pltpu.MemorySpace.VMEM
    return pl.pallas_call(
        lambda *refs: project_tok_kernel(tok_count, *refs),
        out_shape=jax.ShapeDtypeStruct((rows, cols), jnp.float32),
        in_specs=[pl.BlockSpec(memory_space=vmem), pl.BlockSpec(memory_space=pl.ANY)],
        out_specs=pl.BlockSpec(memory_space=vmem),
        scratch_shapes=[
            pltpu.VMEM((tok_count, rows, width), attention.dtype),
            pltpu.VMEM((2, width, cols), w_all.dtype),
            pltpu.SemaphoreType.DMA((8,)),
            pltpu.SemaphoreType.DMA((8,)),
            pltpu.SemaphoreType.DMA((2,)),
        ],
        compiler_params=pltpu.CompilerParams(
            collective_id=collective_id, has_side_effects=True, vmem_limit_bytes=48 * 1024 * 1024
        ),
        cost_estimate=pl.CostEstimate(
            flops=2 * rows * width * tok_count * cols,
            transcendentals=0,
            bytes_accessed=tok_count * width * cols * 2 + rows * cols * 4,
        ),
    )(attention, w_all)


def scatter_tok_kernel(
    tok_count, part_hbm, out_ref, mine, theirs_buf, chip_in, cross_out, cross_in, load_sem, send_sem, recv_sem
):
    mesh_ids = pl.DeviceIdType.MESH
    me = lax.axis_index("tok")
    up = lax.rem(me + 2, tok_count)
    down = lax.rem(me + tok_count - 2, tok_count)
    far = lax.rem(me + 4, tok_count)
    partner = me + 1 - 2 * lax.rem(me, 2)
    share = out_ref.shape[0]

    barrier = pltpu.get_barrier_semaphore()
    for peer in (up, down, far, partner):
        pl.semaphore_signal(barrier, inc=1, device_id={"tok": peer}, device_id_type=mesh_ids)
    pl.semaphore_wait(barrier, 4)

    def remote(src, dst, slot, peer):
        return pltpu.make_async_remote_copy(
            src_ref=src,
            dst_ref=dst,
            send_sem=send_sem.at[slot],
            recv_sem=recv_sem.at[slot],
            device_id={"tok": peer},
            device_id_type=mesh_ids,
        )

    def family(base):
        return (
            base,
            lax.rem(base + 2, tok_count),
            lax.rem(base + tok_count - 2, tok_count),
            lax.rem(base + 4, tok_count),
        )

    def rows_of(block):
        return pl.ds(pl.multiple_of(block * share, share), share)

    order = (3, 1, 2, 0)
    sends = []
    theirs = family(partner)
    staged = []
    for idx in order:
        load = pltpu.make_async_copy(
            part_hbm.at[rows_of(theirs[idx])], theirs_buf.at[idx], load_sem.at[4 + idx]
        )
        load.start()
        staged.append(load)
    own = family(me)
    for pos, idx in enumerate(order):
        staged[pos].wait()
        cross_out[3 + idx] = theirs_buf[idx].astype(cross_out.dtype)
        copy = remote(cross_out.at[3 + idx], chip_in.at[idx], idx, partner)
        copy.start()
        sends.append(copy)
    loads = []
    for idx in order:
        load = pltpu.make_async_copy(part_hbm.at[rows_of(own[idx])], mine.at[idx], load_sem.at[idx])
        load.start()
        loads.append(load)
    targets = {1: (up, 1), 2: (down, 0), 3: (far, 2)}
    for pos, idx in enumerate(order[:3]):
        loads[pos].wait()
        remote(cross_out.at[3 + idx], chip_in.at[idx], idx, partner).wait_recv()
        cross_out[idx - 1] = (mine[idx] + chip_in[idx].astype(jnp.float32)).astype(cross_out.dtype)
        peer, dst_idx = targets[idx]
        copy = remote(cross_out.at[idx - 1], cross_in.at[dst_idx], 4 + dst_idx, peer)
        copy.start()
        sends.append(copy)
    loads[3].wait()
    remote(cross_out.at[3], chip_in.at[0], 0, partner).wait_recv()
    total = mine[0] + chip_in[0].astype(jnp.float32)
    for idx, peer in ((0, up), (1, down), (2, far)):
        remote(cross_out.at[idx], cross_in.at[idx], 4 + idx, peer).wait_recv()
    for idx in range(3):
        total = total + cross_in[idx].astype(jnp.float32)
    out_ref[...] = total
    for copy in sends:
        copy.wait_send()


def scatter_over_tok(partial, tok_count, collective_id):
    assert tok_count == 8
    rows, cols = partial.shape
    share = rows // tok_count
    vmem = pltpu.MemorySpace.VMEM
    return pl.pallas_call(
        lambda *refs: scatter_tok_kernel(tok_count, *refs),
        out_shape=jax.ShapeDtypeStruct((share, cols), jnp.float32),
        in_specs=[pl.BlockSpec(memory_space=pltpu.MemorySpace.HBM)],
        out_specs=pl.BlockSpec(memory_space=vmem),
        scratch_shapes=[
            pltpu.VMEM((4, share, cols), jnp.float32),
            pltpu.VMEM((4, share, cols), jnp.float32),
            pltpu.VMEM((4, share, cols), jnp.bfloat16),
            pltpu.VMEM((7, share, cols), jnp.bfloat16),
            pltpu.VMEM((3, share, cols), jnp.bfloat16),
            pltpu.SemaphoreType.DMA((8,)),
            pltpu.SemaphoreType.DMA((7,)),
            pltpu.SemaphoreType.DMA((7,)),
        ],
        compiler_params=pltpu.CompilerParams(
            collective_id=collective_id, has_side_effects=True, vmem_limit_bytes=48 * 1024 * 1024
        ),
        cost_estimate=pl.CostEstimate(
            flops=8 * share * cols, transcendentals=0, bytes_accessed=rows * cols * 4 * 2
        ),
    )(partial)


def local(
    queries,
    suffix_kv,
    prefix_cache,
    q_gain,
    k_gain,
    lengths,
    group_of,
    owner_order,
    residual,
    w_out,
    attn_gain,
    ffn_in_gain,
    ffn_out_gain,
    w_gate,
    w_up,
    w_down,
):
    req_count = lax.axis_size("req")
    tok_count = lax.axis_size("tok")
    req_index = lax.axis_index("req")
    tok_index = lax.axis_index("tok")
    row_count = queries.shape[0]
    heads_here = queries.shape[1] // HD
    head_ratio = H // KVH
    kv_first = tok_index * heads_here // head_ratio
    kv_width = KVH * HD
    own_count = req_count // GROUPS

    with jax.named_scope("prefix_gather"):
        pref_keys = lax.dynamic_slice_in_dim(prefix_cache, kv_first * HD, HD, 1)
        pref_vals = lax.dynamic_slice_in_dim(prefix_cache, kv_width + kv_first * HD, HD, 1)
        pref_kv = jnp.concatenate([pref_keys, pref_vals], axis=1)
        half_rows = pref_kv.shape[0] // 2
        core = tok_index % 2
        my_half = lax.dynamic_slice_in_dim(pref_kv, core * half_rows, half_rows, 0)
        gathered = lax.all_gather(my_half, "req", axis=0, tiled=False)
        w_out_all = gather_over_tok(w_out, tok_count, 0)
        gathered, w_out_all = lax.optimization_barrier((gathered, w_out_all))
        own_group = group_of[req_index]
        owner_ids = lax.dynamic_slice_in_dim(owner_order, own_group * own_count, own_count)
        picked = jnp.take(gathered, owner_ids, axis=0, mode="clip").reshape(-1, 2 * HD)
        partner = [(t, t ^ 1) for t in range(tok_count)]
        swapped = lax.ppermute(picked, "tok", perm=partner)
        shared = jnp.concatenate([picked, swapped], axis=0)

    with jax.named_scope("attention"):
        query_normed = norm_heads(queries, q_gain, heads_here)
        suf_keys = norm_heads(
            lax.dynamic_slice_in_dim(suffix_kv, kv_first * HD, HD, 1), k_gain, 1
        )
        suf_vals = lax.dynamic_slice_in_dim(suffix_kv, kv_width + kv_first * HD, HD, 1)
        all_keys = jnp.concatenate([shared[:, :HD], suf_keys], axis=0)
        all_vals = jnp.concatenate([shared[:, HD:], suf_vals], axis=0)
        seg_ends = jnp.cumsum(lengths[0])
        positions = jnp.arange(row_count, dtype=jnp.int32)
        segment = jnp.sum((positions[:, None] >= seg_ends[None, :]).astype(jnp.int32), axis=1)
        causal = (segment[:, None] == segment[None, :]) & (positions[None, :] <= positions[:, None])
        visible = jnp.concatenate(
            [jnp.ones((row_count, shared.shape[0]), jnp.bool_), causal], axis=1
        )
        outputs = []
        for head_idx in range(heads_here):
            head_q = query_normed[:, head_idx * HD:(head_idx + 1) * HD]
            scores = jnp.dot(head_q, all_keys.T, preferred_element_type=jnp.float32) * HD ** (-0.5)
            scores = jnp.where(visible, scores, MASKED)
            row_max = jnp.max(scores, axis=-1, keepdims=True)
            weights = jnp.exp(scores - row_max)
            row_sum = jnp.sum(weights, axis=-1, keepdims=True)
            head_out = jnp.dot(
                weights.astype(jnp.bfloat16), all_vals, preferred_element_type=jnp.float32
            ) / row_sum
            outputs.append(head_out)
        attention = jnp.concatenate(outputs, axis=1).astype(jnp.bfloat16)

    share = row_count // tok_count
    first_row = tok_index * share
    with jax.named_scope("out_projection"):
        projected = project_over_tok(attention, w_out_all, tok_count, 1)
        mixed_rows = residual.astype(jnp.float32) + rms_scale(projected, attn_gain)
        normed = rms_scale(mixed_rows, ffn_in_gain).astype(jnp.bfloat16)
        mixed_share = lax.dynamic_slice_in_dim(mixed_rows, first_row, share, 0)
    with jax.named_scope("feed_forward"):
        normed = lax.optimization_barrier(normed)
        gate = jnp.dot(normed, w_gate, preferred_element_type=jnp.float32)
        upward = jnp.dot(normed, w_up, preferred_element_type=jnp.float32)
        hidden = (jax.nn.gelu(gate, approximate=True) * upward).astype(jnp.bfloat16)
        hidden = lax.optimization_barrier(hidden)
        down_share = scatter_over_tok(
            jnp.dot(hidden, w_down, preferred_element_type=jnp.float32), tok_count, 2
        )
    return (mixed_share + rms_scale(down_share.astype(jnp.float32), ffn_out_gain)).astype(
        jnp.bfloat16
    )


def solution(mesh):
    in_specs = (
        P("req", "tok"),
        P("req", None),
        P("req", None),
        P(),
        P(),
        P("req", None),
        P(),
        P(),
        P("req", None),
        P("tok", None),
        P(),
        P(),
        P(),
        P(None, "tok"),
        P(None, "tok"),
        P("tok", None),
    )
    out_specs = P(("req", "tok"), None)
    return jax.shard_map(local, mesh=mesh, in_specs=in_specs, out_specs=out_specs, check_vma=False)
```

```python
import jax
import jax.numpy as jnp
from jax import lax
from jax.sharding import PartitionSpec as P
from jax.experimental import pallas as pl
from jax.experimental.pallas import tpu as pltpu

H = 8
KVH = 4
HD = 256
GROUPS = 2


EPSILON = 1e-06
MASKED = -1e30


def rms_scale(values_in, gain_vec):
    return (
        values_in
        * lax.rsqrt(jnp.mean(values_in * values_in, axis=-1, keepdims=True) + EPSILON)
        * gain_vec
    )


def norm_heads(values_in, gain_vec, head_count):
    row_count = values_in.shape[0]
    shaped = values_in.astype(jnp.float32).reshape(row_count, head_count, HD)
    return rms_scale(shaped, gain_vec).astype(jnp.bfloat16).reshape(row_count, head_count * HD)


def gather_tok_kernel(tok_count, w_ref, out_ref, send_sem, recv_sem, local_sem):
    mesh_ids = pl.DeviceIdType.MESH
    me = lax.axis_index("tok")
    up = lax.rem(me + 2, tok_count)
    down = lax.rem(me + tok_count - 2, tok_count)
    far = lax.rem(me + 4, tok_count)
    partner = me + 1 - 2 * lax.rem(me, 2)
    half = w_ref.shape[0] // 2

    barrier = pltpu.get_barrier_semaphore()
    for peer in (up, down, partner):
        pl.semaphore_signal(barrier, inc=1, device_id={"tok": peer}, device_id_type=mesh_ids)
    pl.semaphore_wait(barrier, 3)

    def remote(src, dst, slot, peer):
        return pltpu.make_async_remote_copy(
            src_ref=src,
            dst_ref=dst,
            send_sem=send_sem.at[slot],
            recv_sem=recv_sem.at[slot],
            device_id={"tok": peer},
            device_id_type=mesh_ids,
        )

    local = pltpu.make_async_copy(w_ref, out_ref.at[me], local_sem.at[0])
    local.start()
    sends = []

    def send(src, dst, slot, peer):
        copy = remote(src, dst, slot, peer)
        copy.start()
        sends.append(copy)

    send(w_ref, out_ref.at[me], 0, up)
    send(w_ref, out_ref.at[me], 1, down)
    send(w_ref, out_ref.at[me], 4, partner)
    remote(w_ref, out_ref.at[down], 0, down).wait_recv()
    remote(w_ref, out_ref.at[up], 1, up).wait_recv()

    first = pl.ds(0, half)
    second = pl.ds(half, half)
    send(out_ref.at[down, first], out_ref.at[down, first], 2, up)
    send(out_ref.at[up, second], out_ref.at[up, second], 3, down)
    send(out_ref.at[up], out_ref.at[up], 5, partner)
    send(out_ref.at[down], out_ref.at[down], 6, partner)
    remote(out_ref.at[far, first], out_ref.at[far, first], 2, down).wait_recv()
    remote(out_ref.at[far, second], out_ref.at[far, second], 3, up).wait_recv()
    send(out_ref.at[far], out_ref.at[far], 7, partner)
    local.wait()

    theirs = (
        partner,
        lax.rem(partner + 2, tok_count),
        lax.rem(partner + tok_count - 2, tok_count),
        lax.rem(partner + 4, tok_count),
    )
    for idx, slot in enumerate(theirs):
        remote(out_ref.at[slot], out_ref.at[slot], 4 + idx, partner).wait_recv()
    for copy in sends:
        copy.wait_send()


def gather_over_tok(block, tok_count, collective_id):
    assert tok_count == 8
    rows, cols = block.shape
    return pl.pallas_call(
        lambda *refs: gather_tok_kernel(tok_count, *refs),
        out_shape=jax.ShapeDtypeStruct((tok_count, rows, cols), block.dtype),
        in_specs=[pl.BlockSpec(memory_space=pl.ANY)],
        out_specs=pl.BlockSpec(memory_space=pl.ANY),
        scratch_shapes=[
            pltpu.SemaphoreType.DMA((8,)),
            pltpu.SemaphoreType.DMA((8,)),
            pltpu.SemaphoreType.DMA((1,)),
        ],
        compiler_params=pltpu.CompilerParams(collective_id=collective_id, has_side_effects=True),
        cost_estimate=pl.CostEstimate(
            flops=0, transcendentals=0, bytes_accessed=2 * tok_count * rows * cols * 2
        ),
    )(block)


def project_tok_kernel(
    tok_count, att_ref, w_hbm, out_ref, att_all, w_buf, send_sem, recv_sem, load_sem
):
    mesh_ids = pl.DeviceIdType.MESH
    me = lax.axis_index("tok")
    up = lax.rem(me + 2, tok_count)
    down = lax.rem(me + tok_count - 2, tok_count)
    far = lax.rem(me + 4, tok_count)
    partner = me + 1 - 2 * lax.rem(me, 2)
    half = att_ref.shape[0] // 2
    cols = out_ref.shape[1]
    tile = 512
    tiles = cols // tile

    barrier = pltpu.get_barrier_semaphore()
    for peer in (up, down, partner):
        pl.semaphore_signal(barrier, inc=1, device_id={"tok": peer}, device_id_type=mesh_ids)
    pl.semaphore_wait(barrier, 3)

    def remote(src, dst, slot, peer):
        return pltpu.make_async_remote_copy(
            src_ref=src,
            dst_ref=dst,
            send_sem=send_sem.at[slot],
            recv_sem=recv_sem.at[slot],
            device_id={"tok": peer},
            device_id_type=mesh_ids,
        )

    theirs = (
        partner,
        lax.rem(partner + 2, tok_count),
        lax.rem(partner + tok_count - 2, tok_count),
        lax.rem(partner + 4, tok_count),
    )
    order = (me, theirs[0], down, up, theirs[1], theirs[2], far, theirs[3])

    def load(idx):
        return pltpu.make_async_copy(w_hbm.at[order[idx]], w_buf.at[idx % 2], load_sem.at[idx % 2])

    def accumulate(idx, source, first):
        load(idx).wait()
        if idx + 1 < len(order):
            load(idx + 1).start()
        weights = w_buf.at[idx % 2]

        def one_tile(col):
            span = pl.ds(pl.multiple_of(col * tile, tile), tile)
            term = jnp.dot(source[...], weights[:, span], preferred_element_type=jnp.float32)
            if first:
                out_ref[:, span] = term
            else:
                out_ref[:, span] = out_ref[:, span] + term

        pl.loop(0, tiles)(one_tile)

    load(0).start()
    sends = []

    def send(src, slot, index, peer):
        copy = remote(src, att_all.at[slot], index, peer)
        copy.start()
        sends.append(copy)

    def arrived(slot, index, peer, rows=None):
        dst = att_all.at[slot] if rows is None else att_all.at[slot, rows]
        remote(dst, dst, index, peer).wait_recv()

    first = pl.ds(0, half)
    second = pl.ds(half, half)
    send(att_ref, me, 0, up)
    send(att_ref, me, 1, down)
    send(att_ref, me, 4, partner)
    accumulate(0, att_ref, True)
    arrived(theirs[0], 4, partner)
    accumulate(1, att_all.at[theirs[0]], False)
    arrived(down, 0, down)
    arrived(up, 1, up)
    for src, index, peer in ((att_all.at[down, first], 2, up), (att_all.at[up, second], 3, down)):
        copy = remote(src, src, index, peer)
        copy.start()
        sends.append(copy)
    send(att_all.at[up], up, 5, partner)
    send(att_all.at[down], down, 6, partner)
    accumulate(2, att_all.at[down], False)
    accumulate(3, att_all.at[up], False)
    for idx in range(1, 3):
        arrived(theirs[idx], 4 + idx, partner)
        accumulate(3 + idx, att_all.at[theirs[idx]], False)
    arrived(far, 2, down, first)
    arrived(far, 3, up, second)
    send(att_all.at[far], far, 7, partner)
    accumulate(6, att_all.at[far], False)
    arrived(theirs[3], 7, partner)
    accumulate(7, att_all.at[theirs[3]], False)
    for copy in sends:
        copy.wait_send()


def project_over_tok(attention, w_all, tok_count, collective_id):
    assert tok_count == 8
    rows, width = attention.shape
    cols = w_all.shape[2]
    vmem = pltpu.MemorySpace.VMEM
    return pl.pallas_call(
        lambda *refs: project_tok_kernel(tok_count, *refs),
        out_shape=jax.ShapeDtypeStruct((rows, cols), jnp.float32),
        in_specs=[pl.BlockSpec(memory_space=vmem), pl.BlockSpec(memory_space=pl.ANY)],
        out_specs=pl.BlockSpec(memory_space=vmem),
        scratch_shapes=[
            pltpu.VMEM((tok_count, rows, width), attention.dtype),
            pltpu.VMEM((2, width, cols), w_all.dtype),
            pltpu.SemaphoreType.DMA((8,)),
            pltpu.SemaphoreType.DMA((8,)),
            pltpu.SemaphoreType.DMA((2,)),
        ],
        compiler_params=pltpu.CompilerParams(
            collective_id=collective_id, has_side_effects=True, vmem_limit_bytes=48 * 1024 * 1024
        ),
        cost_estimate=pl.CostEstimate(
            flops=2 * rows * width * tok_count * cols,
            transcendentals=0,
            bytes_accessed=tok_count * width * cols * 2 + rows * cols * 4,
        ),
    )(attention, w_all)


def scatter_tok_kernel(
    tok_count, part_hbm, out_ref, mine, chip_in, cross_out, cross_in, load_sem, send_sem, recv_sem
):
    mesh_ids = pl.DeviceIdType.MESH
    me = lax.axis_index("tok")
    up = lax.rem(me + 2, tok_count)
    down = lax.rem(me + tok_count - 2, tok_count)
    far = lax.rem(me + 4, tok_count)
    partner = me + 1 - 2 * lax.rem(me, 2)
    share = out_ref.shape[0]

    barrier = pltpu.get_barrier_semaphore()
    for peer in (up, down, far, partner):
        pl.semaphore_signal(barrier, inc=1, device_id={"tok": peer}, device_id_type=mesh_ids)
    pl.semaphore_wait(barrier, 4)

    def remote(src, dst, slot, peer):
        return pltpu.make_async_remote_copy(
            src_ref=src,
            dst_ref=dst,
            send_sem=send_sem.at[slot],
            recv_sem=recv_sem.at[slot],
            device_id={"tok": peer},
            device_id_type=mesh_ids,
        )

    def family(base):
        return (
            base,
            lax.rem(base + 2, tok_count),
            lax.rem(base + tok_count - 2, tok_count),
            lax.rem(base + 4, tok_count),
        )

    def rows_of(block):
        return pl.ds(pl.multiple_of(block * share, share), share)

    order = (3, 1, 2, 0)
    sends = []
    theirs = family(partner)
    for idx in order:
        copy = remote(part_hbm.at[rows_of(theirs[idx])], chip_in.at[idx], idx, partner)
        copy.start()
        sends.append(copy)
    own = family(me)
    loads = []
    for idx in order:
        load = pltpu.make_async_copy(part_hbm.at[rows_of(own[idx])], mine.at[idx], load_sem.at[idx])
        load.start()
        loads.append(load)
    targets = {1: (up, 1), 2: (down, 0), 3: (far, 2)}
    for pos, idx in enumerate(order[:3]):
        loads[pos].wait()
        remote(part_hbm.at[rows_of(own[idx])], chip_in.at[idx], idx, partner).wait_recv()
        cross_out[idx - 1] = (mine[idx] + chip_in[idx]).astype(cross_out.dtype)
        peer, dst_idx = targets[idx]
        copy = remote(cross_out.at[idx - 1], cross_in.at[dst_idx], 4 + dst_idx, peer)
        copy.start()
        sends.append(copy)
    loads[3].wait()
    remote(part_hbm.at[rows_of(own[0])], chip_in.at[0], 0, partner).wait_recv()
    total = mine[0] + chip_in[0]
    for idx, peer in ((0, up), (1, down), (2, far)):
        remote(cross_out.at[idx], cross_in.at[idx], 4 + idx, peer).wait_recv()
    for idx in range(3):
        total = total + cross_in[idx].astype(jnp.float32)
    out_ref[...] = total
    for copy in sends:
        copy.wait_send()


def scatter_over_tok(partial, tok_count, collective_id):
    assert tok_count == 8
    rows, cols = partial.shape
    share = rows // tok_count
    vmem = pltpu.MemorySpace.VMEM
    return pl.pallas_call(
        lambda *refs: scatter_tok_kernel(tok_count, *refs),
        out_shape=jax.ShapeDtypeStruct((share, cols), jnp.float32),
        in_specs=[pl.BlockSpec(memory_space=pltpu.MemorySpace.HBM)],
        out_specs=pl.BlockSpec(memory_space=vmem),
        scratch_shapes=[
            pltpu.VMEM((4, share, cols), jnp.float32),
            pltpu.VMEM((4, share, cols), jnp.float32),
            pltpu.VMEM((3, share, cols), jnp.bfloat16),
            pltpu.VMEM((3, share, cols), jnp.bfloat16),
            pltpu.SemaphoreType.DMA((4,)),
            pltpu.SemaphoreType.DMA((7,)),
            pltpu.SemaphoreType.DMA((7,)),
        ],
        compiler_params=pltpu.CompilerParams(
            collective_id=collective_id, has_side_effects=True, vmem_limit_bytes=48 * 1024 * 1024
        ),
        cost_estimate=pl.CostEstimate(
            flops=8 * share * cols, transcendentals=0, bytes_accessed=rows * cols * 4 * 2
        ),
    )(partial)


def local(
    queries,
    suffix_kv,
    prefix_cache,
    q_gain,
    k_gain,
    lengths,
    group_of,
    owner_order,
    residual,
    w_out,
    attn_gain,
    ffn_in_gain,
    ffn_out_gain,
    w_gate,
    w_up,
    w_down,
):
    req_count = lax.axis_size("req")
    tok_count = lax.axis_size("tok")
    req_index = lax.axis_index("req")
    tok_index = lax.axis_index("tok")
    row_count = queries.shape[0]
    heads_here = queries.shape[1] // HD
    head_ratio = H // KVH
    kv_first = tok_index * heads_here // head_ratio
    kv_width = KVH * HD
    own_count = req_count // GROUPS

    with jax.named_scope("prefix_gather"):
        pref_keys = lax.dynamic_slice_in_dim(prefix_cache, kv_first * HD, HD, 1)
        pref_vals = lax.dynamic_slice_in_dim(prefix_cache, kv_width + kv_first * HD, HD, 1)
        pref_kv = jnp.concatenate([pref_keys, pref_vals], axis=1)
        half_rows = pref_kv.shape[0] // 2
        core = tok_index % 2
        my_half = lax.dynamic_slice_in_dim(pref_kv, core * half_rows, half_rows, 0)
        gathered = lax.all_gather(my_half, "req", axis=0, tiled=False)
        w_out_all = gather_over_tok(w_out, tok_count, 0)
        gathered, w_out_all = lax.optimization_barrier((gathered, w_out_all))
        own_group = group_of[req_index]
        owner_ids = lax.dynamic_slice_in_dim(owner_order, own_group * own_count, own_count)
        picked = jnp.take(gathered, owner_ids, axis=0, mode="clip").reshape(-1, 2 * HD)
        partner = [(t, t ^ 1) for t in range(tok_count)]
        swapped = lax.ppermute(picked, "tok", perm=partner)
        shared = jnp.concatenate([picked, swapped], axis=0)

    with jax.named_scope("attention"):
        query_normed = norm_heads(queries, q_gain, heads_here)
        suf_keys = norm_heads(
            lax.dynamic_slice_in_dim(suffix_kv, kv_first * HD, HD, 1), k_gain, 1
        )
        suf_vals = lax.dynamic_slice_in_dim(suffix_kv, kv_width + kv_first * HD, HD, 1)
        all_keys = jnp.concatenate([shared[:, :HD], suf_keys], axis=0)
        all_vals = jnp.concatenate([shared[:, HD:], suf_vals], axis=0)
        seg_ends = jnp.cumsum(lengths[0])
        positions = jnp.arange(row_count, dtype=jnp.int32)
        segment = jnp.sum((positions[:, None] >= seg_ends[None, :]).astype(jnp.int32), axis=1)
        causal = (segment[:, None] == segment[None, :]) & (positions[None, :] <= positions[:, None])
        visible = jnp.concatenate(
            [jnp.ones((row_count, shared.shape[0]), jnp.bool_), causal], axis=1
        )
        outputs = []
        for head_idx in range(heads_here):
            head_q = query_normed[:, head_idx * HD:(head_idx + 1) * HD]
            scores = jnp.dot(head_q, all_keys.T, preferred_element_type=jnp.float32) * HD ** (-0.5)
            scores = jnp.where(visible, scores, MASKED)
            row_max = jnp.max(scores, axis=-1, keepdims=True)
            weights = jnp.exp(scores - row_max)
            row_sum = jnp.sum(weights, axis=-1, keepdims=True)
            head_out = jnp.dot(
                weights.astype(jnp.bfloat16), all_vals, preferred_element_type=jnp.float32
            ) / row_sum
            outputs.append(head_out)
        attention = jnp.concatenate(outputs, axis=1).astype(jnp.bfloat16)

    share = row_count // tok_count
    first_row = tok_index * share
    with jax.named_scope("out_projection"):
        projected = project_over_tok(attention, w_out_all, tok_count, 1)
        mixed_rows = residual.astype(jnp.float32) + rms_scale(projected, attn_gain)
        normed = rms_scale(mixed_rows, ffn_in_gain).astype(jnp.bfloat16)
        mixed_share = lax.dynamic_slice_in_dim(mixed_rows, first_row, share, 0)
    with jax.named_scope("feed_forward"):
        normed = lax.optimization_barrier(normed)
        gate = jnp.dot(normed, w_gate, preferred_element_type=jnp.float32)
        upward = jnp.dot(normed, w_up, preferred_element_type=jnp.float32)
        hidden = (jax.nn.gelu(gate, approximate=True) * upward).astype(jnp.bfloat16)
        hidden = lax.optimization_barrier(hidden)
        down_share = scatter_over_tok(
            jnp.dot(hidden, w_down, preferred_element_type=jnp.float32), tok_count, 2
        )
    return (mixed_share + rms_scale(down_share.astype(jnp.float32), ffn_out_gain)).astype(
        jnp.bfloat16
    )


def solution(mesh):
    in_specs = (
        P("req", "tok"),
        P("req", None),
        P("req", None),
        P(),
        P(),
        P("req", None),
        P(),
        P(),
        P("req", None),
        P("tok", None),
        P(),
        P(),
        P(),
        P(None, "tok"),
        P(None, "tok"),
        P("tok", None),
    )
    out_specs = P(("req", "tok"), None)
    return jax.shard_map(local, mesh=mesh, in_specs=in_specs, out_specs=out_specs, check_vma=False)
```

```python
import jax
import jax.numpy as jnp
from jax import lax
from jax.sharding import PartitionSpec as P
from jax.experimental import pallas as pl
from jax.experimental.pallas import tpu as pltpu

H = 8
KVH = 4
HD = 256
GROUPS = 2


EPSILON = 1e-06
MASKED = -1e30


def rms_scale(values_in, gain_vec):
    return (
        values_in
        * lax.rsqrt(jnp.mean(values_in * values_in, axis=-1, keepdims=True) + EPSILON)
        * gain_vec
    )


def norm_heads(values_in, gain_vec, head_count):
    row_count = values_in.shape[0]
    shaped = values_in.astype(jnp.float32).reshape(row_count, head_count, HD)
    return rms_scale(shaped, gain_vec).astype(jnp.bfloat16).reshape(row_count, head_count * HD)


def gather_tok_kernel(tok_count, w_ref, out_ref, send_sem, recv_sem, local_sem):
    mesh_ids = pl.DeviceIdType.MESH
    me = lax.axis_index("tok")
    up = lax.rem(me + 2, tok_count)
    down = lax.rem(me + tok_count - 2, tok_count)
    far = lax.rem(me + 4, tok_count)
    partner = me + 1 - 2 * lax.rem(me, 2)
    half = w_ref.shape[0] // 2

    barrier = pltpu.get_barrier_semaphore()
    for peer in (up, down, partner):
        pl.semaphore_signal(barrier, inc=1, device_id={"tok": peer}, device_id_type=mesh_ids)
    pl.semaphore_wait(barrier, 3)

    def remote(src, dst, slot, peer):
        return pltpu.make_async_remote_copy(
            src_ref=src,
            dst_ref=dst,
            send_sem=send_sem.at[slot],
            recv_sem=recv_sem.at[slot],
            device_id={"tok": peer},
            device_id_type=mesh_ids,
        )

    local = pltpu.make_async_copy(w_ref, out_ref.at[me], local_sem.at[0])
    local.start()
    sends = []

    def send(src, dst, slot, peer):
        copy = remote(src, dst, slot, peer)
        copy.start()
        sends.append(copy)

    send(w_ref, out_ref.at[me], 0, up)
    send(w_ref, out_ref.at[me], 1, down)
    send(w_ref, out_ref.at[me], 4, partner)
    remote(w_ref, out_ref.at[down], 0, down).wait_recv()
    remote(w_ref, out_ref.at[up], 1, up).wait_recv()

    first = pl.ds(0, half)
    second = pl.ds(half, half)
    send(out_ref.at[down, first], out_ref.at[down, first], 2, up)
    send(out_ref.at[up, second], out_ref.at[up, second], 3, down)
    send(out_ref.at[up], out_ref.at[up], 5, partner)
    send(out_ref.at[down], out_ref.at[down], 6, partner)
    remote(out_ref.at[far, first], out_ref.at[far, first], 2, down).wait_recv()
    remote(out_ref.at[far, second], out_ref.at[far, second], 3, up).wait_recv()
    send(out_ref.at[far], out_ref.at[far], 7, partner)
    local.wait()

    theirs = (
        partner,
        lax.rem(partner + 2, tok_count),
        lax.rem(partner + tok_count - 2, tok_count),
        lax.rem(partner + 4, tok_count),
    )
    for idx, slot in enumerate(theirs):
        remote(out_ref.at[slot], out_ref.at[slot], 4 + idx, partner).wait_recv()
    for copy in sends:
        copy.wait_send()


def gather_over_tok(block, tok_count, collective_id):
    assert tok_count == 8
    rows, cols = block.shape
    return pl.pallas_call(
        lambda *refs: gather_tok_kernel(tok_count, *refs),
        out_shape=jax.ShapeDtypeStruct((tok_count, rows, cols), block.dtype),
        in_specs=[pl.BlockSpec(memory_space=pl.ANY)],
        out_specs=pl.BlockSpec(memory_space=pl.ANY),
        scratch_shapes=[
            pltpu.SemaphoreType.DMA((8,)),
            pltpu.SemaphoreType.DMA((8,)),
            pltpu.SemaphoreType.DMA((1,)),
        ],
        compiler_params=pltpu.CompilerParams(collective_id=collective_id, has_side_effects=True),
        cost_estimate=pl.CostEstimate(
            flops=0, transcendentals=0, bytes_accessed=2 * tok_count * rows * cols * 2
        ),
    )(block)


def project_tok_kernel(
    tok_count, att_ref, w_hbm, out_ref, att_all, w_buf, send_sem, recv_sem, load_sem
):
    mesh_ids = pl.DeviceIdType.MESH
    me = lax.axis_index("tok")
    up = lax.rem(me + 2, tok_count)
    down = lax.rem(me + tok_count - 2, tok_count)
    far = lax.rem(me + 4, tok_count)
    partner = me + 1 - 2 * lax.rem(me, 2)
    half = att_ref.shape[0] // 2
    cols = out_ref.shape[1]
    tile = 512
    tiles = cols // tile

    barrier = pltpu.get_barrier_semaphore()
    for peer in (up, down, partner):
        pl.semaphore_signal(barrier, inc=1, device_id={"tok": peer}, device_id_type=mesh_ids)
    pl.semaphore_wait(barrier, 3)

    def remote(src, dst, slot, peer):
        return pltpu.make_async_remote_copy(
            src_ref=src,
            dst_ref=dst,
            send_sem=send_sem.at[slot],
            recv_sem=recv_sem.at[slot],
            device_id={"tok": peer},
            device_id_type=mesh_ids,
        )

    theirs = (
        partner,
        lax.rem(partner + 2, tok_count),
        lax.rem(partner + tok_count - 2, tok_count),
        lax.rem(partner + 4, tok_count),
    )
    order = (me, theirs[0], down, up, theirs[1], theirs[2], far, theirs[3])

    def load(idx):
        return pltpu.make_async_copy(w_hbm.at[order[idx]], w_buf.at[idx % 2], load_sem.at[idx % 2])

    def accumulate(idx, source, first):
        load(idx).wait()
        if idx + 1 < len(order):
            load(idx + 1).start()
        weights = w_buf.at[idx % 2]

        def one_tile(col):
            span = pl.ds(pl.multiple_of(col * tile, tile), tile)
            term = jnp.dot(source[...], weights[:, span], preferred_element_type=jnp.float32)
            if first:
                out_ref[:, span] = term
            else:
                out_ref[:, span] = out_ref[:, span] + term

        pl.loop(0, tiles)(one_tile)

    load(0).start()
    sends = []

    def send(src, slot, index, peer):
        copy = remote(src, att_all.at[slot], index, peer)
        copy.start()
        sends.append(copy)

    def arrived(slot, index, peer, rows=None):
        dst = att_all.at[slot] if rows is None else att_all.at[slot, rows]
        remote(dst, dst, index, peer).wait_recv()

    first = pl.ds(0, half)
    second = pl.ds(half, half)
    send(att_ref, me, 0, up)
    send(att_ref, me, 1, down)
    send(att_ref, me, 4, partner)
    accumulate(0, att_ref, True)
    arrived(theirs[0], 4, partner)
    accumulate(1, att_all.at[theirs[0]], False)
    arrived(down, 0, down)
    arrived(up, 1, up)
    for src, index, peer in ((att_all.at[down, first], 2, up), (att_all.at[up, second], 3, down)):
        copy = remote(src, src, index, peer)
        copy.start()
        sends.append(copy)
    send(att_all.at[up], up, 5, partner)
    send(att_all.at[down], down, 6, partner)
    accumulate(2, att_all.at[down], False)
    accumulate(3, att_all.at[up], False)
    for idx in range(1, 3):
        arrived(theirs[idx], 4 + idx, partner)
        accumulate(3 + idx, att_all.at[theirs[idx]], False)
    arrived(far, 2, down, first)
    arrived(far, 3, up, second)
    send(att_all.at[far], far, 7, partner)
    accumulate(6, att_all.at[far], False)
    arrived(theirs[3], 7, partner)
    accumulate(7, att_all.at[theirs[3]], False)
    for copy in sends:
        copy.wait_send()


def project_over_tok(attention, w_all, tok_count, collective_id):
    assert tok_count == 8
    rows, width = attention.shape
    cols = w_all.shape[2]
    vmem = pltpu.MemorySpace.VMEM
    return pl.pallas_call(
        lambda *refs: project_tok_kernel(tok_count, *refs),
        out_shape=jax.ShapeDtypeStruct((rows, cols), jnp.float32),
        in_specs=[pl.BlockSpec(memory_space=vmem), pl.BlockSpec(memory_space=pl.ANY)],
        out_specs=pl.BlockSpec(memory_space=vmem),
        scratch_shapes=[
            pltpu.VMEM((tok_count, rows, width), attention.dtype),
            pltpu.VMEM((2, width, cols), w_all.dtype),
            pltpu.SemaphoreType.DMA((8,)),
            pltpu.SemaphoreType.DMA((8,)),
            pltpu.SemaphoreType.DMA((2,)),
        ],
        compiler_params=pltpu.CompilerParams(
            collective_id=collective_id, has_side_effects=True, vmem_limit_bytes=48 * 1024 * 1024
        ),
        cost_estimate=pl.CostEstimate(
            flops=2 * rows * width * tok_count * cols,
            transcendentals=0,
            bytes_accessed=tok_count * width * cols * 2 + rows * cols * 4,
        ),
    )(attention, w_all)


def scatter_tok_kernel(
    tok_count, part_hbm, out_ref, mine, chip_in, cross_out, cross_in, load_sem, send_sem, recv_sem
):
    mesh_ids = pl.DeviceIdType.MESH
    me = lax.axis_index("tok")
    up = lax.rem(me + 2, tok_count)
    down = lax.rem(me + tok_count - 2, tok_count)
    far = lax.rem(me + 4, tok_count)
    partner = me + 1 - 2 * lax.rem(me, 2)
    share = out_ref.shape[0]

    barrier = pltpu.get_barrier_semaphore()
    for peer in (up, down, far, partner):
        pl.semaphore_signal(barrier, inc=1, device_id={"tok": peer}, device_id_type=mesh_ids)
    pl.semaphore_wait(barrier, 4)

    def remote(src, dst, slot, peer):
        return pltpu.make_async_remote_copy(
            src_ref=src,
            dst_ref=dst,
            send_sem=send_sem.at[slot],
            recv_sem=recv_sem.at[slot],
            device_id={"tok": peer},
            device_id_type=mesh_ids,
        )

    def family(base):
        return (
            base,
            lax.rem(base + 2, tok_count),
            lax.rem(base + tok_count - 2, tok_count),
            lax.rem(base + 4, tok_count),
        )

    def rows_of(block):
        return pl.ds(pl.multiple_of(block * share, share), share)

    order = (3, 1, 2, 0)
    sends = []
    theirs = family(partner)
    for idx in order:
        copy = remote(part_hbm.at[rows_of(theirs[idx])], chip_in.at[idx], idx, partner)
        copy.start()
        sends.append(copy)
    own = family(me)
    loads = []
    for idx in order:
        load = pltpu.make_async_copy(part_hbm.at[rows_of(own[idx])], mine.at[idx], load_sem.at[idx])
        load.start()
        loads.append(load)
    targets = {1: (up, 1), 2: (down, 0), 3: (far, 2)}
    for pos, idx in enumerate(order[:3]):
        loads[pos].wait()
        remote(part_hbm.at[rows_of(own[idx])], chip_in.at[idx], idx, partner).wait_recv()
        cross_out[idx - 1] = (mine[idx] + chip_in[idx]).astype(cross_out.dtype)
        peer, dst_idx = targets[idx]
        copy = remote(cross_out.at[idx - 1], cross_in.at[dst_idx], 4 + dst_idx, peer)
        copy.start()
        sends.append(copy)
    loads[3].wait()
    remote(part_hbm.at[rows_of(own[0])], chip_in.at[0], 0, partner).wait_recv()
    total = mine[0] + chip_in[0]
    for idx, peer in ((0, up), (1, down), (2, far)):
        remote(cross_out.at[idx], cross_in.at[idx], 4 + idx, peer).wait_recv()
    for idx in range(3):
        total = total + cross_in[idx].astype(jnp.float32)
    out_ref[...] = total
    for copy in sends:
        copy.wait_send()


def scatter_over_tok(partial, tok_count, collective_id):
    assert tok_count == 8
    rows, cols = partial.shape
    share = rows // tok_count
    vmem = pltpu.MemorySpace.VMEM
    return pl.pallas_call(
        lambda *refs: scatter_tok_kernel(tok_count, *refs),
        out_shape=jax.ShapeDtypeStruct((share, cols), jnp.float32),
        in_specs=[pl.BlockSpec(memory_space=pltpu.MemorySpace.HBM)],
        out_specs=pl.BlockSpec(memory_space=vmem),
        scratch_shapes=[
            pltpu.VMEM((4, share, cols), jnp.float32),
            pltpu.VMEM((4, share, cols), jnp.float32),
            pltpu.VMEM((3, share, cols), jnp.bfloat16),
            pltpu.VMEM((3, share, cols), jnp.bfloat16),
            pltpu.SemaphoreType.DMA((4,)),
            pltpu.SemaphoreType.DMA((7,)),
            pltpu.SemaphoreType.DMA((7,)),
        ],
        compiler_params=pltpu.CompilerParams(
            collective_id=collective_id, has_side_effects=True, vmem_limit_bytes=48 * 1024 * 1024
        ),
        cost_estimate=pl.CostEstimate(
            flops=8 * share * cols, transcendentals=0, bytes_accessed=rows * cols * 4 * 2
        ),
    )(partial)


def local(
    queries,
    suffix_kv,
    prefix_cache,
    q_gain,
    k_gain,
    lengths,
    group_of,
    owner_order,
    residual,
    w_out,
    attn_gain,
    ffn_in_gain,
    ffn_out_gain,
    w_gate,
    w_up,
    w_down,
):
    req_count = lax.axis_size("req")
    tok_count = lax.axis_size("tok")
    req_index = lax.axis_index("req")
    tok_index = lax.axis_index("tok")
    row_count = queries.shape[0]
    heads_here = queries.shape[1] // HD
    head_ratio = H // KVH
    kv_first = tok_index * heads_here // head_ratio
    kv_width = KVH * HD
    own_count = req_count // GROUPS

    with jax.named_scope("prefix_gather"):
        half_rows = prefix_cache.shape[0] // 2
        core = tok_index % 2
        first_row_kv = core * half_rows
        half_keys = lax.dynamic_slice(prefix_cache, (first_row_kv, kv_first * HD), (half_rows, HD))
        half_vals = lax.dynamic_slice(
            prefix_cache, (first_row_kv, kv_width + kv_first * HD), (half_rows, HD)
        )
        my_half = jnp.concatenate([half_keys, half_vals], axis=1)
        gathered = lax.all_gather(my_half, "req", axis=0, tiled=False)
        w_out_all = gather_over_tok(w_out, tok_count, 0)
        gathered, w_out_all = lax.optimization_barrier((gathered, w_out_all))
        own_group = group_of[req_index]
        owner_ids = lax.dynamic_slice_in_dim(owner_order, own_group * own_count, own_count)
        picked = jnp.take(gathered, owner_ids, axis=0, mode="clip").reshape(-1, 2 * HD)
        partner = [(t, t ^ 1) for t in range(tok_count)]
        swapped = lax.ppermute(picked, "tok", perm=partner)
        shared = jnp.concatenate([picked, swapped], axis=0)

    with jax.named_scope("attention"):
        query_normed = norm_heads(queries, q_gain, heads_here)
        suf_keys = norm_heads(
            lax.dynamic_slice_in_dim(suffix_kv, kv_first * HD, HD, 1), k_gain, 1
        )
        suf_vals = lax.dynamic_slice_in_dim(suffix_kv, kv_width + kv_first * HD, HD, 1)
        all_keys = jnp.concatenate([shared[:, :HD], suf_keys], axis=0)
        all_vals = jnp.concatenate([shared[:, HD:], suf_vals], axis=0)
        seg_ends = jnp.cumsum(lengths[0])
        positions = jnp.arange(row_count, dtype=jnp.int32)
        segment = jnp.sum((positions[:, None] >= seg_ends[None, :]).astype(jnp.int32), axis=1)
        causal = (segment[:, None] == segment[None, :]) & (positions[None, :] <= positions[:, None])
        visible = jnp.concatenate(
            [jnp.ones((row_count, shared.shape[0]), jnp.bool_), causal], axis=1
        )
        outputs = []
        for head_idx in range(heads_here):
            head_q = query_normed[:, head_idx * HD:(head_idx + 1) * HD]
            scores = jnp.dot(head_q, all_keys.T, preferred_element_type=jnp.float32) * HD ** (-0.5)
            scores = jnp.where(visible, scores, MASKED)
            row_max = jnp.max(scores, axis=-1, keepdims=True)
            weights = jnp.exp(scores - row_max)
            row_sum = jnp.sum(weights, axis=-1, keepdims=True)
            head_out = jnp.dot(
                weights.astype(jnp.bfloat16), all_vals, preferred_element_type=jnp.float32
            ) / row_sum
            outputs.append(head_out)
        attention = jnp.concatenate(outputs, axis=1).astype(jnp.bfloat16)

    share = row_count // tok_count
    first_row = tok_index * share
    with jax.named_scope("out_projection"):
        projected = project_over_tok(attention, w_out_all, tok_count, 1)
        mixed_rows = residual.astype(jnp.float32) + rms_scale(projected, attn_gain)
        normed = rms_scale(mixed_rows, ffn_in_gain).astype(jnp.bfloat16)
        mixed_share = lax.dynamic_slice_in_dim(mixed_rows, first_row, share, 0)
    with jax.named_scope("feed_forward"):
        normed = lax.optimization_barrier(normed)
        gate = jnp.dot(normed, w_gate, preferred_element_type=jnp.float32)
        upward = jnp.dot(normed, w_up, preferred_element_type=jnp.float32)
        hidden = (jax.nn.gelu(gate, approximate=True) * upward).astype(jnp.bfloat16)
        hidden = lax.optimization_barrier(hidden)
        down_share = scatter_over_tok(
            jnp.dot(hidden, w_down, preferred_element_type=jnp.float32), tok_count, 2
        )
    return (mixed_share + rms_scale(down_share.astype(jnp.float32), ffn_out_gain)).astype(
        jnp.bfloat16
    )


def solution(mesh):
    in_specs = (
        P("req", "tok"),
        P("req", None),
        P("req", None),
        P(),
        P(),
        P("req", None),
        P(),
        P(),
        P("req", None),
        P("tok", None),
        P(),
        P(),
        P(),
        P(None, "tok"),
        P(None, "tok"),
        P("tok", None),
    )
    out_specs = P(("req", "tok"), None)
    return jax.shard_map(local, mesh=mesh, in_specs=in_specs, out_specs=out_specs, check_vma=False)
```

```python
import jax
import jax.numpy as jnp
from jax import lax
from jax.sharding import PartitionSpec as P
from jax.experimental import pallas as pl
from jax.experimental.pallas import tpu as pltpu

H = 8
KVH = 4
HD = 256
GROUPS = 2


EPSILON = 1e-06
MASKED = -1e30


def rms_scale(values_in, gain_vec):
    return (
        values_in
        * lax.rsqrt(jnp.mean(values_in * values_in, axis=-1, keepdims=True) + EPSILON)
        * gain_vec
    )


def norm_heads(values_in, gain_vec, head_count):
    row_count = values_in.shape[0]
    shaped = values_in.astype(jnp.float32).reshape(row_count, head_count, HD)
    return rms_scale(shaped, gain_vec).astype(jnp.bfloat16).reshape(row_count, head_count * HD)


def gather_tok_kernel(tok_count, w_ref, out_ref, send_sem, recv_sem, local_sem):
    mesh_ids = pl.DeviceIdType.MESH
    me = lax.axis_index("tok")
    up = lax.rem(me + 2, tok_count)
    down = lax.rem(me + tok_count - 2, tok_count)
    far = lax.rem(me + 4, tok_count)
    partner = me + 1 - 2 * lax.rem(me, 2)
    half = w_ref.shape[0] // 2

    barrier = pltpu.get_barrier_semaphore()
    for peer in (up, down, partner):
        pl.semaphore_signal(barrier, inc=1, device_id={"tok": peer}, device_id_type=mesh_ids)
    pl.semaphore_wait(barrier, 3)

    def remote(src, dst, slot, peer):
        return pltpu.make_async_remote_copy(
            src_ref=src,
            dst_ref=dst,
            send_sem=send_sem.at[slot],
            recv_sem=recv_sem.at[slot],
            device_id={"tok": peer},
            device_id_type=mesh_ids,
        )

    local = pltpu.make_async_copy(w_ref, out_ref.at[me], local_sem.at[0])
    local.start()
    sends = []

    def send(src, dst, slot, peer):
        copy = remote(src, dst, slot, peer)
        copy.start()
        sends.append(copy)

    send(w_ref, out_ref.at[me], 0, up)
    send(w_ref, out_ref.at[me], 1, down)
    send(w_ref, out_ref.at[me], 4, partner)
    remote(w_ref, out_ref.at[down], 0, down).wait_recv()
    remote(w_ref, out_ref.at[up], 1, up).wait_recv()

    first = pl.ds(0, half)
    second = pl.ds(half, half)
    send(out_ref.at[down, first], out_ref.at[down, first], 2, up)
    send(out_ref.at[up, second], out_ref.at[up, second], 3, down)
    send(out_ref.at[up], out_ref.at[up], 5, partner)
    send(out_ref.at[down], out_ref.at[down], 6, partner)
    remote(out_ref.at[far, first], out_ref.at[far, first], 2, down).wait_recv()
    remote(out_ref.at[far, second], out_ref.at[far, second], 3, up).wait_recv()
    send(out_ref.at[far], out_ref.at[far], 7, partner)
    local.wait()

    theirs = (
        partner,
        lax.rem(partner + 2, tok_count),
        lax.rem(partner + tok_count - 2, tok_count),
        lax.rem(partner + 4, tok_count),
    )
    for idx, slot in enumerate(theirs):
        remote(out_ref.at[slot], out_ref.at[slot], 4 + idx, partner).wait_recv()
    for copy in sends:
        copy.wait_send()


def gather_over_tok(block, tok_count, collective_id):
    assert tok_count == 8
    rows, cols = block.shape
    return pl.pallas_call(
        lambda *refs: gather_tok_kernel(tok_count, *refs),
        out_shape=jax.ShapeDtypeStruct((tok_count, rows, cols), block.dtype),
        in_specs=[pl.BlockSpec(memory_space=pl.ANY)],
        out_specs=pl.BlockSpec(memory_space=pl.ANY),
        scratch_shapes=[
            pltpu.SemaphoreType.DMA((8,)),
            pltpu.SemaphoreType.DMA((8,)),
            pltpu.SemaphoreType.DMA((1,)),
        ],
        compiler_params=pltpu.CompilerParams(collective_id=collective_id, has_side_effects=True),
        cost_estimate=pl.CostEstimate(
            flops=0, transcendentals=0, bytes_accessed=2 * tok_count * rows * cols * 2
        ),
    )(block)


def project_tok_kernel(
    tok_count,
    att_ref,
    w_hbm,
    res_ref,
    attn_gain_ref,
    ffn_gain_ref,
    normed_ref,
    mixed_ref,
    out_ref,
    att_all,
    w_buf,
    send_sem,
    recv_sem,
    load_sem,
):
    mesh_ids = pl.DeviceIdType.MESH
    me = lax.axis_index("tok")
    up = lax.rem(me + 2, tok_count)
    down = lax.rem(me + tok_count - 2, tok_count)
    far = lax.rem(me + 4, tok_count)
    partner = me + 1 - 2 * lax.rem(me, 2)
    half = att_ref.shape[0] // 2
    cols = out_ref.shape[1]
    tile = 512
    tiles = cols // tile

    barrier = pltpu.get_barrier_semaphore()
    for peer in (up, down, partner):
        pl.semaphore_signal(barrier, inc=1, device_id={"tok": peer}, device_id_type=mesh_ids)
    pl.semaphore_wait(barrier, 3)

    def remote(src, dst, slot, peer):
        return pltpu.make_async_remote_copy(
            src_ref=src,
            dst_ref=dst,
            send_sem=send_sem.at[slot],
            recv_sem=recv_sem.at[slot],
            device_id={"tok": peer},
            device_id_type=mesh_ids,
        )

    theirs = (
        partner,
        lax.rem(partner + 2, tok_count),
        lax.rem(partner + tok_count - 2, tok_count),
        lax.rem(partner + 4, tok_count),
    )
    order = (me, theirs[0], down, up, theirs[1], theirs[2], far, theirs[3])

    def load(idx):
        return pltpu.make_async_copy(w_hbm.at[order[idx]], w_buf.at[idx % 2], load_sem.at[idx % 2])

    def accumulate(idx, source, first):
        load(idx).wait()
        if idx + 1 < len(order):
            load(idx + 1).start()
        weights = w_buf.at[idx % 2]

        def one_tile(col):
            span = pl.ds(pl.multiple_of(col * tile, tile), tile)
            term = jnp.dot(source[...], weights[:, span], preferred_element_type=jnp.float32)
            if first:
                out_ref[:, span] = term
            else:
                out_ref[:, span] = out_ref[:, span] + term

        pl.loop(0, tiles)(one_tile)

    load(0).start()
    sends = []

    def send(src, slot, index, peer):
        copy = remote(src, att_all.at[slot], index, peer)
        copy.start()
        sends.append(copy)

    def arrived(slot, index, peer, rows=None):
        dst = att_all.at[slot] if rows is None else att_all.at[slot, rows]
        remote(dst, dst, index, peer).wait_recv()

    first = pl.ds(0, half)
    second = pl.ds(half, half)
    send(att_ref, me, 0, up)
    send(att_ref, me, 1, down)
    send(att_ref, me, 4, partner)
    accumulate(0, att_ref, True)
    arrived(theirs[0], 4, partner)
    accumulate(1, att_all.at[theirs[0]], False)
    arrived(down, 0, down)
    arrived(up, 1, up)
    for src, index, peer in ((att_all.at[down, first], 2, up), (att_all.at[up, second], 3, down)):
        copy = remote(src, src, index, peer)
        copy.start()
        sends.append(copy)
    send(att_all.at[up], up, 5, partner)
    send(att_all.at[down], down, 6, partner)
    accumulate(2, att_all.at[down], False)
    accumulate(3, att_all.at[up], False)
    for idx in range(1, 3):
        arrived(theirs[idx], 4 + idx, partner)
        accumulate(3 + idx, att_all.at[theirs[idx]], False)
    arrived(far, 2, down, first)
    arrived(far, 3, up, second)
    send(att_all.at[far], far, 7, partner)
    accumulate(6, att_all.at[far], False)
    arrived(theirs[3], 7, partner)
    accumulate(7, att_all.at[theirs[3]], False)

    share = mixed_ref.shape[0]

    def finish(block):
        rows = pl.ds(pl.multiple_of(block * share, share), share)
        mixed = res_ref[rows, :].astype(jnp.float32) + rms_scale(out_ref[rows, :], attn_gain_ref[...])
        normed_ref[rows, :] = rms_scale(mixed, ffn_gain_ref[...]).astype(normed_ref.dtype)

    pl.loop(0, out_ref.shape[0] // share)(finish)
    own_rows = pl.ds(pl.multiple_of(me * share, share), share)
    mixed_ref[...] = res_ref[own_rows, :].astype(jnp.float32) + rms_scale(
        out_ref[own_rows, :], attn_gain_ref[...]
    )
    for copy in sends:
        copy.wait_send()


def project_over_tok(attention, w_all, residual, attn_gain, ffn_gain, tok_count, collective_id):
    assert tok_count == 8
    rows, width = attention.shape
    cols = w_all.shape[2]
    share = rows // tok_count
    vmem = pltpu.MemorySpace.VMEM
    vmem_spec = pl.BlockSpec(memory_space=vmem)
    return pl.pallas_call(
        lambda *refs: project_tok_kernel(tok_count, *refs),
        out_shape=(
            jax.ShapeDtypeStruct((rows, cols), jnp.bfloat16),
            jax.ShapeDtypeStruct((share, cols), jnp.float32),
        ),
        in_specs=[vmem_spec, pl.BlockSpec(memory_space=pl.ANY), vmem_spec, vmem_spec, vmem_spec],
        out_specs=(vmem_spec, vmem_spec),
        scratch_shapes=[
            pltpu.VMEM((rows, cols), jnp.float32),
            pltpu.VMEM((tok_count, rows, width), attention.dtype),
            pltpu.VMEM((2, width, cols), w_all.dtype),
            pltpu.SemaphoreType.DMA((8,)),
            pltpu.SemaphoreType.DMA((8,)),
            pltpu.SemaphoreType.DMA((2,)),
        ],
        compiler_params=pltpu.CompilerParams(
            collective_id=collective_id, has_side_effects=True, vmem_limit_bytes=48 * 1024 * 1024
        ),
        cost_estimate=pl.CostEstimate(
            flops=2 * rows * width * tok_count * cols,
            transcendentals=2 * rows,
            bytes_accessed=tok_count * width * cols * 2 + rows * cols * 4,
        ),
    )(attention, w_all, residual, attn_gain.reshape(1, cols), ffn_gain.reshape(1, cols))


def scatter_tok_kernel(
    tok_count, part_hbm, out_ref, mine, chip_in, cross_out, cross_in, load_sem, send_sem, recv_sem
):
    mesh_ids = pl.DeviceIdType.MESH
    me = lax.axis_index("tok")
    up = lax.rem(me + 2, tok_count)
    down = lax.rem(me + tok_count - 2, tok_count)
    far = lax.rem(me + 4, tok_count)
    partner = me + 1 - 2 * lax.rem(me, 2)
    share = out_ref.shape[0]

    barrier = pltpu.get_barrier_semaphore()
    for peer in (up, down, far, partner):
        pl.semaphore_signal(barrier, inc=1, device_id={"tok": peer}, device_id_type=mesh_ids)
    pl.semaphore_wait(barrier, 4)

    def remote(src, dst, slot, peer):
        return pltpu.make_async_remote_copy(
            src_ref=src,
            dst_ref=dst,
            send_sem=send_sem.at[slot],
            recv_sem=recv_sem.at[slot],
            device_id={"tok": peer},
            device_id_type=mesh_ids,
        )

    def family(base):
        return (
            base,
            lax.rem(base + 2, tok_count),
            lax.rem(base + tok_count - 2, tok_count),
            lax.rem(base + 4, tok_count),
        )

    def rows_of(block):
        return pl.ds(pl.multiple_of(block * share, share), share)

    order = (3, 1, 2, 0)
    sends = []
    theirs = family(partner)
    for idx in order:
        copy = remote(part_hbm.at[rows_of(theirs[idx])], chip_in.at[idx], idx, partner)
        copy.start()
        sends.append(copy)
    own = family(me)
    loads = []
    for idx in order:
        load = pltpu.make_async_copy(part_hbm.at[rows_of(own[idx])], mine.at[idx], load_sem.at[idx])
        load.start()
        loads.append(load)
    targets = {1: (up, 1), 2: (down, 0), 3: (far, 2)}
    for pos, idx in enumerate(order[:3]):
        loads[pos].wait()
        remote(part_hbm.at[rows_of(own[idx])], chip_in.at[idx], idx, partner).wait_recv()
        cross_out[idx - 1] = (mine[idx] + chip_in[idx]).astype(cross_out.dtype)
        peer, dst_idx = targets[idx]
        copy = remote(cross_out.at[idx - 1], cross_in.at[dst_idx], 4 + dst_idx, peer)
        copy.start()
        sends.append(copy)
    loads[3].wait()
    remote(part_hbm.at[rows_of(own[0])], chip_in.at[0], 0, partner).wait_recv()
    total = mine[0] + chip_in[0]
    for idx, peer in ((0, up), (1, down), (2, far)):
        remote(cross_out.at[idx], cross_in.at[idx], 4 + idx, peer).wait_recv()
    for idx in range(3):
        total = total + cross_in[idx].astype(jnp.float32)
    out_ref[...] = total
    for copy in sends:
        copy.wait_send()


def scatter_over_tok(partial, tok_count, collective_id):
    assert tok_count == 8
    rows, cols = partial.shape
    share = rows // tok_count
    vmem = pltpu.MemorySpace.VMEM
    return pl.pallas_call(
        lambda *refs: scatter_tok_kernel(tok_count, *refs),
        out_shape=jax.ShapeDtypeStruct((share, cols), jnp.float32),
        in_specs=[pl.BlockSpec(memory_space=pltpu.MemorySpace.HBM)],
        out_specs=pl.BlockSpec(memory_space=vmem),
        scratch_shapes=[
            pltpu.VMEM((4, share, cols), jnp.float32),
            pltpu.VMEM((4, share, cols), jnp.float32),
            pltpu.VMEM((3, share, cols), jnp.bfloat16),
            pltpu.VMEM((3, share, cols), jnp.bfloat16),
            pltpu.SemaphoreType.DMA((4,)),
            pltpu.SemaphoreType.DMA((7,)),
            pltpu.SemaphoreType.DMA((7,)),
        ],
        compiler_params=pltpu.CompilerParams(
            collective_id=collective_id, has_side_effects=True, vmem_limit_bytes=48 * 1024 * 1024
        ),
        cost_estimate=pl.CostEstimate(
            flops=8 * share * cols, transcendentals=0, bytes_accessed=rows * cols * 4 * 2
        ),
    )(partial)


def local(
    queries,
    suffix_kv,
    prefix_cache,
    q_gain,
    k_gain,
    lengths,
    group_of,
    owner_order,
    residual,
    w_out,
    attn_gain,
    ffn_in_gain,
    ffn_out_gain,
    w_gate,
    w_up,
    w_down,
):
    req_count = lax.axis_size("req")
    tok_count = lax.axis_size("tok")
    req_index = lax.axis_index("req")
    tok_index = lax.axis_index("tok")
    row_count = queries.shape[0]
    heads_here = queries.shape[1] // HD
    head_ratio = H // KVH
    kv_first = tok_index * heads_here // head_ratio
    kv_width = KVH * HD
    own_count = req_count // GROUPS

    with jax.named_scope("prefix_gather"):
        half_rows = prefix_cache.shape[0] // 2
        core = tok_index % 2
        first_row_kv = core * half_rows
        half_keys = lax.dynamic_slice(prefix_cache, (first_row_kv, kv_first * HD), (half_rows, HD))
        half_vals = lax.dynamic_slice(
            prefix_cache, (first_row_kv, kv_width + kv_first * HD), (half_rows, HD)
        )
        my_half = jnp.concatenate([half_keys, half_vals], axis=1)
        gathered = lax.all_gather(my_half, "req", axis=0, tiled=False)
        w_out_all = gather_over_tok(w_out, tok_count, 0)
        gathered, w_out_all = lax.optimization_barrier((gathered, w_out_all))
        own_group = group_of[req_index]
        owner_ids = lax.dynamic_slice_in_dim(owner_order, own_group * own_count, own_count)
        picked = jnp.take(gathered, owner_ids, axis=0, mode="clip").reshape(-1, 2 * HD)
        partner = [(t, t ^ 1) for t in range(tok_count)]
        swapped = lax.ppermute(picked, "tok", perm=partner)
        shared = jnp.concatenate([picked, swapped], axis=0)

    with jax.named_scope("attention"):
        query_normed = norm_heads(queries, q_gain, heads_here)
        suf_keys = norm_heads(
            lax.dynamic_slice_in_dim(suffix_kv, kv_first * HD, HD, 1), k_gain, 1
        )
        suf_vals = lax.dynamic_slice_in_dim(suffix_kv, kv_width + kv_first * HD, HD, 1)
        all_keys = jnp.concatenate([shared[:, :HD], suf_keys], axis=0)
        all_vals = jnp.concatenate([shared[:, HD:], suf_vals], axis=0)
        seg_ends = jnp.cumsum(lengths[0])
        positions = jnp.arange(row_count, dtype=jnp.int32)
        segment = jnp.sum((positions[:, None] >= seg_ends[None, :]).astype(jnp.int32), axis=1)
        causal = (segment[:, None] == segment[None, :]) & (positions[None, :] <= positions[:, None])
        visible = jnp.concatenate(
            [jnp.ones((row_count, shared.shape[0]), jnp.bool_), causal], axis=1
        )
        outputs = []
        for head_idx in range(heads_here):
            head_q = query_normed[:, head_idx * HD:(head_idx + 1) * HD]
            scores = jnp.dot(head_q, all_keys.T, preferred_element_type=jnp.float32) * HD ** (-0.5)
            scores = jnp.where(visible, scores, MASKED)
            row_max = jnp.max(scores, axis=-1, keepdims=True)
            weights = jnp.exp(scores - row_max)
            row_sum = jnp.sum(weights, axis=-1, keepdims=True)
            head_out = jnp.dot(
                weights.astype(jnp.bfloat16), all_vals, preferred_element_type=jnp.float32
            ) / row_sum
            outputs.append(head_out)
        attention = jnp.concatenate(outputs, axis=1).astype(jnp.bfloat16)

    share = row_count // tok_count
    first_row = tok_index * share
    with jax.named_scope("out_projection"):
        normed, mixed_share = project_over_tok(
            attention, w_out_all, residual, attn_gain, ffn_in_gain, tok_count, 1
        )
    with jax.named_scope("feed_forward"):
        normed = lax.optimization_barrier(normed)
        gate = jnp.dot(normed, w_gate, preferred_element_type=jnp.float32)
        upward = jnp.dot(normed, w_up, preferred_element_type=jnp.float32)
        hidden = (jax.nn.gelu(gate, approximate=True) * upward).astype(jnp.bfloat16)
        hidden = lax.optimization_barrier(hidden)
        down_share = scatter_over_tok(
            jnp.dot(hidden, w_down, preferred_element_type=jnp.float32), tok_count, 2
        )
    return (mixed_share + rms_scale(down_share.astype(jnp.float32), ffn_out_gain)).astype(
        jnp.bfloat16
    )


def solution(mesh):
    in_specs = (
        P("req", "tok"),
        P("req", None),
        P("req", None),
        P(),
        P(),
        P("req", None),
        P(),
        P(),
        P("req", None),
        P("tok", None),
        P(),
        P(),
        P(),
        P(None, "tok"),
        P(None, "tok"),
        P("tok", None),
    )
    out_specs = P(("req", "tok"), None)
    return jax.shard_map(local, mesh=mesh, in_specs=in_specs, out_specs=out_specs, check_vma=False)
```

```python
import jax
import jax.numpy as jnp
from jax import lax
from jax.sharding import PartitionSpec as P
from jax.experimental import pallas as pl
from jax.experimental.pallas import tpu as pltpu

H = 8
KVH = 4
HD = 256
GROUPS = 2


EPSILON = 1e-06
MASKED = -1e30


def rms_scale(values_in, gain_vec):
    return (
        values_in
        * lax.rsqrt(jnp.mean(values_in * values_in, axis=-1, keepdims=True) + EPSILON)
        * gain_vec
    )


def norm_heads(values_in, gain_vec, head_count):
    row_count = values_in.shape[0]
    shaped = values_in.astype(jnp.float32).reshape(row_count, head_count, HD)
    return rms_scale(shaped, gain_vec).astype(jnp.bfloat16).reshape(row_count, head_count * HD)


def gather_tok_kernel(tok_count, w_ref, out_ref, send_sem, recv_sem, local_sem):
    mesh_ids = pl.DeviceIdType.MESH
    me = lax.axis_index("tok")
    up = lax.rem(me + 2, tok_count)
    down = lax.rem(me + tok_count - 2, tok_count)
    far = lax.rem(me + 4, tok_count)
    partner = me + 1 - 2 * lax.rem(me, 2)
    half = w_ref.shape[0] // 2

    barrier = pltpu.get_barrier_semaphore()
    for peer in (up, down, partner):
        pl.semaphore_signal(barrier, inc=1, device_id={"tok": peer}, device_id_type=mesh_ids)
    pl.semaphore_wait(barrier, 3)

    def remote(src, dst, slot, peer):
        return pltpu.make_async_remote_copy(
            src_ref=src,
            dst_ref=dst,
            send_sem=send_sem.at[slot],
            recv_sem=recv_sem.at[slot],
            device_id={"tok": peer},
            device_id_type=mesh_ids,
        )

    local = pltpu.make_async_copy(w_ref, out_ref.at[me], local_sem.at[0])
    local.start()
    sends = []

    def send(src, dst, slot, peer):
        copy = remote(src, dst, slot, peer)
        copy.start()
        sends.append(copy)

    send(w_ref, out_ref.at[me], 0, up)
    send(w_ref, out_ref.at[me], 1, down)
    send(w_ref, out_ref.at[me], 4, partner)
    remote(w_ref, out_ref.at[down], 0, down).wait_recv()
    remote(w_ref, out_ref.at[up], 1, up).wait_recv()

    first = pl.ds(0, half)
    second = pl.ds(half, half)
    send(out_ref.at[down, first], out_ref.at[down, first], 2, up)
    send(out_ref.at[up, second], out_ref.at[up, second], 3, down)
    send(out_ref.at[up], out_ref.at[up], 5, partner)
    send(out_ref.at[down], out_ref.at[down], 6, partner)
    remote(out_ref.at[far, first], out_ref.at[far, first], 2, down).wait_recv()
    remote(out_ref.at[far, second], out_ref.at[far, second], 3, up).wait_recv()
    send(out_ref.at[far], out_ref.at[far], 7, partner)
    local.wait()

    theirs = (
        partner,
        lax.rem(partner + 2, tok_count),
        lax.rem(partner + tok_count - 2, tok_count),
        lax.rem(partner + 4, tok_count),
    )
    for idx, slot in enumerate(theirs):
        remote(out_ref.at[slot], out_ref.at[slot], 4 + idx, partner).wait_recv()
    for copy in sends:
        copy.wait_send()


def gather_over_tok(block, tok_count, collective_id):
    assert tok_count == 8
    rows, cols = block.shape
    return pl.pallas_call(
        lambda *refs: gather_tok_kernel(tok_count, *refs),
        out_shape=jax.ShapeDtypeStruct((tok_count, rows, cols), block.dtype),
        in_specs=[pl.BlockSpec(memory_space=pl.ANY)],
        out_specs=pl.BlockSpec(memory_space=pl.ANY),
        scratch_shapes=[
            pltpu.SemaphoreType.DMA((8,)),
            pltpu.SemaphoreType.DMA((8,)),
            pltpu.SemaphoreType.DMA((1,)),
        ],
        compiler_params=pltpu.CompilerParams(collective_id=collective_id, has_side_effects=True),
        cost_estimate=pl.CostEstimate(
            flops=0, transcendentals=0, bytes_accessed=2 * tok_count * rows * cols * 2
        ),
    )(block)


def project_tok_kernel(
    tok_count,
    att_ref,
    w_hbm,
    res_ref,
    attn_gain_ref,
    ffn_gain_ref,
    normed_ref,
    mixed_ref,
    out_ref,
    att_all,
    w_buf,
    send_sem,
    recv_sem,
    load_sem,
):
    mesh_ids = pl.DeviceIdType.MESH
    me = lax.axis_index("tok")
    up = lax.rem(me + 2, tok_count)
    down = lax.rem(me + tok_count - 2, tok_count)
    far = lax.rem(me + 4, tok_count)
    partner = me + 1 - 2 * lax.rem(me, 2)
    half = att_ref.shape[0] // 2
    cols = out_ref.shape[1]
    tile = 512
    tiles = cols // tile

    barrier = pltpu.get_barrier_semaphore()
    for peer in (up, down, partner):
        pl.semaphore_signal(barrier, inc=1, device_id={"tok": peer}, device_id_type=mesh_ids)
    pl.semaphore_wait(barrier, 3)

    def remote(src, dst, slot, peer):
        return pltpu.make_async_remote_copy(
            src_ref=src,
            dst_ref=dst,
            send_sem=send_sem.at[slot],
            recv_sem=recv_sem.at[slot],
            device_id={"tok": peer},
            device_id_type=mesh_ids,
        )

    theirs = (
        partner,
        lax.rem(partner + 2, tok_count),
        lax.rem(partner + tok_count - 2, tok_count),
        lax.rem(partner + 4, tok_count),
    )
    order = (me, theirs[0], down, up, theirs[1], theirs[2], far, theirs[3])

    def load(idx):
        return pltpu.make_async_copy(w_hbm.at[order[idx]], w_buf.at[idx % 2], load_sem.at[idx % 2])

    def accumulate(idx, source, first):
        load(idx).wait()
        if idx + 1 < len(order):
            load(idx + 1).start()
        weights = w_buf.at[idx % 2]

        def one_tile(col):
            span = pl.ds(pl.multiple_of(col * tile, tile), tile)
            term = jnp.dot(source[...], weights[:, span], preferred_element_type=jnp.float32)
            if first:
                out_ref[:, span] = term
            else:
                out_ref[:, span] = out_ref[:, span] + term

        pl.loop(0, tiles)(one_tile)

    load(0).start()
    sends = []

    def send(src, slot, index, peer):
        copy = remote(src, att_all.at[slot], index, peer)
        copy.start()
        sends.append(copy)

    def arrived(slot, index, peer, rows=None):
        dst = att_all.at[slot] if rows is None else att_all.at[slot, rows]
        remote(dst, dst, index, peer).wait_recv()

    first = pl.ds(0, half)
    second = pl.ds(half, half)
    send(att_ref, me, 0, up)
    send(att_ref, me, 1, down)
    send(att_ref, me, 4, partner)
    accumulate(0, att_ref, True)
    arrived(theirs[0], 4, partner)
    accumulate(1, att_all.at[theirs[0]], False)
    arrived(down, 0, down)
    arrived(up, 1, up)
    for src, index, peer in ((att_all.at[down, first], 2, up), (att_all.at[up, second], 3, down)):
        copy = remote(src, src, index, peer)
        copy.start()
        sends.append(copy)
    send(att_all.at[up], up, 5, partner)
    send(att_all.at[down], down, 6, partner)
    accumulate(2, att_all.at[down], False)
    accumulate(3, att_all.at[up], False)
    for idx in range(1, 3):
        arrived(theirs[idx], 4 + idx, partner)
        accumulate(3 + idx, att_all.at[theirs[idx]], False)
    arrived(far, 2, down, first)
    arrived(far, 3, up, second)
    send(att_all.at[far], far, 7, partner)
    accumulate(6, att_all.at[far], False)
    arrived(theirs[3], 7, partner)
    accumulate(7, att_all.at[theirs[3]], False)

    share = mixed_ref.shape[0]

    def finish(block):
        rows = pl.ds(pl.multiple_of(block * share, share), share)
        mixed = res_ref[rows, :].astype(jnp.float32) + rms_scale(out_ref[rows, :], attn_gain_ref[...])
        normed_ref[rows, :] = rms_scale(mixed, ffn_gain_ref[...]).astype(normed_ref.dtype)

    pl.loop(0, out_ref.shape[0] // share)(finish)
    own_rows = pl.ds(pl.multiple_of(me * share, share), share)
    mixed_ref[...] = res_ref[own_rows, :].astype(jnp.float32) + rms_scale(
        out_ref[own_rows, :], attn_gain_ref[...]
    )
    for copy in sends:
        copy.wait_send()


def project_over_tok(attention, w_all, residual, attn_gain, ffn_gain, tok_count, collective_id):
    assert tok_count == 8
    rows, width = attention.shape
    cols = w_all.shape[2]
    share = rows // tok_count
    vmem = pltpu.MemorySpace.VMEM
    vmem_spec = pl.BlockSpec(memory_space=vmem)
    return pl.pallas_call(
        lambda *refs: project_tok_kernel(tok_count, *refs),
        out_shape=(
            jax.ShapeDtypeStruct((rows, cols), jnp.bfloat16),
            jax.ShapeDtypeStruct((share, cols), jnp.float32),
        ),
        in_specs=[vmem_spec, pl.BlockSpec(memory_space=pl.ANY), vmem_spec, vmem_spec, vmem_spec],
        out_specs=(vmem_spec, vmem_spec),
        scratch_shapes=[
            pltpu.VMEM((rows, cols), jnp.float32),
            pltpu.VMEM((tok_count, rows, width), attention.dtype),
            pltpu.VMEM((2, width, cols), w_all.dtype),
            pltpu.SemaphoreType.DMA((8,)),
            pltpu.SemaphoreType.DMA((8,)),
            pltpu.SemaphoreType.DMA((2,)),
        ],
        compiler_params=pltpu.CompilerParams(
            collective_id=collective_id, has_side_effects=True, vmem_limit_bytes=48 * 1024 * 1024
        ),
        cost_estimate=pl.CostEstimate(
            flops=2 * rows * width * tok_count * cols,
            transcendentals=2 * rows,
            bytes_accessed=tok_count * width * cols * 2 + rows * cols * 4,
        ),
    )(attention, w_all, residual, attn_gain.reshape(1, cols), ffn_gain.reshape(1, cols))


def scatter_tok_kernel(
    tok_count,
    part_hbm,
    mixed_ref,
    gain_ref,
    out_ref,
    mine,
    chip_in,
    cross_out,
    cross_in,
    load_sem,
    send_sem,
    recv_sem,
):
    mesh_ids = pl.DeviceIdType.MESH
    me = lax.axis_index("tok")
    up = lax.rem(me + 2, tok_count)
    down = lax.rem(me + tok_count - 2, tok_count)
    far = lax.rem(me + 4, tok_count)
    partner = me + 1 - 2 * lax.rem(me, 2)
    share = out_ref.shape[0]

    barrier = pltpu.get_barrier_semaphore()
    for peer in (up, down, far, partner):
        pl.semaphore_signal(barrier, inc=1, device_id={"tok": peer}, device_id_type=mesh_ids)
    pl.semaphore_wait(barrier, 4)

    def remote(src, dst, slot, peer):
        return pltpu.make_async_remote_copy(
            src_ref=src,
            dst_ref=dst,
            send_sem=send_sem.at[slot],
            recv_sem=recv_sem.at[slot],
            device_id={"tok": peer},
            device_id_type=mesh_ids,
        )

    def family(base):
        return (
            base,
            lax.rem(base + 2, tok_count),
            lax.rem(base + tok_count - 2, tok_count),
            lax.rem(base + 4, tok_count),
        )

    def rows_of(block):
        return pl.ds(pl.multiple_of(block * share, share), share)

    order = (3, 1, 2, 0)
    sends = []
    theirs = family(partner)
    for idx in order:
        copy = remote(part_hbm.at[rows_of(theirs[idx])], chip_in.at[idx], idx, partner)
        copy.start()
        sends.append(copy)
    own = family(me)
    loads = []
    for idx in order:
        load = pltpu.make_async_copy(part_hbm.at[rows_of(own[idx])], mine.at[idx], load_sem.at[idx])
        load.start()
        loads.append(load)
    targets = {1: (up, 1), 2: (down, 0), 3: (far, 2)}
    for pos, idx in enumerate(order[:3]):
        loads[pos].wait()
        remote(part_hbm.at[rows_of(own[idx])], chip_in.at[idx], idx, partner).wait_recv()
        cross_out[idx - 1] = (mine[idx] + chip_in[idx]).astype(cross_out.dtype)
        peer, dst_idx = targets[idx]
        copy = remote(cross_out.at[idx - 1], cross_in.at[dst_idx], 4 + dst_idx, peer)
        copy.start()
        sends.append(copy)
    loads[3].wait()
    remote(part_hbm.at[rows_of(own[0])], chip_in.at[0], 0, partner).wait_recv()
    total = mine[0] + chip_in[0]
    for idx, peer in ((0, up), (1, down), (2, far)):
        remote(cross_out.at[idx], cross_in.at[idx], 4 + idx, peer).wait_recv()
    for idx in range(3):
        total = total + cross_in[idx].astype(jnp.float32)
    out_ref[...] = (mixed_ref[...] + rms_scale(total, gain_ref[...])).astype(out_ref.dtype)
    for copy in sends:
        copy.wait_send()


def scatter_over_tok(partial, mixed_share, gain, tok_count, collective_id):
    assert tok_count == 8
    rows, cols = partial.shape
    share = rows // tok_count
    vmem = pltpu.MemorySpace.VMEM
    return pl.pallas_call(
        lambda *refs: scatter_tok_kernel(tok_count, *refs),
        out_shape=jax.ShapeDtypeStruct((share, cols), jnp.bfloat16),
        in_specs=[
            pl.BlockSpec(memory_space=pltpu.MemorySpace.HBM),
            pl.BlockSpec(memory_space=vmem),
            pl.BlockSpec(memory_space=vmem),
        ],
        out_specs=pl.BlockSpec(memory_space=vmem),
        scratch_shapes=[
            pltpu.VMEM((4, share, cols), jnp.float32),
            pltpu.VMEM((4, share, cols), jnp.float32),
            pltpu.VMEM((3, share, cols), jnp.bfloat16),
            pltpu.VMEM((3, share, cols), jnp.bfloat16),
            pltpu.SemaphoreType.DMA((4,)),
            pltpu.SemaphoreType.DMA((7,)),
            pltpu.SemaphoreType.DMA((7,)),
        ],
        compiler_params=pltpu.CompilerParams(
            collective_id=collective_id, has_side_effects=True, vmem_limit_bytes=48 * 1024 * 1024
        ),
        cost_estimate=pl.CostEstimate(
            flops=8 * share * cols, transcendentals=0, bytes_accessed=rows * cols * 4 * 2
        ),
    )(partial, mixed_share, gain.reshape(1, cols))


def local(
    queries,
    suffix_kv,
    prefix_cache,
    q_gain,
    k_gain,
    lengths,
    group_of,
    owner_order,
    residual,
    w_out,
    attn_gain,
    ffn_in_gain,
    ffn_out_gain,
    w_gate,
    w_up,
    w_down,
):
    req_count = lax.axis_size("req")
    tok_count = lax.axis_size("tok")
    req_index = lax.axis_index("req")
    tok_index = lax.axis_index("tok")
    row_count = queries.shape[0]
    heads_here = queries.shape[1] // HD
    head_ratio = H // KVH
    kv_first = tok_index * heads_here // head_ratio
    kv_width = KVH * HD
    own_count = req_count // GROUPS

    with jax.named_scope("prefix_gather"):
        half_rows = prefix_cache.shape[0] // 2
        core = tok_index % 2
        first_row_kv = core * half_rows
        half_keys = lax.dynamic_slice(prefix_cache, (first_row_kv, kv_first * HD), (half_rows, HD))
        half_vals = lax.dynamic_slice(
            prefix_cache, (first_row_kv, kv_width + kv_first * HD), (half_rows, HD)
        )
        my_half = jnp.concatenate([half_keys, half_vals], axis=1)
        gathered = lax.all_gather(my_half, "req", axis=0, tiled=False)
        w_out_all = gather_over_tok(w_out, tok_count, 0)
        gathered, w_out_all = lax.optimization_barrier((gathered, w_out_all))
        own_group = group_of[req_index]
        owner_ids = lax.dynamic_slice_in_dim(owner_order, own_group * own_count, own_count)
        picked = jnp.take(gathered, owner_ids, axis=0, mode="clip").reshape(-1, 2 * HD)
        partner = [(t, t ^ 1) for t in range(tok_count)]
        swapped = lax.ppermute(picked, "tok", perm=partner)
        shared = jnp.concatenate([picked, swapped], axis=0)

    with jax.named_scope("attention"):
        query_normed = norm_heads(queries, q_gain, heads_here)
        suf_keys = norm_heads(
            lax.dynamic_slice_in_dim(suffix_kv, kv_first * HD, HD, 1), k_gain, 1
        )
        suf_vals = lax.dynamic_slice_in_dim(suffix_kv, kv_width + kv_first * HD, HD, 1)
        all_keys = jnp.concatenate([shared[:, :HD], suf_keys], axis=0)
        all_vals = jnp.concatenate([shared[:, HD:], suf_vals], axis=0)
        seg_ends = jnp.cumsum(lengths[0])
        positions = jnp.arange(row_count, dtype=jnp.int32)
        segment = jnp.sum((positions[:, None] >= seg_ends[None, :]).astype(jnp.int32), axis=1)
        causal = (segment[:, None] == segment[None, :]) & (positions[None, :] <= positions[:, None])
        visible = jnp.concatenate(
            [jnp.ones((row_count, shared.shape[0]), jnp.bool_), causal], axis=1
        )
        outputs = []
        for head_idx in range(heads_here):
            head_q = query_normed[:, head_idx * HD:(head_idx + 1) * HD]
            scores = jnp.dot(head_q, all_keys.T, preferred_element_type=jnp.float32) * HD ** (-0.5)
            scores = jnp.where(visible, scores, MASKED)
            row_max = jnp.max(scores, axis=-1, keepdims=True)
            weights = jnp.exp(scores - row_max)
            row_sum = jnp.sum(weights, axis=-1, keepdims=True)
            head_out = jnp.dot(
                weights.astype(jnp.bfloat16), all_vals, preferred_element_type=jnp.float32
            ) / row_sum
            outputs.append(head_out)
        attention = jnp.concatenate(outputs, axis=1).astype(jnp.bfloat16)

    share = row_count // tok_count
    first_row = tok_index * share
    with jax.named_scope("out_projection"):
        normed, mixed_share = project_over_tok(
            attention, w_out_all, residual, attn_gain, ffn_in_gain, tok_count, 1
        )
    with jax.named_scope("feed_forward"):
        normed = lax.optimization_barrier(normed)
        gate = jnp.dot(normed, w_gate, preferred_element_type=jnp.float32)
        upward = jnp.dot(normed, w_up, preferred_element_type=jnp.float32)
        hidden = (jax.nn.gelu(gate, approximate=True) * upward).astype(jnp.bfloat16)
        hidden = lax.optimization_barrier(hidden)
        return scatter_over_tok(
            jnp.dot(hidden, w_down, preferred_element_type=jnp.float32),
            mixed_share,
            ffn_out_gain,
            tok_count,
            2,
        )


def solution(mesh):
    in_specs = (
        P("req", "tok"),
        P("req", None),
        P("req", None),
        P(),
        P(),
        P("req", None),
        P(),
        P(),
        P("req", None),
        P("tok", None),
        P(),
        P(),
        P(),
        P(None, "tok"),
        P(None, "tok"),
        P("tok", None),
    )
    out_specs = P(("req", "tok"), None)
    return jax.shard_map(local, mesh=mesh, in_specs=in_specs, out_specs=out_specs, check_vma=False)
```

```python
import jax
import jax.numpy as jnp
from jax import lax
from jax.sharding import PartitionSpec as P
from jax.experimental import pallas as pl
from jax.experimental.pallas import tpu as pltpu

H = 8
KVH = 4
HD = 256
GROUPS = 2


EPSILON = 1e-06
MASKED = -1e30


def rms_scale(values_in, gain_vec):
    return (
        values_in
        * lax.rsqrt(jnp.mean(values_in * values_in, axis=-1, keepdims=True) + EPSILON)
        * gain_vec
    )


def norm_heads(values_in, gain_vec, head_count):
    row_count = values_in.shape[0]
    shaped = values_in.astype(jnp.float32).reshape(row_count, head_count, HD)
    return rms_scale(shaped, gain_vec).astype(jnp.bfloat16).reshape(row_count, head_count * HD)


def gather_tok_kernel(tok_count, w_ref, out_ref, send_sem, recv_sem, local_sem):
    mesh_ids = pl.DeviceIdType.MESH
    me = lax.axis_index("tok")
    up = lax.rem(me + 2, tok_count)
    down = lax.rem(me + tok_count - 2, tok_count)
    far = lax.rem(me + 4, tok_count)
    partner = me + 1 - 2 * lax.rem(me, 2)
    half = w_ref.shape[0] // 2

    barrier = pltpu.get_barrier_semaphore()
    for peer in (up, down, partner):
        pl.semaphore_signal(barrier, inc=1, device_id={"tok": peer}, device_id_type=mesh_ids)
    pl.semaphore_wait(barrier, 3)

    def remote(src, dst, slot, peer):
        return pltpu.make_async_remote_copy(
            src_ref=src,
            dst_ref=dst,
            send_sem=send_sem.at[slot],
            recv_sem=recv_sem.at[slot],
            device_id={"tok": peer},
            device_id_type=mesh_ids,
        )

    local = pltpu.make_async_copy(w_ref, out_ref.at[me], local_sem.at[0])
    local.start()
    sends = []

    def send(src, dst, slot, peer):
        copy = remote(src, dst, slot, peer)
        copy.start()
        sends.append(copy)

    send(w_ref, out_ref.at[me], 0, up)
    send(w_ref, out_ref.at[me], 1, down)
    send(w_ref, out_ref.at[me], 4, partner)
    remote(w_ref, out_ref.at[down], 0, down).wait_recv()
    remote(w_ref, out_ref.at[up], 1, up).wait_recv()

    first = pl.ds(0, half)
    second = pl.ds(half, half)
    send(out_ref.at[down, first], out_ref.at[down, first], 2, up)
    send(out_ref.at[up, second], out_ref.at[up, second], 3, down)
    send(out_ref.at[up], out_ref.at[up], 5, partner)
    send(out_ref.at[down], out_ref.at[down], 6, partner)
    remote(out_ref.at[far, first], out_ref.at[far, first], 2, down).wait_recv()
    remote(out_ref.at[far, second], out_ref.at[far, second], 3, up).wait_recv()
    send(out_ref.at[far], out_ref.at[far], 7, partner)
    local.wait()

    theirs = (
        partner,
        lax.rem(partner + 2, tok_count),
        lax.rem(partner + tok_count - 2, tok_count),
        lax.rem(partner + 4, tok_count),
    )
    for idx, slot in enumerate(theirs):
        remote(out_ref.at[slot], out_ref.at[slot], 4 + idx, partner).wait_recv()
    for copy in sends:
        copy.wait_send()


def gather_over_tok(block, tok_count, collective_id):
    assert tok_count == 8
    rows, cols = block.shape
    return pl.pallas_call(
        lambda *refs: gather_tok_kernel(tok_count, *refs),
        out_shape=jax.ShapeDtypeStruct((tok_count, rows, cols), block.dtype),
        in_specs=[pl.BlockSpec(memory_space=pl.ANY)],
        out_specs=pl.BlockSpec(memory_space=pl.ANY),
        scratch_shapes=[
            pltpu.SemaphoreType.DMA((8,)),
            pltpu.SemaphoreType.DMA((8,)),
            pltpu.SemaphoreType.DMA((1,)),
        ],
        compiler_params=pltpu.CompilerParams(collective_id=collective_id, has_side_effects=True),
        cost_estimate=pl.CostEstimate(
            flops=0, transcendentals=0, bytes_accessed=2 * tok_count * rows * cols * 2
        ),
    )(block)


def project_tok_kernel(
    tok_count,
    att_ref,
    w_hbm,
    res_ref,
    attn_gain_ref,
    ffn_gain_ref,
    normed_ref,
    mixed_ref,
    out_ref,
    att_all,
    w_buf,
    send_sem,
    recv_sem,
    load_sem,
):
    mesh_ids = pl.DeviceIdType.MESH
    me = lax.axis_index("tok")
    up = lax.rem(me + 2, tok_count)
    down = lax.rem(me + tok_count - 2, tok_count)
    far = lax.rem(me + 4, tok_count)
    partner = me + 1 - 2 * lax.rem(me, 2)
    half = att_ref.shape[0] // 2
    cols = out_ref.shape[1]
    tile = 512
    tiles = cols // tile

    barrier = pltpu.get_barrier_semaphore()
    for peer in (up, down, partner):
        pl.semaphore_signal(barrier, inc=1, device_id={"tok": peer}, device_id_type=mesh_ids)
    pl.semaphore_wait(barrier, 3)

    def remote(src, dst, slot, peer):
        return pltpu.make_async_remote_copy(
            src_ref=src,
            dst_ref=dst,
            send_sem=send_sem.at[slot],
            recv_sem=recv_sem.at[slot],
            device_id={"tok": peer},
            device_id_type=mesh_ids,
        )

    theirs = (
        partner,
        lax.rem(partner + 2, tok_count),
        lax.rem(partner + tok_count - 2, tok_count),
        lax.rem(partner + 4, tok_count),
    )
    order = (me, theirs[0], down, up, theirs[1], theirs[2], far, theirs[3])

    def load(idx):
        return pltpu.make_async_copy(w_hbm.at[order[idx]], w_buf.at[idx % 2], load_sem.at[idx % 2])

    def accumulate(idx, source, first):
        load(idx).wait()
        if idx + 1 < len(order):
            load(idx + 1).start()
        weights = w_buf.at[idx % 2]

        def one_tile(col):
            span = pl.ds(pl.multiple_of(col * tile, tile), tile)
            term = jnp.dot(source[...], weights[:, span], preferred_element_type=jnp.float32)
            if first:
                out_ref[:, span] = term
            else:
                out_ref[:, span] = out_ref[:, span] + term

        pl.loop(0, tiles)(one_tile)

    load(0).start()
    sends = []

    def send(src, slot, index, peer):
        copy = remote(src, att_all.at[slot], index, peer)
        copy.start()
        sends.append(copy)

    def arrived(slot, index, peer, rows=None):
        dst = att_all.at[slot] if rows is None else att_all.at[slot, rows]
        remote(dst, dst, index, peer).wait_recv()

    first = pl.ds(0, half)
    second = pl.ds(half, half)
    send(att_ref, me, 0, up)
    send(att_ref, me, 1, down)
    send(att_ref, me, 4, partner)
    accumulate(0, att_ref, True)
    arrived(theirs[0], 4, partner)
    accumulate(1, att_all.at[theirs[0]], False)
    arrived(down, 0, down)
    arrived(up, 1, up)
    for src, index, peer in ((att_all.at[down, first], 2, up), (att_all.at[up, second], 3, down)):
        copy = remote(src, src, index, peer)
        copy.start()
        sends.append(copy)
    send(att_all.at[up], up, 5, partner)
    send(att_all.at[down], down, 6, partner)
    accumulate(2, att_all.at[down], False)
    accumulate(3, att_all.at[up], False)
    for idx in range(1, 3):
        arrived(theirs[idx], 4 + idx, partner)
        accumulate(3 + idx, att_all.at[theirs[idx]], False)
    arrived(far, 2, down, first)
    arrived(far, 3, up, second)
    send(att_all.at[far], far, 7, partner)
    accumulate(6, att_all.at[far], False)
    arrived(theirs[3], 7, partner)
    accumulate(7, att_all.at[theirs[3]], False)

    share = mixed_ref.shape[0]

    def finish(block):
        rows = pl.ds(pl.multiple_of(block * share, share), share)
        mixed = res_ref[rows, :].astype(jnp.float32) + rms_scale(out_ref[rows, :], attn_gain_ref[...])
        normed_ref[rows, :] = rms_scale(mixed, ffn_gain_ref[...]).astype(normed_ref.dtype)

    pl.loop(0, out_ref.shape[0] // share)(finish)
    own_rows = pl.ds(pl.multiple_of(me * share, share), share)
    mixed_ref[...] = res_ref[own_rows, :].astype(jnp.float32) + rms_scale(
        out_ref[own_rows, :], attn_gain_ref[...]
    )
    for copy in sends:
        copy.wait_send()


def project_over_tok(attention, w_all, residual, attn_gain, ffn_gain, tok_count, collective_id):
    assert tok_count == 8
    rows, width = attention.shape
    cols = w_all.shape[2]
    share = rows // tok_count
    vmem = pltpu.MemorySpace.VMEM
    vmem_spec = pl.BlockSpec(memory_space=vmem)
    return pl.pallas_call(
        lambda *refs: project_tok_kernel(tok_count, *refs),
        out_shape=(
            jax.ShapeDtypeStruct((rows, cols), jnp.bfloat16),
            jax.ShapeDtypeStruct((share, cols), jnp.float32),
        ),
        in_specs=[vmem_spec, pl.BlockSpec(memory_space=pl.ANY), vmem_spec, vmem_spec, vmem_spec],
        out_specs=(vmem_spec, vmem_spec),
        scratch_shapes=[
            pltpu.VMEM((rows, cols), jnp.float32),
            pltpu.VMEM((tok_count, rows, width), attention.dtype),
            pltpu.VMEM((2, width, cols), w_all.dtype),
            pltpu.SemaphoreType.DMA((8,)),
            pltpu.SemaphoreType.DMA((8,)),
            pltpu.SemaphoreType.DMA((2,)),
        ],
        compiler_params=pltpu.CompilerParams(
            collective_id=collective_id, has_side_effects=True, vmem_limit_bytes=48 * 1024 * 1024
        ),
        cost_estimate=pl.CostEstimate(
            flops=2 * rows * width * tok_count * cols,
            transcendentals=2 * rows,
            bytes_accessed=tok_count * width * cols * 2 + rows * cols * 4,
        ),
    )(attention, w_all, residual, attn_gain.reshape(1, cols), ffn_gain.reshape(1, cols))


def scatter_tok_kernel(
    tok_count, part_hbm, out_ref, mine, chip_in, cross_out, cross_in, load_sem, send_sem, recv_sem
):
    mesh_ids = pl.DeviceIdType.MESH
    me = lax.axis_index("tok")
    up = lax.rem(me + 2, tok_count)
    down = lax.rem(me + tok_count - 2, tok_count)
    far = lax.rem(me + 4, tok_count)
    partner = me + 1 - 2 * lax.rem(me, 2)
    share = out_ref.shape[0]

    barrier = pltpu.get_barrier_semaphore()
    for peer in (up, down, far, partner):
        pl.semaphore_signal(barrier, inc=1, device_id={"tok": peer}, device_id_type=mesh_ids)
    pl.semaphore_wait(barrier, 4)

    def remote(src, dst, slot, peer):
        return pltpu.make_async_remote_copy(
            src_ref=src,
            dst_ref=dst,
            send_sem=send_sem.at[slot],
            recv_sem=recv_sem.at[slot],
            device_id={"tok": peer},
            device_id_type=mesh_ids,
        )

    def family(base):
        return (
            base,
            lax.rem(base + 2, tok_count),
            lax.rem(base + tok_count - 2, tok_count),
            lax.rem(base + 4, tok_count),
        )

    def rows_of(block):
        return pl.ds(pl.multiple_of(block * share, share), share)

    order = (3, 1, 2, 0)
    sends = []
    theirs = family(partner)
    for idx in order:
        copy = remote(part_hbm.at[rows_of(theirs[idx])], chip_in.at[idx], idx, partner)
        copy.start()
        sends.append(copy)
    own = family(me)
    loads = []
    for idx in order:
        load = pltpu.make_async_copy(part_hbm.at[rows_of(own[idx])], mine.at[idx], load_sem.at[idx])
        load.start()
        loads.append(load)
    targets = {1: (up, 1), 2: (down, 0), 3: (far, 2)}
    for pos, idx in enumerate(order[:3]):
        loads[pos].wait()
        remote(part_hbm.at[rows_of(own[idx])], chip_in.at[idx], idx, partner).wait_recv()
        cross_out[idx - 1] = (mine[idx] + chip_in[idx]).astype(cross_out.dtype)
        peer, dst_idx = targets[idx]
        copy = remote(cross_out.at[idx - 1], cross_in.at[dst_idx], 4 + dst_idx, peer)
        copy.start()
        sends.append(copy)
    loads[3].wait()
    remote(part_hbm.at[rows_of(own[0])], chip_in.at[0], 0, partner).wait_recv()
    total = mine[0] + chip_in[0]
    for idx, peer in ((0, up), (1, down), (2, far)):
        remote(cross_out.at[idx], cross_in.at[idx], 4 + idx, peer).wait_recv()
    for idx in range(3):
        total = total + cross_in[idx].astype(jnp.float32)
    out_ref[...] = total
    for copy in sends:
        copy.wait_send()


def scatter_over_tok(partial, tok_count, collective_id):
    assert tok_count == 8
    rows, cols = partial.shape
    share = rows // tok_count
    vmem = pltpu.MemorySpace.VMEM
    return pl.pallas_call(
        lambda *refs: scatter_tok_kernel(tok_count, *refs),
        out_shape=jax.ShapeDtypeStruct((share, cols), jnp.float32),
        in_specs=[pl.BlockSpec(memory_space=pltpu.MemorySpace.HBM)],
        out_specs=pl.BlockSpec(memory_space=vmem),
        scratch_shapes=[
            pltpu.VMEM((4, share, cols), jnp.float32),
            pltpu.VMEM((4, share, cols), jnp.float32),
            pltpu.VMEM((3, share, cols), jnp.bfloat16),
            pltpu.VMEM((3, share, cols), jnp.bfloat16),
            pltpu.SemaphoreType.DMA((4,)),
            pltpu.SemaphoreType.DMA((7,)),
            pltpu.SemaphoreType.DMA((7,)),
        ],
        compiler_params=pltpu.CompilerParams(
            collective_id=collective_id, has_side_effects=True, vmem_limit_bytes=48 * 1024 * 1024
        ),
        cost_estimate=pl.CostEstimate(
            flops=8 * share * cols, transcendentals=0, bytes_accessed=rows * cols * 4 * 2
        ),
    )(partial)


def local(
    queries,
    suffix_kv,
    prefix_cache,
    q_gain,
    k_gain,
    lengths,
    group_of,
    owner_order,
    residual,
    w_out,
    attn_gain,
    ffn_in_gain,
    ffn_out_gain,
    w_gate,
    w_up,
    w_down,
):
    req_count = lax.axis_size("req")
    tok_count = lax.axis_size("tok")
    req_index = lax.axis_index("req")
    tok_index = lax.axis_index("tok")
    row_count = queries.shape[0]
    heads_here = queries.shape[1] // HD
    head_ratio = H // KVH
    kv_first = tok_index * heads_here // head_ratio
    kv_width = KVH * HD
    own_count = req_count // GROUPS

    with jax.named_scope("prefix_gather"):
        half_rows = prefix_cache.shape[0] // 2
        core = tok_index % 2
        first_row_kv = core * half_rows
        half_keys = lax.dynamic_slice(prefix_cache, (first_row_kv, kv_first * HD), (half_rows, HD))
        half_vals = lax.dynamic_slice(
            prefix_cache, (first_row_kv, kv_width + kv_first * HD), (half_rows, HD)
        )
        my_half = jnp.concatenate([half_keys, half_vals], axis=1)
        gathered = lax.all_gather(my_half, "req", axis=0, tiled=False)
        w_out_all = gather_over_tok(w_out, tok_count, 0)
        gathered, w_out_all = lax.optimization_barrier((gathered, w_out_all))
        own_group = jnp.sum(jnp.where(jnp.arange(req_count) == req_index, group_of, 0))
        owner_ids = lax.dynamic_slice_in_dim(owner_order, own_group * own_count, own_count)
        picked = jnp.take(gathered, owner_ids, axis=0, mode="clip").reshape(-1, 2 * HD)
        partner = [(t, t ^ 1) for t in range(tok_count)]
        swapped = lax.ppermute(picked, "tok", perm=partner)
        shared = jnp.concatenate([picked, swapped], axis=0)

    with jax.named_scope("attention"):
        query_normed = norm_heads(queries, q_gain, heads_here)
        suf_keys = norm_heads(
            lax.dynamic_slice_in_dim(suffix_kv, kv_first * HD, HD, 1), k_gain, 1
        )
        suf_vals = lax.dynamic_slice_in_dim(suffix_kv, kv_width + kv_first * HD, HD, 1)
        all_keys = jnp.concatenate([shared[:, :HD], suf_keys], axis=0)
        all_vals = jnp.concatenate([shared[:, HD:], suf_vals], axis=0)
        seg_ends = jnp.cumsum(lengths[0])
        positions = jnp.arange(row_count, dtype=jnp.int32)
        segment = jnp.sum((positions[:, None] >= seg_ends[None, :]).astype(jnp.int32), axis=1)
        causal = (segment[:, None] == segment[None, :]) & (positions[None, :] <= positions[:, None])
        visible = jnp.concatenate(
            [jnp.ones((row_count, shared.shape[0]), jnp.bool_), causal], axis=1
        )
        outputs = []
        for head_idx in range(heads_here):
            head_q = query_normed[:, head_idx * HD:(head_idx + 1) * HD]
            scores = jnp.dot(head_q, all_keys.T, preferred_element_type=jnp.float32) * HD ** (-0.5)
            scores = jnp.where(visible, scores, MASKED)
            row_max = jnp.max(scores, axis=-1, keepdims=True)
            weights = jnp.exp(scores - row_max)
            row_sum = jnp.sum(weights, axis=-1, keepdims=True)
            head_out = jnp.dot(
                weights.astype(jnp.bfloat16), all_vals, preferred_element_type=jnp.float32
            ) / row_sum
            outputs.append(head_out)
        attention = jnp.concatenate(outputs, axis=1).astype(jnp.bfloat16)

    share = row_count // tok_count
    first_row = tok_index * share
    with jax.named_scope("out_projection"):
        normed, mixed_share = project_over_tok(
            attention, w_out_all, residual, attn_gain, ffn_in_gain, tok_count, 1
        )
    with jax.named_scope("feed_forward"):
        normed = lax.optimization_barrier(normed)
        gate = jnp.dot(normed, w_gate, preferred_element_type=jnp.float32)
        upward = jnp.dot(normed, w_up, preferred_element_type=jnp.float32)
        hidden = (jax.nn.gelu(gate, approximate=True) * upward).astype(jnp.bfloat16)
        hidden = lax.optimization_barrier(hidden)
        down_share = scatter_over_tok(
            jnp.dot(hidden, w_down, preferred_element_type=jnp.float32), tok_count, 2
        )
    return (mixed_share + rms_scale(down_share.astype(jnp.float32), ffn_out_gain)).astype(
        jnp.bfloat16
    )


def solution(mesh):
    in_specs = (
        P("req", "tok"),
        P("req", None),
        P("req", None),
        P(),
        P(),
        P("req", None),
        P(),
        P(),
        P("req", None),
        P("tok", None),
        P(),
        P(),
        P(),
        P(None, "tok"),
        P(None, "tok"),
        P("tok", None),
    )
    out_specs = P(("req", "tok"), None)
    return jax.shard_map(local, mesh=mesh, in_specs=in_specs, out_specs=out_specs, check_vma=False)
```

```python
import jax
import jax.numpy as jnp
from jax import lax
from jax.sharding import PartitionSpec as P
from jax.experimental import pallas as pl
from jax.experimental.pallas import tpu as pltpu

H = 8
KVH = 4
HD = 256
GROUPS = 2


EPSILON = 1e-06
MASKED = -1e30


def rms_scale(values_in, gain_vec):
    return (
        values_in
        * lax.rsqrt(jnp.mean(values_in * values_in, axis=-1, keepdims=True) + EPSILON)
        * gain_vec
    )


def norm_heads(values_in, gain_vec, head_count):
    row_count = values_in.shape[0]
    shaped = values_in.astype(jnp.float32).reshape(row_count, head_count, HD)
    return rms_scale(shaped, gain_vec).astype(jnp.bfloat16).reshape(row_count, head_count * HD)


def gather_tok_kernel(tok_count, w_ref, out_ref, send_sem, recv_sem, local_sem):
    mesh_ids = pl.DeviceIdType.MESH
    me = lax.axis_index("tok")
    up = lax.rem(me + 2, tok_count)
    down = lax.rem(me + tok_count - 2, tok_count)
    far = lax.rem(me + 4, tok_count)
    partner = me + 1 - 2 * lax.rem(me, 2)
    half = w_ref.shape[0] // 2

    barrier = pltpu.get_barrier_semaphore()
    for peer in (up, down, partner):
        pl.semaphore_signal(barrier, inc=1, device_id={"tok": peer}, device_id_type=mesh_ids)
    pl.semaphore_wait(barrier, 3)

    def remote(src, dst, slot, peer):
        return pltpu.make_async_remote_copy(
            src_ref=src,
            dst_ref=dst,
            send_sem=send_sem.at[slot],
            recv_sem=recv_sem.at[slot],
            device_id={"tok": peer},
            device_id_type=mesh_ids,
        )

    local = pltpu.make_async_copy(w_ref, out_ref.at[me], local_sem.at[0])
    local.start()
    sends = []

    def send(src, dst, slot, peer):
        copy = remote(src, dst, slot, peer)
        copy.start()
        sends.append(copy)

    send(w_ref, out_ref.at[me], 0, up)
    send(w_ref, out_ref.at[me], 1, down)
    send(w_ref, out_ref.at[me], 4, partner)
    remote(w_ref, out_ref.at[down], 0, down).wait_recv()
    remote(w_ref, out_ref.at[up], 1, up).wait_recv()

    first = pl.ds(0, half)
    second = pl.ds(half, half)
    send(out_ref.at[down, first], out_ref.at[down, first], 2, up)
    send(out_ref.at[up, second], out_ref.at[up, second], 3, down)
    send(out_ref.at[up], out_ref.at[up], 5, partner)
    send(out_ref.at[down], out_ref.at[down], 6, partner)
    remote(out_ref.at[far, first], out_ref.at[far, first], 2, down).wait_recv()
    remote(out_ref.at[far, second], out_ref.at[far, second], 3, up).wait_recv()
    send(out_ref.at[far], out_ref.at[far], 7, partner)
    local.wait()

    theirs = (
        partner,
        lax.rem(partner + 2, tok_count),
        lax.rem(partner + tok_count - 2, tok_count),
        lax.rem(partner + 4, tok_count),
    )
    for idx, slot in enumerate(theirs):
        remote(out_ref.at[slot], out_ref.at[slot], 4 + idx, partner).wait_recv()
    for copy in sends:
        copy.wait_send()


def gather_over_tok(block, tok_count, collective_id):
    assert tok_count == 8
    rows, cols = block.shape
    return pl.pallas_call(
        lambda *refs: gather_tok_kernel(tok_count, *refs),
        out_shape=jax.ShapeDtypeStruct((tok_count, rows, cols), block.dtype),
        in_specs=[pl.BlockSpec(memory_space=pl.ANY)],
        out_specs=pl.BlockSpec(memory_space=pl.ANY),
        scratch_shapes=[
            pltpu.SemaphoreType.DMA((8,)),
            pltpu.SemaphoreType.DMA((8,)),
            pltpu.SemaphoreType.DMA((1,)),
        ],
        compiler_params=pltpu.CompilerParams(collective_id=collective_id, has_side_effects=True),
        cost_estimate=pl.CostEstimate(
            flops=0, transcendentals=0, bytes_accessed=2 * tok_count * rows * cols * 2
        ),
    )(block)


def project_tok_kernel(
    tok_count,
    att_ref,
    w_hbm,
    res_ref,
    attn_gain_ref,
    ffn_gain_ref,
    normed_ref,
    mixed_ref,
    out_ref,
    att_all,
    w_buf,
    send_sem,
    recv_sem,
    load_sem,
):
    mesh_ids = pl.DeviceIdType.MESH
    me = lax.axis_index("tok")
    up = lax.rem(me + 2, tok_count)
    down = lax.rem(me + tok_count - 2, tok_count)
    far = lax.rem(me + 4, tok_count)
    partner = me + 1 - 2 * lax.rem(me, 2)
    half = att_ref.shape[0] // 2
    cols = out_ref.shape[1]
    tile = 512
    tiles = cols // tile


    def remote(src, dst, slot, peer):
        return pltpu.make_async_remote_copy(
            src_ref=src,
            dst_ref=dst,
            send_sem=send_sem.at[slot],
            recv_sem=recv_sem.at[slot],
            device_id={"tok": peer},
            device_id_type=mesh_ids,
        )

    theirs = (
        partner,
        lax.rem(partner + 2, tok_count),
        lax.rem(partner + tok_count - 2, tok_count),
        lax.rem(partner + 4, tok_count),
    )
    order = (me, theirs[0], down, up, theirs[1], theirs[2], far, theirs[3])

    def load(idx):
        return pltpu.make_async_copy(w_hbm.at[order[idx]], w_buf.at[idx % 2], load_sem.at[idx % 2])

    def accumulate(idx, source, first):
        load(idx).wait()
        if idx + 1 < len(order):
            load(idx + 1).start()
        weights = w_buf.at[idx % 2]

        def one_tile(col):
            span = pl.ds(pl.multiple_of(col * tile, tile), tile)
            term = jnp.dot(source[...], weights[:, span], preferred_element_type=jnp.float32)
            if first:
                out_ref[:, span] = term
            else:
                out_ref[:, span] = out_ref[:, span] + term

        pl.loop(0, tiles)(one_tile)

    load(0).start()
    barrier = pltpu.get_barrier_semaphore()
    for peer in (up, down, partner):
        pl.semaphore_signal(barrier, inc=1, device_id={"tok": peer}, device_id_type=mesh_ids)
    pl.semaphore_wait(barrier, 3)
    sends = []

    def send(src, slot, index, peer):
        copy = remote(src, att_all.at[slot], index, peer)
        copy.start()
        sends.append(copy)

    def arrived(slot, index, peer, rows=None):
        dst = att_all.at[slot] if rows is None else att_all.at[slot, rows]
        remote(dst, dst, index, peer).wait_recv()

    first = pl.ds(0, half)
    second = pl.ds(half, half)
    send(att_ref, me, 0, up)
    send(att_ref, me, 1, down)
    send(att_ref, me, 4, partner)
    accumulate(0, att_ref, True)
    arrived(theirs[0], 4, partner)
    accumulate(1, att_all.at[theirs[0]], False)
    arrived(down, 0, down)
    arrived(up, 1, up)
    for src, index, peer in ((att_all.at[down, first], 2, up), (att_all.at[up, second], 3, down)):
        copy = remote(src, src, index, peer)
        copy.start()
        sends.append(copy)
    send(att_all.at[up], up, 5, partner)
    send(att_all.at[down], down, 6, partner)
    accumulate(2, att_all.at[down], False)
    accumulate(3, att_all.at[up], False)
    for idx in range(1, 3):
        arrived(theirs[idx], 4 + idx, partner)
        accumulate(3 + idx, att_all.at[theirs[idx]], False)
    arrived(far, 2, down, first)
    arrived(far, 3, up, second)
    send(att_all.at[far], far, 7, partner)
    accumulate(6, att_all.at[far], False)
    arrived(theirs[3], 7, partner)
    accumulate(7, att_all.at[theirs[3]], False)

    share = mixed_ref.shape[0]

    def finish(block):
        rows = pl.ds(pl.multiple_of(block * share, share), share)
        mixed = res_ref[rows, :].astype(jnp.float32) + rms_scale(out_ref[rows, :], attn_gain_ref[...])
        normed_ref[rows, :] = rms_scale(mixed, ffn_gain_ref[...]).astype(normed_ref.dtype)

    pl.loop(0, out_ref.shape[0] // share)(finish)
    own_rows = pl.ds(pl.multiple_of(me * share, share), share)
    mixed_ref[...] = res_ref[own_rows, :].astype(jnp.float32) + rms_scale(
        out_ref[own_rows, :], attn_gain_ref[...]
    )
    for copy in sends:
        copy.wait_send()


def project_over_tok(attention, w_all, residual, attn_gain, ffn_gain, tok_count, collective_id):
    assert tok_count == 8
    rows, width = attention.shape
    cols = w_all.shape[2]
    share = rows // tok_count
    vmem = pltpu.MemorySpace.VMEM
    vmem_spec = pl.BlockSpec(memory_space=vmem)
    return pl.pallas_call(
        lambda *refs: project_tok_kernel(tok_count, *refs),
        out_shape=(
            jax.ShapeDtypeStruct((rows, cols), jnp.bfloat16),
            jax.ShapeDtypeStruct((share, cols), jnp.float32),
        ),
        in_specs=[vmem_spec, pl.BlockSpec(memory_space=pl.ANY), vmem_spec, vmem_spec, vmem_spec],
        out_specs=(vmem_spec, vmem_spec),
        scratch_shapes=[
            pltpu.VMEM((rows, cols), jnp.float32),
            pltpu.VMEM((tok_count, rows, width), attention.dtype),
            pltpu.VMEM((2, width, cols), w_all.dtype),
            pltpu.SemaphoreType.DMA((8,)),
            pltpu.SemaphoreType.DMA((8,)),
            pltpu.SemaphoreType.DMA((2,)),
        ],
        compiler_params=pltpu.CompilerParams(
            collective_id=collective_id, has_side_effects=True, vmem_limit_bytes=48 * 1024 * 1024
        ),
        cost_estimate=pl.CostEstimate(
            flops=2 * rows * width * tok_count * cols,
            transcendentals=2 * rows,
            bytes_accessed=tok_count * width * cols * 2 + rows * cols * 4,
        ),
    )(attention, w_all, residual, attn_gain.reshape(1, cols), ffn_gain.reshape(1, cols))


def scatter_tok_kernel(
    tok_count, part_hbm, out_ref, mine, chip_in, cross_out, cross_in, load_sem, send_sem, recv_sem
):
    mesh_ids = pl.DeviceIdType.MESH
    me = lax.axis_index("tok")
    up = lax.rem(me + 2, tok_count)
    down = lax.rem(me + tok_count - 2, tok_count)
    far = lax.rem(me + 4, tok_count)
    partner = me + 1 - 2 * lax.rem(me, 2)
    share = out_ref.shape[0]


    def remote(src, dst, slot, peer):
        return pltpu.make_async_remote_copy(
            src_ref=src,
            dst_ref=dst,
            send_sem=send_sem.at[slot],
            recv_sem=recv_sem.at[slot],
            device_id={"tok": peer},
            device_id_type=mesh_ids,
        )

    def family(base):
        return (
            base,
            lax.rem(base + 2, tok_count),
            lax.rem(base + tok_count - 2, tok_count),
            lax.rem(base + 4, tok_count),
        )

    def rows_of(block):
        return pl.ds(pl.multiple_of(block * share, share), share)

    order = (3, 1, 2, 0)
    own = family(me)
    loads = []
    for idx in order:
        load = pltpu.make_async_copy(part_hbm.at[rows_of(own[idx])], mine.at[idx], load_sem.at[idx])
        load.start()
        loads.append(load)
    barrier = pltpu.get_barrier_semaphore()
    for peer in (up, down, far, partner):
        pl.semaphore_signal(barrier, inc=1, device_id={"tok": peer}, device_id_type=mesh_ids)
    pl.semaphore_wait(barrier, 4)
    sends = []
    theirs = family(partner)
    for idx in order:
        copy = remote(part_hbm.at[rows_of(theirs[idx])], chip_in.at[idx], idx, partner)
        copy.start()
        sends.append(copy)
    targets = {1: (up, 1), 2: (down, 0), 3: (far, 2)}
    for pos, idx in enumerate(order[:3]):
        loads[pos].wait()
        remote(part_hbm.at[rows_of(own[idx])], chip_in.at[idx], idx, partner).wait_recv()
        cross_out[idx - 1] = (mine[idx] + chip_in[idx]).astype(cross_out.dtype)
        peer, dst_idx = targets[idx]
        copy = remote(cross_out.at[idx - 1], cross_in.at[dst_idx], 4 + dst_idx, peer)
        copy.start()
        sends.append(copy)
    loads[3].wait()
    remote(part_hbm.at[rows_of(own[0])], chip_in.at[0], 0, partner).wait_recv()
    total = mine[0] + chip_in[0]
    for idx, peer in ((0, up), (1, down), (2, far)):
        remote(cross_out.at[idx], cross_in.at[idx], 4 + idx, peer).wait_recv()
    for idx in range(3):
        total = total + cross_in[idx].astype(jnp.float32)
    out_ref[...] = total
    for copy in sends:
        copy.wait_send()


def scatter_over_tok(partial, tok_count, collective_id):
    assert tok_count == 8
    rows, cols = partial.shape
    share = rows // tok_count
    vmem = pltpu.MemorySpace.VMEM
    return pl.pallas_call(
        lambda *refs: scatter_tok_kernel(tok_count, *refs),
        out_shape=jax.ShapeDtypeStruct((share, cols), jnp.float32),
        in_specs=[pl.BlockSpec(memory_space=pltpu.MemorySpace.HBM)],
        out_specs=pl.BlockSpec(memory_space=vmem),
        scratch_shapes=[
            pltpu.VMEM((4, share, cols), jnp.float32),
            pltpu.VMEM((4, share, cols), jnp.float32),
            pltpu.VMEM((3, share, cols), jnp.bfloat16),
            pltpu.VMEM((3, share, cols), jnp.bfloat16),
            pltpu.SemaphoreType.DMA((4,)),
            pltpu.SemaphoreType.DMA((7,)),
            pltpu.SemaphoreType.DMA((7,)),
        ],
        compiler_params=pltpu.CompilerParams(
            collective_id=collective_id, has_side_effects=True, vmem_limit_bytes=48 * 1024 * 1024
        ),
        cost_estimate=pl.CostEstimate(
            flops=8 * share * cols, transcendentals=0, bytes_accessed=rows * cols * 4 * 2
        ),
    )(partial)


def local(
    queries,
    suffix_kv,
    prefix_cache,
    q_gain,
    k_gain,
    lengths,
    group_of,
    owner_order,
    residual,
    w_out,
    attn_gain,
    ffn_in_gain,
    ffn_out_gain,
    w_gate,
    w_up,
    w_down,
):
    req_count = lax.axis_size("req")
    tok_count = lax.axis_size("tok")
    req_index = lax.axis_index("req")
    tok_index = lax.axis_index("tok")
    row_count = queries.shape[0]
    heads_here = queries.shape[1] // HD
    head_ratio = H // KVH
    kv_first = tok_index * heads_here // head_ratio
    kv_width = KVH * HD
    own_count = req_count // GROUPS

    with jax.named_scope("prefix_gather"):
        half_rows = prefix_cache.shape[0] // 2
        core = tok_index % 2
        first_row_kv = core * half_rows
        half_keys = lax.dynamic_slice(prefix_cache, (first_row_kv, kv_first * HD), (half_rows, HD))
        half_vals = lax.dynamic_slice(
            prefix_cache, (first_row_kv, kv_width + kv_first * HD), (half_rows, HD)
        )
        my_half = jnp.concatenate([half_keys, half_vals], axis=1)
        gathered = lax.all_gather(my_half, "req", axis=0, tiled=False)
        w_out_all = gather_over_tok(w_out, tok_count, 0)
        gathered, w_out_all = lax.optimization_barrier((gathered, w_out_all))
        own_group = group_of[req_index]
        owner_ids = lax.dynamic_slice_in_dim(owner_order, own_group * own_count, own_count)
        picked = jnp.take(gathered, owner_ids, axis=0, mode="clip").reshape(-1, 2 * HD)
        partner = [(t, t ^ 1) for t in range(tok_count)]
        swapped = lax.ppermute(picked, "tok", perm=partner)
        shared = jnp.concatenate([picked, swapped], axis=0)

    with jax.named_scope("attention"):
        query_normed = norm_heads(queries, q_gain, heads_here)
        suf_keys = norm_heads(
            lax.dynamic_slice_in_dim(suffix_kv, kv_first * HD, HD, 1), k_gain, 1
        )
        suf_vals = lax.dynamic_slice_in_dim(suffix_kv, kv_width + kv_first * HD, HD, 1)
        all_keys = jnp.concatenate([shared[:, :HD], suf_keys], axis=0)
        all_vals = jnp.concatenate([shared[:, HD:], suf_vals], axis=0)
        seg_ends = jnp.cumsum(lengths[0])
        positions = jnp.arange(row_count, dtype=jnp.int32)
        segment = jnp.sum((positions[:, None] >= seg_ends[None, :]).astype(jnp.int32), axis=1)
        causal = (segment[:, None] == segment[None, :]) & (positions[None, :] <= positions[:, None])
        visible = jnp.concatenate(
            [jnp.ones((row_count, shared.shape[0]), jnp.bool_), causal], axis=1
        )
        outputs = []
        for head_idx in range(heads_here):
            head_q = query_normed[:, head_idx * HD:(head_idx + 1) * HD]
            scores = jnp.dot(head_q, all_keys.T, preferred_element_type=jnp.float32) * HD ** (-0.5)
            scores = jnp.where(visible, scores, MASKED)
            row_max = jnp.max(scores, axis=-1, keepdims=True)
            weights = jnp.exp(scores - row_max)
            row_sum = jnp.sum(weights, axis=-1, keepdims=True)
            head_out = jnp.dot(
                weights.astype(jnp.bfloat16), all_vals, preferred_element_type=jnp.float32
            ) / row_sum
            outputs.append(head_out)
        attention = jnp.concatenate(outputs, axis=1).astype(jnp.bfloat16)

    share = row_count // tok_count
    first_row = tok_index * share
    with jax.named_scope("out_projection"):
        normed, mixed_share = project_over_tok(
            attention, w_out_all, residual, attn_gain, ffn_in_gain, tok_count, 1
        )
    with jax.named_scope("feed_forward"):
        normed = lax.optimization_barrier(normed)
        gate = jnp.dot(normed, w_gate, preferred_element_type=jnp.float32)
        upward = jnp.dot(normed, w_up, preferred_element_type=jnp.float32)
        hidden = (jax.nn.gelu(gate, approximate=True) * upward).astype(jnp.bfloat16)
        hidden = lax.optimization_barrier(hidden)
        down_share = scatter_over_tok(
            jnp.dot(hidden, w_down, preferred_element_type=jnp.float32), tok_count, 2
        )
    return (mixed_share + rms_scale(down_share.astype(jnp.float32), ffn_out_gain)).astype(
        jnp.bfloat16
    )


def solution(mesh):
    in_specs = (
        P("req", "tok"),
        P("req", None),
        P("req", None),
        P(),
        P(),
        P("req", None),
        P(),
        P(),
        P("req", None),
        P("tok", None),
        P(),
        P(),
        P(),
        P(None, "tok"),
        P(None, "tok"),
        P("tok", None),
    )
    out_specs = P(("req", "tok"), None)
    return jax.shard_map(local, mesh=mesh, in_specs=in_specs, out_specs=out_specs, check_vma=False)
```

```python
import jax
import jax.numpy as jnp
from jax import lax
from jax.sharding import PartitionSpec as P
from jax.experimental import pallas as pl
from jax.experimental.pallas import tpu as pltpu

H = 8
KVH = 4
HD = 256
GROUPS = 2


EPSILON = 1e-06
MASKED = -1e30


def rms_scale(values_in, gain_vec):
    return (
        values_in
        * lax.rsqrt(jnp.mean(values_in * values_in, axis=-1, keepdims=True) + EPSILON)
        * gain_vec
    )


def norm_heads(values_in, gain_vec, head_count):
    row_count = values_in.shape[0]
    shaped = values_in.astype(jnp.float32).reshape(row_count, head_count, HD)
    return rms_scale(shaped, gain_vec).astype(jnp.bfloat16).reshape(row_count, head_count * HD)


def gather_tok_kernel(tok_count, w_ref, out_ref, send_sem, recv_sem, local_sem):
    mesh_ids = pl.DeviceIdType.MESH
    me = lax.axis_index("tok")
    up = lax.rem(me + 2, tok_count)
    down = lax.rem(me + tok_count - 2, tok_count)
    far = lax.rem(me + 4, tok_count)
    partner = me + 1 - 2 * lax.rem(me, 2)
    half = w_ref.shape[0] // 2

    barrier = pltpu.get_barrier_semaphore()
    for peer in (up, down, partner):
        pl.semaphore_signal(barrier, inc=1, device_id={"tok": peer}, device_id_type=mesh_ids)
    pl.semaphore_wait(barrier, 3)

    def remote(src, dst, slot, peer):
        return pltpu.make_async_remote_copy(
            src_ref=src,
            dst_ref=dst,
            send_sem=send_sem.at[slot],
            recv_sem=recv_sem.at[slot],
            device_id={"tok": peer},
            device_id_type=mesh_ids,
        )

    local = pltpu.make_async_copy(w_ref, out_ref.at[me], local_sem.at[0])
    local.start()
    sends = []

    def send(src, dst, slot, peer):
        copy = remote(src, dst, slot, peer)
        copy.start()
        sends.append(copy)

    send(w_ref, out_ref.at[me], 0, up)
    send(w_ref, out_ref.at[me], 1, down)
    send(w_ref, out_ref.at[me], 4, partner)
    remote(w_ref, out_ref.at[down], 0, down).wait_recv()
    remote(w_ref, out_ref.at[up], 1, up).wait_recv()

    first = pl.ds(0, half)
    second = pl.ds(half, half)
    send(out_ref.at[down, first], out_ref.at[down, first], 2, up)
    send(out_ref.at[up, second], out_ref.at[up, second], 3, down)
    send(out_ref.at[up], out_ref.at[up], 5, partner)
    send(out_ref.at[down], out_ref.at[down], 6, partner)
    remote(out_ref.at[far, first], out_ref.at[far, first], 2, down).wait_recv()
    remote(out_ref.at[far, second], out_ref.at[far, second], 3, up).wait_recv()
    send(out_ref.at[far], out_ref.at[far], 7, partner)
    local.wait()

    theirs = (
        partner,
        lax.rem(partner + 2, tok_count),
        lax.rem(partner + tok_count - 2, tok_count),
        lax.rem(partner + 4, tok_count),
    )
    for idx, slot in enumerate(theirs):
        remote(out_ref.at[slot], out_ref.at[slot], 4 + idx, partner).wait_recv()
    for copy in sends:
        copy.wait_send()


def gather_over_tok(block, tok_count, collective_id):
    assert tok_count == 8
    rows, cols = block.shape
    return pl.pallas_call(
        lambda *refs: gather_tok_kernel(tok_count, *refs),
        out_shape=jax.ShapeDtypeStruct((tok_count, rows, cols), block.dtype),
        in_specs=[pl.BlockSpec(memory_space=pl.ANY)],
        out_specs=pl.BlockSpec(memory_space=pl.ANY),
        scratch_shapes=[
            pltpu.SemaphoreType.DMA((8,)),
            pltpu.SemaphoreType.DMA((8,)),
            pltpu.SemaphoreType.DMA((1,)),
        ],
        compiler_params=pltpu.CompilerParams(collective_id=collective_id, has_side_effects=True),
        cost_estimate=pl.CostEstimate(
            flops=0, transcendentals=0, bytes_accessed=2 * tok_count * rows * cols * 2
        ),
    )(block)


def project_tok_kernel(
    tok_count,
    att_ref,
    w_hbm,
    res_ref,
    attn_gain_ref,
    ffn_gain_ref,
    normed_ref,
    mixed_ref,
    out_ref,
    att_all,
    w_buf,
    send_sem,
    recv_sem,
    load_sem,
):
    mesh_ids = pl.DeviceIdType.MESH
    me = lax.axis_index("tok")
    up = lax.rem(me + 2, tok_count)
    down = lax.rem(me + tok_count - 2, tok_count)
    far = lax.rem(me + 4, tok_count)
    partner = me + 1 - 2 * lax.rem(me, 2)
    half = att_ref.shape[0] // 2
    cols = out_ref.shape[1]
    tile = 1280
    tiles = cols // tile

    barrier = pltpu.get_barrier_semaphore()
    for peer in (up, down, partner):
        pl.semaphore_signal(barrier, inc=1, device_id={"tok": peer}, device_id_type=mesh_ids)
    pl.semaphore_wait(barrier, 3)

    def remote(src, dst, slot, peer):
        return pltpu.make_async_remote_copy(
            src_ref=src,
            dst_ref=dst,
            send_sem=send_sem.at[slot],
            recv_sem=recv_sem.at[slot],
            device_id={"tok": peer},
            device_id_type=mesh_ids,
        )

    theirs = (
        partner,
        lax.rem(partner + 2, tok_count),
        lax.rem(partner + tok_count - 2, tok_count),
        lax.rem(partner + 4, tok_count),
    )
    order = (me, theirs[0], down, up, theirs[1], theirs[2], far, theirs[3])

    def load(idx):
        return pltpu.make_async_copy(w_hbm.at[order[idx]], w_buf.at[idx % 2], load_sem.at[idx % 2])

    def accumulate(idx, source, first):
        load(idx).wait()
        if idx + 1 < len(order):
            load(idx + 1).start()
        weights = w_buf.at[idx % 2]

        def one_tile(col):
            span = pl.ds(pl.multiple_of(col * tile, tile), tile)
            term = jnp.dot(source[...], weights[:, span], preferred_element_type=jnp.float32)
            if first:
                out_ref[:, span] = term
            else:
                out_ref[:, span] = out_ref[:, span] + term

        pl.loop(0, tiles)(one_tile)

    load(0).start()
    sends = []

    def send(src, slot, index, peer):
        copy = remote(src, att_all.at[slot], index, peer)
        copy.start()
        sends.append(copy)

    def arrived(slot, index, peer, rows=None):
        dst = att_all.at[slot] if rows is None else att_all.at[slot, rows]
        remote(dst, dst, index, peer).wait_recv()

    first = pl.ds(0, half)
    second = pl.ds(half, half)
    send(att_ref, me, 0, up)
    send(att_ref, me, 1, down)
    send(att_ref, me, 4, partner)
    accumulate(0, att_ref, True)
    arrived(theirs[0], 4, partner)
    accumulate(1, att_all.at[theirs[0]], False)
    arrived(down, 0, down)
    arrived(up, 1, up)
    for src, index, peer in ((att_all.at[down, first], 2, up), (att_all.at[up, second], 3, down)):
        copy = remote(src, src, index, peer)
        copy.start()
        sends.append(copy)
    send(att_all.at[up], up, 5, partner)
    send(att_all.at[down], down, 6, partner)
    accumulate(2, att_all.at[down], False)
    accumulate(3, att_all.at[up], False)
    for idx in range(1, 3):
        arrived(theirs[idx], 4 + idx, partner)
        accumulate(3 + idx, att_all.at[theirs[idx]], False)
    arrived(far, 2, down, first)
    arrived(far, 3, up, second)
    send(att_all.at[far], far, 7, partner)
    accumulate(6, att_all.at[far], False)
    arrived(theirs[3], 7, partner)
    accumulate(7, att_all.at[theirs[3]], False)

    share = mixed_ref.shape[0]

    def finish(block):
        rows = pl.ds(pl.multiple_of(block * share, share), share)
        mixed = res_ref[rows, :].astype(jnp.float32) + rms_scale(out_ref[rows, :], attn_gain_ref[...])
        normed_ref[rows, :] = rms_scale(mixed, ffn_gain_ref[...]).astype(normed_ref.dtype)

    pl.loop(0, out_ref.shape[0] // share)(finish)
    own_rows = pl.ds(pl.multiple_of(me * share, share), share)
    mixed_ref[...] = res_ref[own_rows, :].astype(jnp.float32) + rms_scale(
        out_ref[own_rows, :], attn_gain_ref[...]
    )
    for copy in sends:
        copy.wait_send()


def project_over_tok(attention, w_all, residual, attn_gain, ffn_gain, tok_count, collective_id):
    assert tok_count == 8
    rows, width = attention.shape
    cols = w_all.shape[2]
    share = rows // tok_count
    vmem = pltpu.MemorySpace.VMEM
    vmem_spec = pl.BlockSpec(memory_space=vmem)
    return pl.pallas_call(
        lambda *refs: project_tok_kernel(tok_count, *refs),
        out_shape=(
            jax.ShapeDtypeStruct((rows, cols), jnp.bfloat16),
            jax.ShapeDtypeStruct((share, cols), jnp.float32),
        ),
        in_specs=[vmem_spec, pl.BlockSpec(memory_space=pl.ANY), vmem_spec, vmem_spec, vmem_spec],
        out_specs=(vmem_spec, vmem_spec),
        scratch_shapes=[
            pltpu.VMEM((rows, cols), jnp.float32),
            pltpu.VMEM((tok_count, rows, width), attention.dtype),
            pltpu.VMEM((2, width, cols), w_all.dtype),
            pltpu.SemaphoreType.DMA((8,)),
            pltpu.SemaphoreType.DMA((8,)),
            pltpu.SemaphoreType.DMA((2,)),
        ],
        compiler_params=pltpu.CompilerParams(
            collective_id=collective_id, has_side_effects=True, vmem_limit_bytes=48 * 1024 * 1024
        ),
        cost_estimate=pl.CostEstimate(
            flops=2 * rows * width * tok_count * cols,
            transcendentals=2 * rows,
            bytes_accessed=tok_count * width * cols * 2 + rows * cols * 4,
        ),
    )(attention, w_all, residual, attn_gain.reshape(1, cols), ffn_gain.reshape(1, cols))


def scatter_tok_kernel(
    tok_count, part_hbm, out_ref, mine, chip_in, cross_out, cross_in, load_sem, send_sem, recv_sem
):
    mesh_ids = pl.DeviceIdType.MESH
    me = lax.axis_index("tok")
    up = lax.rem(me + 2, tok_count)
    down = lax.rem(me + tok_count - 2, tok_count)
    far = lax.rem(me + 4, tok_count)
    partner = me + 1 - 2 * lax.rem(me, 2)
    share = out_ref.shape[0]

    barrier = pltpu.get_barrier_semaphore()
    for peer in (up, down, far, partner):
        pl.semaphore_signal(barrier, inc=1, device_id={"tok": peer}, device_id_type=mesh_ids)
    pl.semaphore_wait(barrier, 4)

    def remote(src, dst, slot, peer):
        return pltpu.make_async_remote_copy(
            src_ref=src,
            dst_ref=dst,
            send_sem=send_sem.at[slot],
            recv_sem=recv_sem.at[slot],
            device_id={"tok": peer},
            device_id_type=mesh_ids,
        )

    def family(base):
        return (
            base,
            lax.rem(base + 2, tok_count),
            lax.rem(base + tok_count - 2, tok_count),
            lax.rem(base + 4, tok_count),
        )

    def rows_of(block):
        return pl.ds(pl.multiple_of(block * share, share), share)

    order = (3, 1, 2, 0)
    sends = []
    theirs = family(partner)
    for idx in order:
        copy = remote(part_hbm.at[rows_of(theirs[idx])], chip_in.at[idx], idx, partner)
        copy.start()
        sends.append(copy)
    own = family(me)
    loads = []
    for idx in order:
        load = pltpu.make_async_copy(part_hbm.at[rows_of(own[idx])], mine.at[idx], load_sem.at[idx])
        load.start()
        loads.append(load)
    targets = {1: (up, 1), 2: (down, 0), 3: (far, 2)}
    for pos, idx in enumerate(order[:3]):
        loads[pos].wait()
        remote(part_hbm.at[rows_of(own[idx])], chip_in.at[idx], idx, partner).wait_recv()
        cross_out[idx - 1] = (mine[idx] + chip_in[idx]).astype(cross_out.dtype)
        peer, dst_idx = targets[idx]
        copy = remote(cross_out.at[idx - 1], cross_in.at[dst_idx], 4 + dst_idx, peer)
        copy.start()
        sends.append(copy)
    loads[3].wait()
    remote(part_hbm.at[rows_of(own[0])], chip_in.at[0], 0, partner).wait_recv()
    total = mine[0] + chip_in[0]
    for idx, peer in ((0, up), (1, down), (2, far)):
        remote(cross_out.at[idx], cross_in.at[idx], 4 + idx, peer).wait_recv()
    for idx in range(3):
        total = total + cross_in[idx].astype(jnp.float32)
    out_ref[...] = total
    for copy in sends:
        copy.wait_send()


def scatter_over_tok(partial, tok_count, collective_id):
    assert tok_count == 8
    rows, cols = partial.shape
    share = rows // tok_count
    vmem = pltpu.MemorySpace.VMEM
    return pl.pallas_call(
        lambda *refs: scatter_tok_kernel(tok_count, *refs),
        out_shape=jax.ShapeDtypeStruct((share, cols), jnp.float32),
        in_specs=[pl.BlockSpec(memory_space=pltpu.MemorySpace.HBM)],
        out_specs=pl.BlockSpec(memory_space=vmem),
        scratch_shapes=[
            pltpu.VMEM((4, share, cols), jnp.float32),
            pltpu.VMEM((4, share, cols), jnp.float32),
            pltpu.VMEM((3, share, cols), jnp.bfloat16),
            pltpu.VMEM((3, share, cols), jnp.bfloat16),
            pltpu.SemaphoreType.DMA((4,)),
            pltpu.SemaphoreType.DMA((7,)),
            pltpu.SemaphoreType.DMA((7,)),
        ],
        compiler_params=pltpu.CompilerParams(
            collective_id=collective_id, has_side_effects=True, vmem_limit_bytes=48 * 1024 * 1024
        ),
        cost_estimate=pl.CostEstimate(
            flops=8 * share * cols, transcendentals=0, bytes_accessed=rows * cols * 4 * 2
        ),
    )(partial)


def local(
    queries,
    suffix_kv,
    prefix_cache,
    q_gain,
    k_gain,
    lengths,
    group_of,
    owner_order,
    residual,
    w_out,
    attn_gain,
    ffn_in_gain,
    ffn_out_gain,
    w_gate,
    w_up,
    w_down,
):
    req_count = lax.axis_size("req")
    tok_count = lax.axis_size("tok")
    req_index = lax.axis_index("req")
    tok_index = lax.axis_index("tok")
    row_count = queries.shape[0]
    heads_here = queries.shape[1] // HD
    head_ratio = H // KVH
    kv_first = tok_index * heads_here // head_ratio
    kv_width = KVH * HD
    own_count = req_count // GROUPS

    with jax.named_scope("prefix_gather"):
        half_rows = prefix_cache.shape[0] // 2
        core = tok_index % 2
        first_row_kv = core * half_rows
        half_keys = lax.dynamic_slice(prefix_cache, (first_row_kv, kv_first * HD), (half_rows, HD))
        half_vals = lax.dynamic_slice(
            prefix_cache, (first_row_kv, kv_width + kv_first * HD), (half_rows, HD)
        )
        my_half = jnp.concatenate([half_keys, half_vals], axis=1)
        gathered = lax.all_gather(my_half, "req", axis=0, tiled=False)
        w_out_all = gather_over_tok(w_out, tok_count, 0)
        gathered, w_out_all = lax.optimization_barrier((gathered, w_out_all))
        own_group = group_of[req_index]
        owner_ids = lax.dynamic_slice_in_dim(owner_order, own_group * own_count, own_count)
        picked = jnp.take(gathered, owner_ids, axis=0, mode="clip").reshape(-1, 2 * HD)
        partner = [(t, t ^ 1) for t in range(tok_count)]
        swapped = lax.ppermute(picked, "tok", perm=partner)
        shared = jnp.concatenate([picked, swapped], axis=0)

    with jax.named_scope("attention"):
        query_normed = norm_heads(queries, q_gain, heads_here)
        suf_keys = norm_heads(
            lax.dynamic_slice_in_dim(suffix_kv, kv_first * HD, HD, 1), k_gain, 1
        )
        suf_vals = lax.dynamic_slice_in_dim(suffix_kv, kv_width + kv_first * HD, HD, 1)
        all_keys = jnp.concatenate([shared[:, :HD], suf_keys], axis=0)
        all_vals = jnp.concatenate([shared[:, HD:], suf_vals], axis=0)
        seg_ends = jnp.cumsum(lengths[0])
        positions = jnp.arange(row_count, dtype=jnp.int32)
        segment = jnp.sum((positions[:, None] >= seg_ends[None, :]).astype(jnp.int32), axis=1)
        causal = (segment[:, None] == segment[None, :]) & (positions[None, :] <= positions[:, None])
        visible = jnp.concatenate(
            [jnp.ones((row_count, shared.shape[0]), jnp.bool_), causal], axis=1
        )
        outputs = []
        for head_idx in range(heads_here):
            head_q = query_normed[:, head_idx * HD:(head_idx + 1) * HD]
            scores = jnp.dot(head_q, all_keys.T, preferred_element_type=jnp.float32) * HD ** (-0.5)
            scores = jnp.where(visible, scores, MASKED)
            row_max = jnp.max(scores, axis=-1, keepdims=True)
            weights = jnp.exp(scores - row_max)
            row_sum = jnp.sum(weights, axis=-1, keepdims=True)
            head_out = jnp.dot(
                weights.astype(jnp.bfloat16), all_vals, preferred_element_type=jnp.float32
            ) / row_sum
            outputs.append(head_out)
        attention = jnp.concatenate(outputs, axis=1).astype(jnp.bfloat16)

    share = row_count // tok_count
    first_row = tok_index * share
    with jax.named_scope("out_projection"):
        normed, mixed_share = project_over_tok(
            attention, w_out_all, residual, attn_gain, ffn_in_gain, tok_count, 1
        )
    with jax.named_scope("feed_forward"):
        normed = lax.optimization_barrier(normed)
        gate = jnp.dot(normed, w_gate, preferred_element_type=jnp.float32)
        upward = jnp.dot(normed, w_up, preferred_element_type=jnp.float32)
        hidden = (jax.nn.gelu(gate, approximate=True) * upward).astype(jnp.bfloat16)
        hidden = lax.optimization_barrier(hidden)
        down_share = scatter_over_tok(
            jnp.dot(hidden, w_down, preferred_element_type=jnp.float32), tok_count, 2
        )
    return (mixed_share + rms_scale(down_share.astype(jnp.float32), ffn_out_gain)).astype(
        jnp.bfloat16
    )


def solution(mesh):
    in_specs = (
        P("req", "tok"),
        P("req", None),
        P("req", None),
        P(),
        P(),
        P("req", None),
        P(),
        P(),
        P("req", None),
        P("tok", None),
        P(),
        P(),
        P(),
        P(None, "tok"),
        P(None, "tok"),
        P("tok", None),
    )
    out_specs = P(("req", "tok"), None)
    return jax.shard_map(local, mesh=mesh, in_specs=in_specs, out_specs=out_specs, check_vma=False)
```
